32 devices in a mesh: cell: 2 (over x), blk: 16 (over z, y, core).
Axes of the slice: x: 2, y: 2, z: 4, core: 2. Of those that a mesh axis runs over, the one named last changes fastest.
Arguments:
- psi_val: float32 [256, 64, 64, 64], P('cell', 'blk'), parts along dimension 0, may hold values from -6 to 6
- psi_cond: float32 [6, 64, 64, 64], P('cell', 'blk'), parts along dimension 0, may hold values from -6 to 6
- e_val: float32 [256], P('cell'), parts along dimension 0, may hold values from -8 to -1
- e_cond: float32 [6], P('cell'), parts along dimension 0, may hold values from 1 to 8
- occ: int32 [256], P('cell'), parts along dimension 0, may hold values from 1 to 2
- freq: float32 [10], P('cell'), parts along dimension 0, may hold values from 0.5 to 16
- gmap: int32 [8192], P('cell'), parts along dimension 0, may hold values from 0 to 262143, as said below
Outputs:
- chi_real: float32 [10, 4096, 4096], P('cell', 'blk'), parts along dimension 0
- chi_imag: float32 [10, 4096, 4096], P('cell', 'blk'), parts along dimension 0
The draws below stay inside these ranges and needn't reach their ends.
There are 2 independent parts, one for each index of `cell`. The reference program is written for one: setup_inputs(seed, part) draws one part's arguments, and reference() takes and returns one part's arrays. A program takes and returns all parts, laid end to end along the dimension named above; each array names one. Nothing has to cross between parts.
Inputs may be any that keep to these rules, and one draw needn't show every extreme that they name: `gmap`: the 4096 indices are distinct; index 0 and index 262143 are always among them.
All inputs are finite; a program needn't handle non-finite values.
Results may differ from the reference program's by a relative error of at most 0.0001.
Values sent between devices are 32-bit elements; how exact they have to be, the bound alone decides.
No kernel may reach another device: no remote copies, remote signals or barrier semaphores. Data moves between devices by JAX's collectives and lax.ppermute only.
A program may use at most 256 MiB of HBM per device.

```python
import math
import jax
import jax.numpy as jnp
from jax import lax

GX = 64
GY = 64
GZ = 64
NG = 4096
VAL = 128
COND = 3
NFREQ = 5


def draw_gmap(key, part):
    total_points = GX * GY * GZ
    inner = jax.random.permutation(jax.random.fold_in(key, 11), total_points - 2)[:NG - 2] + 1
    ends = jnp.array([0, total_points - 1], dtype=jnp.int32)
    joined = jnp.concatenate([inner.astype(jnp.int32), ends])
    return jax.random.permutation(jax.random.fold_in(key, 23), joined).astype(jnp.int32)


def plant(drawn, stream_key, least, high):
    longest = drawn.shape.index(max(drawn.shape))
    spots = []
    for shift in (0, 1):
        where = [jax.random.randint(jax.random.fold_in(stream_key, axis), (), 0, length) for axis, length in enumerate(drawn.shape)]
        where[longest] = (where[longest] + shift) % drawn.shape[longest]
        spots.append(tuple(where))
    return drawn.at[spots[0]].set(least).at[spots[1]].set(high)


def block_scale(own_key, extent, cuts, smallest, largest):
    def one(position, shards_of):
        heights = jax.random.uniform(jax.random.fold_in(jax.random.fold_in(own_key, 6), position), (shards_of,), jnp.float32, smallest / len(cuts), largest / len(cuts))
        return jnp.repeat(jnp.exp(heights), extent[position] // shards_of).reshape((-1,) + (1,) * (len(extent) - position - 1))

    gain = one(*cuts[0])
    for cut in cuts[1:]:
        gain = gain * one(*cut)
    return gain


def scatter_about(own_key, shape, deviation, most, pieces=(), held_as=jnp.bfloat16):
    drawn = jax.random.normal(own_key, shape, jnp.float32) * deviation
    if len(pieces) > 0:
        drawn = block_scale(own_key, shape, pieces, -0.22, 0.18) * drawn
    return jnp.clip(drawn, min=-most, max=most).astype(held_as)


def setup_inputs(seed: int = 0, part: int = 0) -> dict:
    streams_of = jax.random.split(jax.random.key(seed), 8)
    own_keys = jax.random.split(jax.random.fold_in(streams_of[7], part), 8)
    psi_val = scatter_about(own_keys[0], (VAL, GX, GY, GZ), 1.0, 6.0, ((1, 16),), jnp.float32)
    psi_cond = scatter_about(own_keys[1], (COND, GX, GY, GZ), 1.0, 6.0, ((1, 16),), jnp.float32)
    e_val = jnp.clip(jax.random.uniform(own_keys[2], (VAL,), jnp.float32, -8.0, -1.0), -8.0, -1.0)
    e_cond = jnp.clip(jax.random.uniform(own_keys[3], (COND,), jnp.float32, 1.0, 8.0), 1.0, 8.0)
    occ = plant(jax.random.randint(own_keys[4], (VAL,), 1, 3), jax.random.fold_in(own_keys[4], 1), 1, 2).astype(jnp.int32)
    freq = jnp.clip(jnp.exp(jax.random.uniform(own_keys[5], (NFREQ,), jnp.float32, math.log(0.5), math.log(16.0))), 0.5, 16.0)
    gmap = draw_gmap(jax.random.fold_in(jax.random.fold_in(streams_of[7], part), 71), part)
    return {"psi_val": psi_val, "psi_cond": psi_cond, "e_val": e_val, "e_cond": e_cond, "occ": occ, "freq": freq, "gmap": gmap}


def reference(psi_val, psi_cond, e_val, e_cond, occ, freq, gmap):
    total_points = GX * GY * GZ
    norm_factor = 1.0 / math.sqrt(total_points)

    def one_band(band):
        density = psi_val[band][None] * psi_cond
        spectrum = jnp.fft.fftn(density, axes=(1, 2, 3)).reshape(COND, total_points)
        picked = jnp.take(spectrum, gmap, axis=1)
        return (picked.real * norm_factor, picked.imag * norm_factor)
    real_m, imag_m = lax.map(one_band, jnp.arange(VAL, dtype=jnp.int32))
    real_m = real_m.reshape(VAL * COND, NG)
    imag_m = imag_m.reshape(VAL * COND, NG)
    gaps = (e_val[:, None] - e_cond[None, :]).reshape(VAL * COND)
    occ_pairs = jnp.broadcast_to(occ.astype(jnp.float32)[:, None], (VAL, COND)).reshape(VAL * COND)
    stacked = jnp.concatenate([real_m, imag_m], axis=0)
    real_list = []
    imag_list = []
    for step in range(NFREQ):
        weights = occ_pairs * gaps / (gaps * gaps + freq[step] * freq[step])
        weights = weights / math.sqrt(VAL * COND)
        left_real = jnp.concatenate([weights[:, None] * real_m, weights[:, None] * imag_m], axis=0)
        left_imag = jnp.concatenate([weights[:, None] * imag_m, -weights[:, None] * real_m], axis=0)
        real_list.append(jnp.dot(left_real.T, stacked, precision=lax.Precision.HIGHEST, preferred_element_type=jnp.float32))
        imag_list.append(jnp.dot(left_imag.T, stacked, precision=lax.Precision.HIGHEST, preferred_element_type=jnp.float32))
    return (jnp.stack(real_list), jnp.stack(imag_list))
```

```python
import functools
import math

import jax
import jax.numpy as jnp
import ml_dtypes
import numpy as np
from jax import lax
from jax.experimental import pallas as pl
from jax.experimental.pallas import tpu as pltpu
from jax.sharding import PartitionSpec as P

LANES = 128
SUB = 8
SLOTS = 4
f32 = jnp.float32
bf16 = jnp.bfloat16


def split_np(table):
    high = table.astype(ml_dtypes.bfloat16)
    low = (table - high.astype(np.float64)).astype(ml_dtypes.bfloat16)
    return np.concatenate([high, high, low], axis=1)


def split3(block):
    high = block.astype(bf16)
    low = (block - high.astype(f32)).astype(bf16)
    return jnp.concatenate([high, low, high], axis=0)


def z_table(size_z):
    half = size_z // 2
    z = np.arange(size_z)
    cos_rows = np.cos(2 * np.pi * ((np.arange(half + 1)[:, None] * z) % size_z) / size_z)
    sin_rows = -np.sin(2 * np.pi * ((np.arange(1, half)[:, None] * z) % size_z) / size_z)
    return np.concatenate([cos_rows, sin_rows], axis=0)


def y_tables(size_y):
    k = np.arange(size_y)
    ang = 2 * np.pi * ((k[:, None] * k[None, :]) % size_y) / size_y
    cos_t, sin_t = np.cos(ang), np.sin(ang)
    real_rows = np.concatenate([cos_t, sin_t], axis=1)
    imag_rows = np.concatenate([-sin_t, cos_t], axis=1)
    full = np.stack([real_rows, imag_rows], axis=0).reshape(2, size_y // 4, 4, 2 * size_y)
    full = full.transpose(1, 0, 2, 3).reshape(2 * size_y, 2 * size_y)
    return full, full[:, :size_y]


def roll_sub(x, shift):
    return pltpu.roll(x, shift % SUB, axis=x.ndim - 2)


def transform_kernel(
    pick_ref, val_ref, cond_ref, dz_ref, dy_ref, dyr_ref, cs_ref, out_ref, z_scr, tab_scr
):
    slots, size_y, size_z, lanes = val_ref.shape
    half = size_z // 2
    groups_y = size_y // SUB

    def z_stage(step, carry):
        x = step // groups_y
        yg = step % groups_y
        cond = cond_ref[x, yg]
        parts = []
        for j in range(SUB):
            block = val_ref[x, yg * SUB + j]
            parts.append(block * jnp.broadcast_to(cond[:, j : j + 1], (size_z, lanes)))
        rhs = split3(jnp.concatenate(parts, axis=1))
        got = jnp.dot(dz_ref[...], rhs, preferred_element_type=f32)
        for j in range(SUB):
            z_scr[x, pl.ds(yg * SUB + j, size_z, stride=size_y), :] = got[
                :, j * lanes : (j + 1) * lanes
            ]
        return carry

    lax.fori_loop(0, slots * groups_y, z_stage, 0)

    shape = (size_y // 4, SUB, lanes)
    sub = lax.broadcasted_iota(jnp.int32, shape, 1)
    low2 = (sub % 4) < 2
    low1 = (sub % 2) == 0

    def put(kz, got):
        a = [got[:, x * lanes : (x + 1) * lanes].reshape(shape) for x in range(slots)]
        p0 = jnp.where(low2, a[0], roll_sub(a[2], 2))
        p2 = jnp.where(low2, roll_sub(a[0], -2), a[2])
        p1 = jnp.where(low2, a[1], roll_sub(a[3], 2))
        p3 = jnp.where(low2, roll_sub(a[1], -2), a[3])
        tab_scr[kz, :, 0] = jnp.where(low1, p0, roll_sub(p1, 1))
        tab_scr[kz, :, 1] = jnp.where(low1, roll_sub(p0, -1), p1)
        tab_scr[kz, :, 2] = jnp.where(low1, p2, roll_sub(p3, 1))
        tab_scr[kz, :, 3] = jnp.where(low1, roll_sub(p2, -1), p3)

    def rows(k):
        start = pl.multiple_of(k * size_y, size_y)
        return jnp.concatenate([z_scr[x, pl.ds(start, size_y), :] for x in range(slots)], axis=1)

    for kz in (0, half):
        put(kz, jnp.dot(dyr_ref[...], split3(rows(kz)), preferred_element_type=f32))

    def y_stage(kz, carry):
        block = jnp.concatenate([rows(kz), rows(half + kz)], axis=0)
        put(kz, jnp.dot(dy_ref[...], split3(block), preferred_element_type=f32))
        return carry

    lax.fori_loop(1, half, y_stage, 0)

    sub1 = lax.broadcasted_iota(jnp.int32, (SUB, lanes), 0)
    m2 = (sub1 % 4) < 2
    m1 = (sub1 % 2) == 0
    kzs, kyq, _, _, _ = tab_scr.shape
    tab = tab_scr.reshape(kzs * kyq * 4, SUB, lanes)
    quads = out_ref.shape[0]

    def quad(q):
        t = []
        for i in range(4):
            word = pick_ref[q * 4 + i]
            col = lax.shift_right_logical(word, 8)
            ph = word & 255
            d = tab[col]
            t.append(d * cs_ref[0, ph] + roll_sub(d, 4) * cs_ref[1, ph])
        v0 = jnp.where(m2, t[0], roll_sub(t[2], 2)) + jnp.where(m2, roll_sub(t[0], -2), t[2])
        v1 = jnp.where(m2, t[1], roll_sub(t[3], 2)) + jnp.where(m2, roll_sub(t[1], -2), t[3])
        out_ref[q] = jnp.where(m1, v0, roll_sub(v1, 1)) + jnp.where(m1, roll_sub(v0, -1), v1)

    def gather(step, carry):
        for u in range(4):
            quad(step * 4 + u)
        return carry

    lax.fori_loop(0, quads // 4, gather, 0)


def transform(pick, val, cond, cs, num_g):
    slots, size_y, size_z, lanes = val.shape
    dz = jnp.asarray(split_np(z_table(size_z)))
    full, real_only = y_tables(size_y)
    dy, dyr = jnp.asarray(split_np(full)), jnp.asarray(split_np(real_only))
    vmem = pl.BlockSpec(memory_space=pltpu.VMEM)
    return pl.pallas_call(
        transform_kernel,
        out_shape=jax.ShapeDtypeStruct((num_g // 4, SUB, lanes), f32),
        in_specs=[pl.BlockSpec(memory_space=pltpu.SMEM)] + [vmem] * 6,
        out_specs=vmem,
        scratch_shapes=[
            pltpu.VMEM((slots, size_z * size_y, lanes), f32),
            pltpu.VMEM((size_z // 2 + 1, size_y // 4, 4, SUB, lanes), f32),
        ],
        name="transform",
    )(pick, val, cond, dz, dy, dyr, cs)


def split_lanes(block):
    high = block.astype(bf16)
    low = (block - high.astype(f32)).astype(bf16)
    return high, low


def chi_kernel(w_ref, own_ref, all_ref, real_ref, imag_ref, left_scr):
    freqs, rows, _ = real_ref.shape
    pairs2 = own_ref.shape[1]
    pairs = pairs2 // 2

    @pl.when(pl.program_id(0) == 0)
    def _():
        own = own_ref[...]
        for w in range(freqs):
            a = own[:, :pairs] * w_ref[w : w + 1, :]
            b = own[:, pairs:] * w_ref[w : w + 1, :]
            ah, al = split_lanes(a)
            bh, bl = split_lanes(b)
            for half, parts in enumerate(([ah, bh, ah, bh, al, bl], [bh, -ah, bh, -ah, bl, -al])):
                r0 = (half * freqs + w) * rows
                for n, part in enumerate(parts):
                    left_scr[r0 : r0 + rows, n * pairs : (n + 1) * pairs] = part

    high, low = split_lanes(all_ref[...])
    right = jnp.concatenate([high, low, high], axis=1)
    got = lax.dot_general(
        left_scr[...], right, (((1,), (1,)), ((), ())), preferred_element_type=f32
    )
    for w in range(freqs):
        real_ref[w] = got[w * rows : (w + 1) * rows]
        imag_ref[w] = got[(freqs + w) * rows : (freqs + w + 1) * rows]


def chi(weights, own, everyone, tile=512):
    freqs, pairs = weights.shape
    rows = own.shape[0]
    num_g = everyone.shape[0]
    out = jax.ShapeDtypeStruct((freqs, rows, num_g), f32)
    out_spec = pl.BlockSpec((freqs, rows, tile), lambda t: (0, 0, t))
    return pl.pallas_call(
        chi_kernel,
        grid=(num_g // tile,),
        out_shape=(out, out),
        in_specs=[
            pl.BlockSpec((freqs, pairs), lambda t: (0, 0)),
            pl.BlockSpec((rows, 2 * pairs), lambda t: (0, 0)),
            pl.BlockSpec((tile, 2 * pairs), lambda t: (t, 0)),
        ],
        out_specs=(out_spec, out_spec),
        scratch_shapes=[pltpu.VMEM((2 * freqs * rows, 6 * pairs), bf16)],
        name="chi",
    )(weights, own, everyone)


def phase_table(size_x, first, planes, norm):
    x = first + jnp.arange(SLOTS, dtype=jnp.int32)
    k = jnp.arange(size_x, dtype=jnp.int32)
    ang = (k[:, None] * x[None, :] % size_x).astype(f32) * (2.0 * math.pi / size_x)
    live = (jnp.arange(SLOTS) < planes).astype(f32) * norm
    cos_t, sin_t = jnp.cos(ang) * live, jnp.sin(ang) * live
    plain = jnp.stack(
        [jnp.concatenate([cos_t, cos_t], 1), jnp.concatenate([sin_t, -sin_t], 1)]
    )
    mirror = jnp.stack(
        [jnp.concatenate([cos_t, -cos_t], 1), jnp.concatenate([-sin_t, -sin_t], 1)]
    )
    table = jnp.concatenate([plain, mirror], axis=1)
    return jnp.broadcast_to(table[..., None], table.shape + (LANES,))


def body(psi_val, psi_cond, e_val, e_cond, occ, freq, gmap):
    num_val, planes, size_y, size_z = psi_val.shape
    num_cond = psi_cond.shape[0]
    num_g = gmap.shape[0]
    pairs = num_val * num_cond
    size_x = planes * lax.axis_size("blk")
    norm = 1.0 / math.sqrt(size_x * size_y * size_z)

    val = jnp.transpose(psi_val, (1, 2, 3, 0))
    cond = jnp.transpose(
        psi_cond.reshape(num_cond, planes, size_y // SUB, SUB, size_z), (0, 1, 2, 4, 3)
    )
    if planes < SLOTS:
        val = jnp.pad(val, ((0, SLOTS - planes), (0, 0), (0, 0), (0, 0)))
        cond = jnp.pad(cond, ((0, 0), (0, SLOTS - planes), (0, 0), (0, 0), (0, 0)))

    kz = gmap % size_z
    ky = gmap // size_z % size_y
    kx = gmap // (size_z * size_y)
    mirrored = kz > size_z // 2
    col = jnp.where(mirrored, size_z - kz, kz) * size_y + jnp.where(
        mirrored, (size_y - ky) % size_y, ky
    )
    pick = col * 256 + kx + jnp.where(mirrored, size_x, 0)
    cs = phase_table(size_x, lax.axis_index("blk") * planes, planes, norm)

    owned = []
    for c in range(num_cond):
        part = transform(pick, val, cond[c], cs, num_g)
        owned.append(lax.psum_scatter(part, "blk", scatter_dimension=0, tiled=True))
    own = jnp.stack(owned).reshape(num_cond, -1, 2, 4, num_val)
    own = jnp.transpose(own, (1, 3, 2, 0, 4)).reshape(-1, 2 * pairs)

    gaps = e_val[None, :] - e_cond[:, None]
    gaps = gaps.reshape(1, pairs)
    occ_row = jnp.broadcast_to(occ.astype(f32)[None, :], (num_cond, num_val)).reshape(1, pairs)
    weights = occ_row * gaps / (gaps * gaps + (freq * freq)[:, None]) / math.sqrt(pairs)

    return chi(weights, own, lax.all_gather(own, "blk", axis=0, tiled=True))


def solution(mesh):
    return jax.shard_map(
        body,
        mesh=mesh,
        in_specs=(
            P("cell", "blk", None, None),
            P("cell", "blk", None, None),
            P("cell"),
            P("cell"),
            P("cell"),
            P("cell"),
            P("cell"),
        ),
        out_specs=(P("cell", "blk", None), P("cell", "blk", None)),
        check_vma=False,
    )
```

```python
import functools
import math

import jax
import jax.numpy as jnp
import ml_dtypes
import numpy as np
from jax import lax
from jax.experimental import pallas as pl
from jax.experimental.pallas import tpu as pltpu
from jax.sharding import PartitionSpec as P


LANES = 128
SUB = 8
SLOTS = 4
f32 = jnp.float32
bf16 = jnp.bfloat16


def split_np(table):
    high = table.astype(ml_dtypes.bfloat16)
    low = (table - high.astype(np.float64)).astype(ml_dtypes.bfloat16)
    return np.concatenate([high, high, low], axis=1)


def split3(block):
    high = block.astype(bf16)
    low = (block - high.astype(f32)).astype(bf16)
    return jnp.concatenate([high, low, high], axis=0)


def z_table(size_z):
    half = size_z // 2
    z = np.arange(size_z)
    cos_rows = np.cos(2 * np.pi * ((np.arange(half + 1)[:, None] * z) % size_z) / size_z)
    sin_rows = -np.sin(2 * np.pi * ((np.arange(1, half)[:, None] * z) % size_z) / size_z)
    return np.concatenate([cos_rows, sin_rows], axis=0)


def y_tables(size_y):
    k = np.arange(size_y)
    ang = 2 * np.pi * ((k[:, None] * k[None, :]) % size_y) / size_y
    cos_t, sin_t = np.cos(ang), np.sin(ang)
    real_rows = np.concatenate([cos_t, sin_t], axis=1)
    imag_rows = np.concatenate([-sin_t, cos_t], axis=1)
    full = np.stack([real_rows, imag_rows], axis=0).reshape(2, size_y // 4, 4, 2 * size_y)
    full = full.transpose(1, 0, 2, 3).reshape(2 * size_y, 2 * size_y)
    return full, full[:, :size_y]


def roll_sub(x, shift):
    return pltpu.roll(x, shift % SUB, axis=x.ndim - 2)


def transform_kernel(
    pick_ref, val_ref, cond_ref, dz_ref, dy_ref, dyr_ref, cs_ref, keep_ref, send_ref, z_scr, tab_scr
):
    slots, size_y, size_z, lanes = val_ref.shape
    half = size_z // 2
    groups_y = size_y // SUB

    def z_stage(step, carry):
        x = step // groups_y
        yg = step % groups_y
        cond = cond_ref[x, yg]
        parts = []
        for j in range(SUB):
            block = val_ref[x, yg * SUB + j]
            parts.append(block * jnp.broadcast_to(cond[:, j : j + 1], (size_z, lanes)))
        rhs = split3(jnp.concatenate(parts, axis=1))
        got = jnp.dot(dz_ref[...], rhs, preferred_element_type=f32)
        for j in range(SUB):
            z_scr[x, pl.ds(yg * SUB + j, size_z, stride=size_y), :] = got[
                :, j * lanes : (j + 1) * lanes
            ]
        return carry

    lax.fori_loop(0, slots * groups_y, z_stage, 0)

    shape = (size_y // 4, SUB, lanes)
    sub = lax.broadcasted_iota(jnp.int32, shape, 1)
    low2 = (sub % 4) < 2
    low1 = (sub % 2) == 0

    def put(kz, got):
        a = [got[:, x * lanes : (x + 1) * lanes].reshape(shape) for x in range(slots)]
        p0 = jnp.where(low2, a[0], roll_sub(a[2], 2))
        p2 = jnp.where(low2, roll_sub(a[0], -2), a[2])
        p1 = jnp.where(low2, a[1], roll_sub(a[3], 2))
        p3 = jnp.where(low2, roll_sub(a[1], -2), a[3])
        tab_scr[kz, :, 0] = jnp.where(low1, p0, roll_sub(p1, 1))
        tab_scr[kz, :, 1] = jnp.where(low1, roll_sub(p0, -1), p1)
        tab_scr[kz, :, 2] = jnp.where(low1, p2, roll_sub(p3, 1))
        tab_scr[kz, :, 3] = jnp.where(low1, roll_sub(p2, -1), p3)

    def rows(k):
        start = pl.multiple_of(k * size_y, size_y)
        return jnp.concatenate([z_scr[x, pl.ds(start, size_y), :] for x in range(slots)], axis=1)

    for kz in (0, half):
        put(kz, jnp.dot(dyr_ref[...], split3(rows(kz)), preferred_element_type=f32))

    def y_stage(kz, carry):
        block = jnp.concatenate([rows(kz), rows(half + kz)], axis=0)
        put(kz, jnp.dot(dy_ref[...], split3(block), preferred_element_type=f32))
        return carry

    lax.fori_loop(1, half, y_stage, 0)

    sub1 = lax.broadcasted_iota(jnp.int32, (SUB, lanes), 0)
    m2 = (sub1 % 4) < 2
    m1 = (sub1 % 2) == 0
    kzs, kyq, _, _, _ = tab_scr.shape
    tab = tab_scr.reshape(kzs * kyq * 4, SUB, lanes)
    quads = keep_ref.shape[0]

    def quad(out_ref, first, q):
        t = []
        for i in range(4):
            word = pick_ref[first + q * 4 + i]
            col = lax.shift_right_logical(word, 8)
            ph = word & 255
            d = tab[col]
            t.append(d * cs_ref[0, ph] + roll_sub(d, 4) * cs_ref[1, ph])
        v0 = jnp.where(m2, t[0], roll_sub(t[2], 2)) + jnp.where(m2, roll_sub(t[0], -2), t[2])
        v1 = jnp.where(m2, t[1], roll_sub(t[3], 2)) + jnp.where(m2, roll_sub(t[1], -2), t[3])
        out_ref[q] = jnp.where(m1, v0, roll_sub(v1, 1)) + jnp.where(m1, roll_sub(v0, -1), v1)

    for out_ref, first in ((send_ref, quads * 4), (keep_ref, 0)):

        def gather(step, carry, out_ref=out_ref, first=first):
            for u in range(4):
                quad(out_ref, first, step * 4 + u)
            return carry

        lax.fori_loop(0, quads // 4, gather, 0)


def transform(pick, val, cond, cs, num_g):
    slots, size_y, size_z, lanes = val.shape
    dz = jnp.asarray(split_np(z_table(size_z)))
    full, real_only = y_tables(size_y)
    dy, dyr = jnp.asarray(split_np(full)), jnp.asarray(split_np(real_only))
    vmem = pl.BlockSpec(memory_space=pltpu.VMEM)
    return pl.pallas_call(
        transform_kernel,
        out_shape=(jax.ShapeDtypeStruct((num_g // 8, SUB, lanes), f32),) * 2,
        in_specs=[pl.BlockSpec(memory_space=pltpu.SMEM)] + [vmem] * 6,
        out_specs=(vmem, vmem),
        scratch_shapes=[
            pltpu.VMEM((slots, size_z * size_y, lanes), f32),
            pltpu.VMEM((size_z // 2 + 1, size_y // 4, 4, SUB, lanes), f32),
        ],
        name="transform",
    )(pick, val, cond, dz, dy, dyr, cs)


def split_lanes(block):
    high = block.astype(bf16)
    low = (block - high.astype(f32)).astype(bf16)
    return high, low


def fill_left(w_ref, own_ref, left_scr):
    freqs = w_ref.shape[0]
    rows, pairs2 = own_ref.shape

    def fill(w, carry):
        row = w_ref[pl.ds(w, 1), :]
        high, low = split_lanes(own_ref[...] * jnp.concatenate([row, row], axis=1))
        at = pl.ds(pl.multiple_of(w * rows, rows), rows)
        left_scr[at, :pairs2] = high
        left_scr[at, pairs2 : 2 * pairs2] = high
        left_scr[at, 2 * pairs2 :] = low
        return carry

    lax.fori_loop(0, freqs, fill, 0)


def chi_tile(block, left_scr, real_ref, imag_ref):
    freqs, rows, _ = real_ref.shape
    pairs = block.shape[1] // 2
    turned = jnp.concatenate([-block[:, pairs:], block[:, :pairs]], axis=1)
    for value, out_ref in ((block, real_ref), (turned, imag_ref)):
        high, low = split_lanes(value)
        right = jnp.concatenate([high, low, high], axis=1)
        got = lax.dot_general(
            left_scr[...], right, (((1,), (1,)), ((), ())), preferred_element_type=f32
        )
        out_ref[...] = got.reshape(freqs, rows, -1)


def chi_kernel(w_ref, own_ref, all_ref, real_ref, imag_ref, left_scr):
    @pl.when(pl.program_id(0) == 0)
    def _():
        fill_left(w_ref, own_ref, left_scr)

    chi_tile(all_ref[...], left_scr, real_ref, imag_ref)


def chi(weights, own, everyone):
    freqs, pairs = weights.shape
    rows = own.shape[0]
    num_g = everyone.shape[0]
    tile = min(num_g, 4 * LANES)
    out = jax.ShapeDtypeStruct((freqs, rows, num_g), f32)
    out_spec = pl.BlockSpec((freqs, rows, tile), lambda t: (0, 0, t))
    return pl.pallas_call(
        chi_kernel,
        grid=(num_g // tile,),
        out_shape=(out, out),
        in_specs=[
            pl.BlockSpec((freqs, pairs), lambda t: (0, 0)),
            pl.BlockSpec((rows, 2 * pairs), lambda t: (0, 0)),
            pl.BlockSpec((tile, 2 * pairs), lambda t: (t, 0)),
        ],
        out_specs=(out_spec, out_spec),
        scratch_shapes=[pltpu.VMEM((freqs * rows, 6 * pairs), bf16)],
        name="chi",
    )(weights, own, everyone)


def chi_group_kernel(counts, with_old, *refs):
    total = sum(counts)
    n = len(counts)
    _, w_ref, own_ref = refs[:3]
    pieces = refs[3 : 3 + total]
    rest = refs[3 + total + (2 if with_old else 0) :]
    real_ref, imag_ref, left_scr, got_scr, sems = rest
    step = pl.program_id(0)

    def copies(i):
        at, first = 0, sum(counts[:i])
        for j in range(counts[i]):
            ref = pieces[first + j]
            yield pltpu.make_async_copy(
                ref, got_scr.at[i, pl.ds(at, ref.shape[0])], sems.at[first + j]
            )
            at += ref.shape[0]

    @pl.when(step == 0)
    def _():
        for i in range(n):
            for copy in copies(i):
                copy.start()
        fill_left(w_ref, own_ref, left_scr)

    for i in range(n):

        @pl.when(step == i)
        def _(i=i):
            for copy in copies(i):
                copy.wait()

    chi_tile(got_scr[step], left_scr, real_ref, imag_ref)


def chi_group(weights, own, blocks, ids, num_g, old):
    freqs, pairs = weights.shape
    rows = own.shape[0]
    counts = tuple(len(b) for b in blocks)
    pieces = [p for b in blocks for p in b]
    out = jax.ShapeDtypeStruct((freqs, rows, num_g), f32)
    out_spec = pl.BlockSpec((freqs, rows, rows), lambda t, ids: (0, 0, ids[t]))
    hbm = pl.BlockSpec(memory_space=pl.ANY)
    olds = () if old is None else old
    return pl.pallas_call(
        functools.partial(chi_group_kernel, counts, old is not None),
        grid_spec=pltpu.PrefetchScalarGridSpec(
            num_scalar_prefetch=1,
            grid=(len(blocks),),
            in_specs=[
                pl.BlockSpec((freqs, pairs), lambda t, ids: (0, 0)),
                pl.BlockSpec((rows, 2 * pairs), lambda t, ids: (0, 0)),
            ]
            + [hbm] * (len(pieces) + len(olds)),
            out_specs=(out_spec, out_spec),
            scratch_shapes=[
                pltpu.VMEM((freqs * rows, 6 * pairs), bf16),
                pltpu.VMEM((len(blocks), rows, 2 * pairs), f32),
                pltpu.SemaphoreType.DMA((len(pieces),)),
            ],
        ),
        out_shape=(out, out),
        input_output_aliases={3 + len(pieces) + i: i for i in range(len(olds))},
        name="chi",
    )(ids, weights, own, *pieces, *olds)


RING = (0, 2, 3, 1)


class Links:
    def __init__(self, count):
        def place(i):
            return i // 4, i // 2 % 2, i % 2

        def at(z, y, core):
            return z * 4 + y * 2 + core

        def turn(i, by):
            z, y, core = place(i)
            return at(RING[(RING.index(z) + by) % 4], y, core)

        every = range(count)
        self.core = [(i, i ^ 1) for i in every]
        self.y = [(i, i ^ 2) for i in every]
        self.cw = [(i, turn(i, 1)) for i in every]
        self.ccw = [(i, turn(i, -1)) for i in every]
        self.near = np.array(
            [
                [[[turn(i ^ (2 * b) ^ a, r) for r in range(4)] for b in range(2)] for a in range(2)]
                for i in every
            ],
            dtype=np.int32,
        )

    @staticmethod
    def fits(count):
        return count == len(RING) * 4


def send(value, pairs):
    return lax.ppermute(value, "blk", pairs)


def reduce_scatter(keep, other, links):
    half = keep.shape[0] // 2
    got = send(other, links.core)
    far = send(keep[half:] + got[half:], links.y)
    near = keep[:half] + got[:half] + far
    block = half // 4
    part = block // 2
    cw = send(near[2 * block : 2 * block + part], links.cw)
    ccw = send(near[2 * block + part : 3 * block], links.ccw)
    cw, ccw = lax.optimization_barrier((cw, ccw))
    from_cw = send(
        jnp.concatenate([near[block : block + part] + cw, near[block + part : 2 * block]]), links.cw
    )
    from_ccw = send(
        jnp.concatenate([near[3 * block : 3 * block + part], near[3 * block + part :] + ccw]),
        links.ccw,
    )
    from_cw, from_ccw = lax.optimization_barrier((from_cw, from_ccw))
    return near[:block] + from_cw + from_ccw


GROUPS = (((0, 0),), ((1, 0),), ((0, 1), (0, 3)), ((0, 2),), ((1, 1), (1, 3)), ((1, 2),))


def gather_and_chi(weights, own, links, near, num_g):
    part = own.shape[0] // 2

    def over(pieces, pairs):
        return [send(p, pairs) for p in pieces]

    mine = {(0, 0): [own]}
    mine[0, 3] = over([own], links.cw)
    mine[0, 1] = over([own], links.ccw)
    mine[0, 2] = [send(mine[0, 3][0][:part], links.cw), send(mine[0, 1][0][part:], links.ccw)]
    for r in range(4):
        mine[1, r] = over(mine[0, r], links.y)
    old = None
    for group in GROUPS:
        blocks, ids = [], []
        for b, r in group:
            blocks += [mine[b, r], over(mine[b, r], links.core)]
            ids += [near[0, b, r], near[1, b, r]]
        old = chi_group(weights, own, blocks, jnp.stack(ids), num_g, old)
    return old


def phase_table(size_x, first, planes, norm):
    x = first + jnp.arange(SLOTS, dtype=jnp.int32)
    k = jnp.arange(size_x, dtype=jnp.int32)
    ang = (k[:, None] * x[None, :] % size_x).astype(f32) * (2.0 * math.pi / size_x)
    live = (jnp.arange(SLOTS) < planes).astype(f32) * norm
    cos_t, sin_t = jnp.cos(ang) * live, jnp.sin(ang) * live
    plain = jnp.stack(
        [jnp.concatenate([cos_t, cos_t], 1), jnp.concatenate([sin_t, -sin_t], 1)]
    )
    mirror = jnp.stack(
        [jnp.concatenate([cos_t, -cos_t], 1), jnp.concatenate([-sin_t, -sin_t], 1)]
    )
    table = jnp.concatenate([plain, mirror], axis=1)
    return jnp.broadcast_to(table[..., None], table.shape + (LANES,))


def polarizability(psi_val, psi_cond, e_val, e_cond, occ, freq, gmap):
    num_val, planes, size_y, size_z = psi_val.shape
    num_cond = psi_cond.shape[0]
    num_g = gmap.shape[0]
    pairs = num_val * num_cond
    size_x = planes * lax.axis_size("blk")
    norm = 1.0 / math.sqrt(size_x * size_y * size_z)

    val = jnp.transpose(psi_val, (1, 2, 3, 0))
    cond = jnp.transpose(
        psi_cond.reshape(num_cond, planes, size_y // SUB, SUB, size_z), (0, 1, 2, 4, 3)
    )
    if planes < SLOTS:
        val = jnp.pad(val, ((0, SLOTS - planes), (0, 0), (0, 0), (0, 0)))
        cond = jnp.pad(cond, ((0, 0), (0, SLOTS - planes), (0, 0), (0, 0), (0, 0)))

    kz = gmap % size_z
    ky = gmap // size_z % size_y
    kx = gmap // (size_z * size_y)
    mirrored = kz > size_z // 2
    col = jnp.where(mirrored, size_z - kz, kz) * size_y + jnp.where(
        mirrored, (size_y - ky) % size_y, ky
    )
    pick = col * 256 + kx + jnp.where(mirrored, size_x, 0)
    cs = phase_table(size_x, lax.axis_index("blk") * planes, planes, norm)

    count = lax.axis_size("blk")
    links = Links(count) if Links.fits(count) else None
    if links is not None:
        near = jnp.asarray(links.near)[lax.axis_index("blk")]
        pick = pick.reshape(count, -1)[near.reshape(-1)].reshape(-1)
    owned = []
    for c in range(num_cond):
        keep, other = transform(pick, val, cond[c], cs, num_g)
        if links is not None:
            owned.append(reduce_scatter(keep, other, links))
        else:
            whole = jnp.concatenate([keep, other])
            owned.append(lax.psum_scatter(whole, "blk", scatter_dimension=0, tiled=True))
    own = jnp.stack(owned).reshape(num_cond, -1, 2, 4, num_val)
    own = jnp.transpose(own, (1, 3, 2, 0, 4)).reshape(-1, 2 * pairs)

    gaps = e_val[None, :] - e_cond[:, None]
    gaps = gaps.reshape(1, pairs)
    occ_row = jnp.broadcast_to(occ.astype(f32)[None, :], (num_cond, num_val)).reshape(1, pairs)
    weights = occ_row * gaps / (gaps * gaps + (freq * freq)[:, None]) / math.sqrt(pairs)

    if links is not None:
        return gather_and_chi(weights, own, links, near, num_g)
    return chi(weights, own, lax.all_gather(own, "blk", axis=0, tiled=True))


def solution(mesh):
    step = jax.shard_map(
        polarizability,
        mesh=mesh,
        in_specs=(
            P("cell", "blk", None, None),
            P("cell", "blk", None, None),
            P("cell"),
            P("cell"),
            P("cell"),
            P("cell"),
            P("cell"),
        ),
        out_specs=(P("cell", "blk", None), P("cell", "blk", None)),
        check_vma=False,
    )
    if not Links.fits(mesh.shape["blk"]):
        return step
    return step
```

```python
import functools
import math

import jax
import jax.numpy as jnp
import ml_dtypes
import numpy as np
from jax import lax
from jax.experimental import pallas as pl
from jax.experimental.pallas import tpu as pltpu
from jax.sharding import PartitionSpec as P


LANES = 128
SUB = 8
SLOTS = 4
f32 = jnp.float32
bf16 = jnp.bfloat16


def split_np(table):
    high = table.astype(ml_dtypes.bfloat16)
    low = (table - high.astype(np.float64)).astype(ml_dtypes.bfloat16)
    return np.concatenate([high, high, low], axis=1)


def split3(block):
    high = block.astype(bf16)
    low = (block - high.astype(f32)).astype(bf16)
    return jnp.concatenate([high, low, high], axis=0)


def z_table(size_z):
    half = size_z // 2
    z = np.arange(size_z)
    cos_rows = np.cos(2 * np.pi * ((np.arange(half + 1)[:, None] * z) % size_z) / size_z)
    sin_rows = -np.sin(2 * np.pi * ((np.arange(1, half)[:, None] * z) % size_z) / size_z)
    return np.concatenate([cos_rows, sin_rows], axis=0)


def y_tables(size_y):
    k = np.arange(size_y)
    ang = 2 * np.pi * ((k[:, None] * k[None, :]) % size_y) / size_y
    cos_t, sin_t = np.cos(ang), np.sin(ang)
    real_rows = np.concatenate([cos_t, sin_t], axis=1)
    imag_rows = np.concatenate([-sin_t, cos_t], axis=1)
    full = np.stack([real_rows, imag_rows], axis=0).reshape(2, size_y // 4, 4, 2 * size_y)
    full = full.transpose(1, 0, 2, 3).reshape(2 * size_y, 2 * size_y)
    return full, full[:, :size_y]


def roll_sub(x, shift):
    return pltpu.roll(x, shift % SUB, axis=x.ndim - 2)


def in_steps(count, at_once, step):
    def several(i, carry):
        for u in range(at_once):
            step(i * at_once + u)
        return carry

    lax.fori_loop(0, count // at_once, several, 0)
    for i in range(count // at_once * at_once, count):
        step(i)


def transform_kernel(
    col_ref,
    phase_ref,
    val_hbm,
    cond_ref,
    dz_ref,
    dy_ref,
    dyr_ref,
    cs_hbm,
    keep_hbm,
    send_hbm,
    val_scr,
    cs_scr,
    z_scr,
    tab_scr,
    out_scr,
    in_sems,
    out_sems,
):
    slots, size_y, size_z, lanes = val_hbm.shape
    half = size_z // 2
    groups_y = size_y // SUB
    pitch = size_z + SUB

    def plane(x):
        return pltpu.make_async_copy(val_hbm.at[x], val_scr.at[x], in_sems.at[x])

    phases = pltpu.make_async_copy(cs_hbm, cs_scr, in_sems.at[slots])
    for x in range(slots):
        plane(x).start()
    phases.start()

    def z_stage(x, yg):
        cond = cond_ref[x, yg]
        parts = []
        for j in range(SUB):
            block = val_scr[x, yg * SUB + j]
            parts.append(block * jnp.broadcast_to(cond[:, j : j + 1], (size_z, lanes)))
        rhs = split3(jnp.concatenate(parts, axis=1))
        got = jnp.dot(dz_ref[...], rhs, preferred_element_type=f32)
        for j in range(SUB):
            at = pl.multiple_of((yg * SUB + j) * pitch, SUB)
            z_scr[x, pl.ds(at, size_z), :] = got[:, j * lanes : (j + 1) * lanes]

    def z_plane(x, carry):
        plane(x).wait()
        in_steps(groups_y, 4, functools.partial(z_stage, x))
        return carry

    lax.fori_loop(0, slots, z_plane, 0)

    shape = (size_y // 4, SUB, lanes)
    sub = lax.broadcasted_iota(jnp.int32, shape, 1)
    low2 = (sub % 4) < 2
    low1 = (sub % 2) == 0

    def put(kz, got):
        a = [got[:, x * lanes : (x + 1) * lanes].reshape(shape) for x in range(slots)]
        p0 = jnp.where(low2, a[0], roll_sub(a[2], 2))
        p2 = jnp.where(low2, roll_sub(a[0], -2), a[2])
        p1 = jnp.where(low2, a[1], roll_sub(a[3], 2))
        p3 = jnp.where(low2, roll_sub(a[1], -2), a[3])
        tab_scr[kz, :, 0] = jnp.where(low1, p0, roll_sub(p1, 1))
        tab_scr[kz, :, 1] = jnp.where(low1, roll_sub(p0, -1), p1)
        tab_scr[kz, :, 2] = jnp.where(low1, p2, roll_sub(p3, 1))
        tab_scr[kz, :, 3] = jnp.where(low1, roll_sub(p2, -1), p3)

    def rows(k):
        return jnp.concatenate(
            [z_scr[x, pl.ds(k, size_y, stride=pitch), :] for x in range(slots)], axis=1
        )

    for kz in (0, half):
        put(kz, jnp.dot(dyr_ref[...], split3(rows(kz)), preferred_element_type=f32))

    def y_stage(step):
        kz = step + 1
        block = jnp.concatenate([rows(kz), rows(half + kz)], axis=0)
        put(kz, jnp.dot(dy_ref[...], split3(block), preferred_element_type=f32))

    in_steps(half - 1, 3, y_stage)

    sub1 = lax.broadcasted_iota(jnp.int32, (SUB, lanes), 0)
    m2 = (sub1 % 4) < 2
    m1 = (sub1 % 2) == 0
    kzs, kyq, _, _, _ = tab_scr.shape
    tab = tab_scr.reshape(kzs * kyq * 4 * SUB, lanes)
    quads = keep_hbm.shape[0]
    phases.wait()

    def quad(q):
        t = []
        for i in range(4):
            d = tab[pl.ds(pl.multiple_of(col_ref[q * 4 + i], SUB), SUB), :]
            at = pl.ds(pl.multiple_of(phase_ref[q * 4 + i], SUB), SUB)
            t.append(d * cs_scr[0, at, :] + roll_sub(d, 4) * cs_scr[1, at, :])
        v0 = jnp.where(m2, t[0], roll_sub(t[2], 2)) + jnp.where(m2, roll_sub(t[0], -2), t[2])
        v1 = jnp.where(m2, t[1], roll_sub(t[3], 2)) + jnp.where(m2, roll_sub(t[1], -2), t[3])
        out_scr[q] = jnp.where(m1, v0, roll_sub(v1, 1)) + jnp.where(m1, roll_sub(v0, -1), v1)

    at_once = math.gcd(quads // 2, SUB)
    copies = []
    for n, (out_hbm, first, at, size) in enumerate(
        (
            (send_hbm, quads, 0, quads),
            (keep_hbm, 0, 0, quads // 2),
            (keep_hbm, 0, quads // 2, quads // 2),
        )
    ):
        in_steps(size, at_once, lambda q, start=first + at: quad(start + q))
        copies.append(
            pltpu.make_async_copy(
                out_scr.at[pl.ds(first + at, size)], out_hbm.at[pl.ds(at, size)], out_sems.at[n]
            )
        )
        copies[-1].start()
    for copy in copies:
        copy.wait()


def transform(col, phase, val, cond, cs, num_g):
    slots, size_y, size_z, lanes = val.shape
    dz = jnp.asarray(split_np(z_table(size_z)))
    full, real_only = y_tables(size_y)
    dy, dyr = jnp.asarray(split_np(full)), jnp.asarray(split_np(real_only))
    vmem = pl.BlockSpec(memory_space=pltpu.VMEM)
    smem = pl.BlockSpec(memory_space=pltpu.SMEM)
    hbm = pl.BlockSpec(memory_space=pl.ANY)
    return pl.pallas_call(
        transform_kernel,
        out_shape=(jax.ShapeDtypeStruct((num_g // 8, SUB, lanes), f32),) * 2,
        in_specs=[smem, smem, hbm, vmem, vmem, vmem, vmem, hbm],
        out_specs=(hbm, hbm),
        scratch_shapes=[
            pltpu.VMEM(val.shape, f32),
            pltpu.VMEM(cs.shape, f32),
            pltpu.VMEM((slots, (size_z + SUB) * size_y, lanes), f32),
            pltpu.VMEM((size_z // 2 + 1, size_y // 4, 4, SUB, lanes), f32),
            pltpu.VMEM((num_g // 4, SUB, lanes), f32),
            pltpu.SemaphoreType.DMA((slots + 1,)),
            pltpu.SemaphoreType.DMA((3,)),
        ],
        name="transform",
    )(col, phase, val, cond, dz, dy, dyr, cs)


def split_lanes(block):
    high = block.astype(bf16)
    low = (block - high.astype(f32)).astype(bf16)
    return high, low


def fill_left(w_ref, own_ref, left_scr):
    freqs = w_ref.shape[0]
    rows, pairs2 = own_ref.shape

    def fill(w, carry):
        row = w_ref[pl.ds(w, 1), :]
        high, low = split_lanes(own_ref[...] * jnp.concatenate([row, row], axis=1))
        at = pl.ds(pl.multiple_of(w * rows, rows), rows)
        left_scr[at, :pairs2] = high
        left_scr[at, pairs2 : 2 * pairs2] = high
        left_scr[at, 2 * pairs2 :] = low
        return carry

    lax.fori_loop(0, freqs, fill, 0)


def chi_tile(block, left_scr, real_ref, imag_ref):
    freqs, rows, _ = real_ref.shape
    pairs = block.shape[1] // 2
    turned = jnp.concatenate([-block[:, pairs:], block[:, :pairs]], axis=1)
    for value, out_ref in ((block, real_ref), (turned, imag_ref)):
        high, low = split_lanes(value)
        right = jnp.concatenate([high, low, high], axis=1)
        got = lax.dot_general(
            left_scr[...], right, (((1,), (1,)), ((), ())), preferred_element_type=f32
        )
        out_ref[...] = got.reshape(freqs, rows, -1)


def chi_kernel(w_ref, own_ref, all_ref, real_ref, imag_ref, left_scr):
    @pl.when(pl.program_id(0) == 0)
    def _():
        fill_left(w_ref, own_ref, left_scr)

    chi_tile(all_ref[...], left_scr, real_ref, imag_ref)


def chi(weights, own, everyone):
    freqs, pairs = weights.shape
    rows = own.shape[0]
    num_g = everyone.shape[0]
    tile = min(num_g, 4 * LANES)
    out = jax.ShapeDtypeStruct((freqs, rows, num_g), f32)
    out_spec = pl.BlockSpec((freqs, rows, tile), lambda t: (0, 0, t))
    return pl.pallas_call(
        chi_kernel,
        grid=(num_g // tile,),
        out_shape=(out, out),
        in_specs=[
            pl.BlockSpec((freqs, pairs), lambda t: (0, 0)),
            pl.BlockSpec((rows, 2 * pairs), lambda t: (0, 0)),
            pl.BlockSpec((tile, 2 * pairs), lambda t: (t, 0)),
        ],
        out_specs=(out_spec, out_spec),
        scratch_shapes=[pltpu.VMEM((freqs * rows, 6 * pairs), bf16)],
        name="chi",
    )(weights, own, everyone)


def chi_group_kernel(counts, with_old, *refs):
    total = sum(counts)
    n = len(counts)
    _, w_ref, own_ref = refs[:3]
    pieces = refs[3 : 3 + total]
    rest = refs[3 + total + (2 if with_old else 0) :]
    real_ref, imag_ref, left_scr, got_scr, sems = rest
    step = pl.program_id(0)

    def copies(i):
        at, first = 0, sum(counts[:i])
        for j in range(counts[i]):
            ref = pieces[first + j]
            yield pltpu.make_async_copy(
                ref, got_scr.at[i, pl.ds(at, ref.shape[0])], sems.at[first + j]
            )
            at += ref.shape[0]

    @pl.when(step == 0)
    def _():
        for i in range(n):
            for copy in copies(i):
                copy.start()
        fill_left(w_ref, own_ref, left_scr)

    for i in range(n):

        @pl.when(step == i)
        def _(i=i):
            for copy in copies(i):
                copy.wait()

    chi_tile(got_scr[step], left_scr, real_ref, imag_ref)


def chi_group(weights, own, blocks, ids, first, num_g, old):
    freqs, pairs = weights.shape
    rows = own.shape[0]
    counts = tuple(len(b) for b in blocks)
    pieces = [p for b in blocks for p in b]
    out = jax.ShapeDtypeStruct((freqs, rows, num_g), f32)
    out_spec = pl.BlockSpec((freqs, rows, rows), lambda t, ids: (0, 0, ids[first + t]))
    hbm = pl.BlockSpec(memory_space=pl.ANY)
    olds = () if old is None else old
    return pl.pallas_call(
        functools.partial(chi_group_kernel, counts, old is not None),
        grid_spec=pltpu.PrefetchScalarGridSpec(
            num_scalar_prefetch=1,
            grid=(len(blocks),),
            in_specs=[
                pl.BlockSpec((freqs, pairs), lambda t, ids: (0, 0)),
                pl.BlockSpec((rows, 2 * pairs), lambda t, ids: (0, 0)),
            ]
            + [hbm] * (len(pieces) + len(olds)),
            out_specs=(out_spec, out_spec),
            scratch_shapes=[
                pltpu.VMEM((freqs * rows, 6 * pairs), bf16),
                pltpu.VMEM((len(blocks), rows, 2 * pairs), f32),
                pltpu.SemaphoreType.DMA((len(pieces),)),
            ],
        ),
        out_shape=(out, out),
        input_output_aliases={3 + len(pieces) + i: i for i in range(len(olds))},
        name="chi",
    )(ids, weights, own, *pieces, *olds)


GROUPS = (((0, 0),), ((1, 0),), ((0, 1), (0, 3)), ((0, 2),), ((1, 1), (1, 3)), ((1, 2),))
RING = (0, 2, 3, 1)


class Links:
    def __init__(self, count):
        def place(i):
            return i // 4, i // 2 % 2, i % 2

        def at(z, y, core):
            return z * 4 + y * 2 + core

        def turn(i, by):
            z, y, core = place(i)
            return at(RING[(RING.index(z) + by) % 4], y, core)

        every = range(count)
        self.core = [(i, i ^ 1) for i in every]
        self.y = [(i, i ^ 2) for i in every]
        self.cw = [(i, turn(i, 1)) for i in every]
        self.ccw = [(i, turn(i, -1)) for i in every]
        self.near = np.array(
            [
                [[[turn(i ^ (2 * b) ^ a, r) for r in range(4)] for b in range(2)] for a in range(2)]
                for i in every
            ],
            dtype=np.int32,
        )
        self.order = np.stack([self.near[:, :, b, r] for g in GROUPS for b, r in g], axis=1)

    @staticmethod
    def fits(count):
        return count == len(RING) * 4


def send(value, pairs):
    return lax.ppermute(value, "blk", pairs)


def reduce_scatter(keep, other, links, ahead):
    half = keep.shape[0] // 2
    got = send(other, links.core)
    far = send(keep[half:] + got[half:], links.y)
    if ahead:
        far, ahead = lax.optimization_barrier((far, ahead))
    near = keep[:half] + got[:half] + far
    block = half // 4
    part = block // 2
    cw = send(near[2 * block : 2 * block + part], links.cw)
    ccw = send(near[2 * block + part : 3 * block], links.ccw)
    cw, ccw = lax.optimization_barrier((cw, ccw))
    to_cw = jnp.concatenate([near[block : block + part] + cw, near[block + part : 2 * block]])
    to_ccw = jnp.concatenate([near[3 * block : 3 * block + part], near[3 * block + part :] + ccw])
    from_cw = send(to_cw, links.cw)
    from_ccw = send(to_ccw, links.ccw)
    from_cw, from_ccw = lax.optimization_barrier((from_cw, from_ccw))
    return near[:block], from_cw, from_ccw


def gather_and_chi(weights, own, links, ids, num_g):
    part = own.shape[0] // 2

    def over(pieces, pairs):
        return [send(p, pairs) for p in pieces]

    mine = {(0, 0): [own]}
    mine[0, 3] = over([own], links.cw)
    mine[0, 1] = over([own], links.ccw)
    mine[0, 2] = [send(mine[0, 3][0][:part], links.cw), send(mine[0, 1][0][part:], links.ccw)]
    for r in range(4):
        mine[1, r] = over(mine[0, r], links.y)
    old = None
    first = 0
    for group in GROUPS:
        blocks = []
        for b, r in group:
            blocks += [mine[b, r], over(mine[b, r], links.core)]
        old = chi_group(weights, own, blocks, ids, first, num_g, old)
        first += len(blocks)
    return old


def phase_table(size_x, first, planes, norm):
    x = first + jnp.arange(SLOTS, dtype=jnp.int32)
    k = jnp.arange(size_x, dtype=jnp.int32)
    ang = (k[:, None] * x[None, :] % size_x).astype(f32) * (2.0 * math.pi / size_x)
    live = (jnp.arange(SLOTS) < planes).astype(f32) * norm
    cos_t, sin_t = jnp.cos(ang) * live, jnp.sin(ang) * live
    plain = jnp.stack(
        [jnp.concatenate([cos_t, cos_t], 1), jnp.concatenate([sin_t, -sin_t], 1)]
    )
    mirror = jnp.stack(
        [jnp.concatenate([cos_t, -cos_t], 1), jnp.concatenate([-sin_t, -sin_t], 1)]
    )
    table = jnp.concatenate([plain, mirror], axis=1)
    return jnp.broadcast_to(table.reshape(2, -1, 1), (2, table[0].size, LANES))


def polarizability(psi_val, psi_cond, e_val, e_cond, occ, freq, gmap):
    num_val, planes, size_y, size_z = psi_val.shape
    num_cond = psi_cond.shape[0]
    num_g = gmap.shape[0]
    pairs = num_val * num_cond
    size_x = planes * lax.axis_size("blk")
    norm = 1.0 / math.sqrt(size_x * size_y * size_z)

    val = jnp.transpose(psi_val, (1, 2, 3, 0))
    cond = jnp.transpose(
        psi_cond.reshape(num_cond, planes, size_y // SUB, SUB, size_z), (0, 1, 2, 4, 3)
    )
    if planes < SLOTS:
        val = jnp.pad(val, ((0, SLOTS - planes), (0, 0), (0, 0), (0, 0)))
        cond = jnp.pad(cond, ((0, 0), (0, SLOTS - planes), (0, 0), (0, 0), (0, 0)))

    kz = gmap % size_z
    ky = gmap // size_z % size_y
    kx = gmap // (size_z * size_y)
    mirrored = kz > size_z // 2
    col = jnp.where(mirrored, size_z - kz, kz) * size_y + jnp.where(
        mirrored, (size_y - ky) % size_y, ky
    )
    pick = jnp.stack([col, kx + jnp.where(mirrored, size_x, 0)]) * SUB
    cs = phase_table(size_x, lax.axis_index("blk") * planes, planes, norm)

    count = lax.axis_size("blk")
    links = Links(count) if Links.fits(count) else None
    if links is not None:
        near = jnp.asarray(links.near)[lax.axis_index("blk")]
        ids = jnp.asarray(links.order.reshape(count, -1))[lax.axis_index("blk")]
        pick = pick.reshape(2, count, -1)[:, near.reshape(-1)].reshape(2, -1)
    owned = []
    for c in range(num_cond):
        keep, other = transform(pick[0], pick[1], val, cond[c], cs, num_g)
        if links is not None:
            ahead = owned[-1][1:] if c == num_cond - 1 else ()
            owned.append(reduce_scatter(keep, other, links, ahead))
        else:
            whole = jnp.concatenate([keep, other])
            owned.append((lax.psum_scatter(whole, "blk", scatter_dimension=0, tiled=True),))
    own = jnp.stack([sum(parts) for parts in owned]).reshape(num_cond, -1, 2, 4, num_val)
    own = jnp.transpose(own, (1, 3, 2, 0, 4)).reshape(-1, 2 * pairs)

    gaps = e_val[None, :] - e_cond[:, None]
    gaps = gaps.reshape(1, pairs)
    occ_row = jnp.broadcast_to(occ.astype(f32)[None, :], (num_cond, num_val)).reshape(1, pairs)
    weights = occ_row * gaps / (gaps * gaps + (freq * freq)[:, None]) / math.sqrt(pairs)

    if links is not None:
        return gather_and_chi(weights, own, links, ids, num_g)
    return chi(weights, own, lax.all_gather(own, "blk", axis=0, tiled=True))


def solution(mesh):
    step = jax.shard_map(
        polarizability,
        mesh=mesh,
        in_specs=(
            P("cell", "blk", None, None),
            P("cell", "blk", None, None),
            P("cell"),
            P("cell"),
            P("cell"),
            P("cell"),
            P("cell"),
        ),
        out_specs=(P("cell", "blk", None), P("cell", "blk", None)),
        check_vma=False,
    )
    if not Links.fits(mesh.shape["blk"]):
        return step
    return step
```

```python
import functools
import math

import jax
import jax.numpy as jnp
import ml_dtypes
import numpy as np
from jax import lax
from jax.experimental import pallas as pl
from jax.experimental.pallas import tpu as pltpu
from jax.sharding import PartitionSpec as P


VMEM_BYTES = 64 * 2**20
LANES = 128
SUB = 8
SLOTS = 4
f32 = jnp.float32
bf16 = jnp.bfloat16


def split_np(table):
    high = table.astype(ml_dtypes.bfloat16)
    low = (table - high.astype(np.float64)).astype(ml_dtypes.bfloat16)
    return np.concatenate([high, high, low], axis=1)


def split3(block):
    high = block.astype(bf16)
    low = (block - high.astype(f32)).astype(bf16)
    return jnp.concatenate([high, low, high], axis=0)


def z_table(size_z):
    half = size_z // 2
    z = np.arange(size_z)
    cos_rows = np.cos(2 * np.pi * ((np.arange(half + 1)[:, None] * z) % size_z) / size_z)
    sin_rows = -np.sin(2 * np.pi * ((np.arange(1, half)[:, None] * z) % size_z) / size_z)
    return np.concatenate([cos_rows, sin_rows], axis=0)


def y_tables(size_y):
    k = np.arange(size_y)
    ang = 2 * np.pi * ((k[:, None] * k[None, :]) % size_y) / size_y
    cos_t, sin_t = np.cos(ang), np.sin(ang)
    real_rows = np.concatenate([cos_t, sin_t], axis=1)
    imag_rows = np.concatenate([-sin_t, cos_t], axis=1)
    full = np.stack([real_rows, imag_rows], axis=0).reshape(2, size_y // 4, 4, 2 * size_y)
    full = full.transpose(1, 0, 2, 3).reshape(2 * size_y, 2 * size_y)
    return full, full[:, :size_y]


def roll_sub(x, shift):
    return pltpu.roll(x, shift % SUB, axis=x.ndim - 2)


def in_steps(count, at_once, step):
    def several(i, carry):
        for u in range(at_once):
            step(i * at_once + u)
        return carry

    lax.fori_loop(0, count // at_once, several, 0)
    for i in range(count // at_once * at_once, count):
        step(i)


def transform_kernel(
    col_ref,
    phase_ref,
    val_hbm,
    cond_ref,
    dz_ref,
    dy_ref,
    dyr_ref,
    cs_hbm,
    keep_hbm,
    send_hbm,
    val_scr,
    cs_scr,
    z_scr,
    tab_scr,
    out_scr,
    in_sems,
    out_sems,
):
    slots, size_y, size_z, lanes = val_hbm.shape
    half = size_z // 2
    groups_y = size_y // SUB
    pitch = size_z + SUB

    def plane(x):
        return pltpu.make_async_copy(val_hbm.at[x], val_scr.at[x], in_sems.at[x])

    phases = pltpu.make_async_copy(cs_hbm, cs_scr, in_sems.at[slots])
    for x in range(slots):
        plane(x).start()
    phases.start()

    def z_stage(x, yg):
        cond = cond_ref[x, yg]
        parts = []
        for j in range(SUB):
            block = val_scr[x, yg * SUB + j]
            parts.append(block * jnp.broadcast_to(cond[:, j : j + 1], (size_z, lanes)))
        rhs = split3(jnp.concatenate(parts, axis=1))
        got = jnp.dot(dz_ref[...], rhs, preferred_element_type=f32)
        for j in range(SUB):
            at = pl.multiple_of((yg * SUB + j) * pitch, SUB)
            z_scr[x, pl.ds(at, size_z), :] = got[:, j * lanes : (j + 1) * lanes]

    def z_plane(x, carry):
        plane(x).wait()
        in_steps(groups_y, 4, functools.partial(z_stage, x))
        return carry

    lax.fori_loop(0, slots, z_plane, 0)

    shape = (size_y // 4, SUB, lanes)
    sub = lax.broadcasted_iota(jnp.int32, shape, 1)
    low2 = (sub % 4) < 2
    low1 = (sub % 2) == 0

    def put(kz, got):
        a = [got[:, x * lanes : (x + 1) * lanes].reshape(shape) for x in range(slots)]
        p0 = jnp.where(low2, a[0], roll_sub(a[2], 2))
        p2 = jnp.where(low2, roll_sub(a[0], -2), a[2])
        p1 = jnp.where(low2, a[1], roll_sub(a[3], 2))
        p3 = jnp.where(low2, roll_sub(a[1], -2), a[3])
        tab_scr[kz, :, 0] = jnp.where(low1, p0, roll_sub(p1, 1))
        tab_scr[kz, :, 1] = jnp.where(low1, roll_sub(p0, -1), p1)
        tab_scr[kz, :, 2] = jnp.where(low1, p2, roll_sub(p3, 1))
        tab_scr[kz, :, 3] = jnp.where(low1, roll_sub(p2, -1), p3)

    def rows(k):
        return jnp.concatenate(
            [z_scr[x, pl.ds(k, size_y, stride=pitch), :] for x in range(slots)], axis=1
        )

    for kz in (0, half):
        put(kz, jnp.dot(dyr_ref[...], split3(rows(kz)), preferred_element_type=f32))

    def y_stage(step):
        kz = step + 1
        block = jnp.concatenate([rows(kz), rows(half + kz)], axis=0)
        put(kz, jnp.dot(dy_ref[...], split3(block), preferred_element_type=f32))

    in_steps(half - 1, 3, y_stage)

    sub1 = lax.broadcasted_iota(jnp.int32, (SUB, lanes), 0)
    m2 = (sub1 % 4) < 2
    m1 = (sub1 % 2) == 0
    kzs, kyq, _, _, _ = tab_scr.shape
    tab = tab_scr.reshape(kzs * kyq * 4 * SUB, lanes)
    quads = keep_hbm.shape[0]
    phases.wait()

    def quad(q):
        t = []
        for i in range(4):
            d = tab[pl.ds(pl.multiple_of(col_ref[q * 4 + i], SUB), SUB), :]
            at = pl.ds(pl.multiple_of(phase_ref[q * 4 + i], SUB), SUB)
            t.append(d * cs_scr[0, at, :] + roll_sub(d, 4) * cs_scr[1, at, :])
        v0 = jnp.where(m2, t[0], roll_sub(t[2], 2)) + jnp.where(m2, roll_sub(t[0], -2), t[2])
        v1 = jnp.where(m2, t[1], roll_sub(t[3], 2)) + jnp.where(m2, roll_sub(t[1], -2), t[3])
        out_scr[q] = jnp.where(m1, v0, roll_sub(v1, 1)) + jnp.where(m1, roll_sub(v0, -1), v1)

    at_once = math.gcd(quads // 2, SUB)
    copies = []
    for n, (out_hbm, first, at, size) in enumerate(
        (
            (send_hbm, quads, 0, quads),
            (keep_hbm, 0, 0, quads // 2),
            (keep_hbm, 0, quads // 2, quads // 2),
        )
    ):
        in_steps(size, at_once, lambda q, start=first + at: quad(start + q))
        copies.append(
            pltpu.make_async_copy(
                out_scr.at[pl.ds(first + at, size)], out_hbm.at[pl.ds(at, size)], out_sems.at[n]
            )
        )
        copies[-1].start()
    for copy in copies:
        copy.wait()


def transform(col, phase, val, cond, cs, num_g):
    slots, size_y, size_z, lanes = val.shape
    dz = jnp.asarray(split_np(z_table(size_z)))
    full, real_only = y_tables(size_y)
    dy, dyr = jnp.asarray(split_np(full)), jnp.asarray(split_np(real_only))
    vmem = pl.BlockSpec(memory_space=pltpu.VMEM)
    smem = pl.BlockSpec(memory_space=pltpu.SMEM)
    hbm = pl.BlockSpec(memory_space=pl.ANY)
    return pl.pallas_call(
        transform_kernel,
        out_shape=(jax.ShapeDtypeStruct((num_g // 8, SUB, lanes), f32),) * 2,
        in_specs=[smem, smem, hbm, vmem, vmem, vmem, vmem, hbm],
        out_specs=(hbm, hbm),
        scratch_shapes=[
            pltpu.VMEM(val.shape, f32),
            pltpu.VMEM(cs.shape, f32),
            pltpu.VMEM((slots, (size_z + SUB) * size_y, lanes), f32),
            pltpu.VMEM((size_z // 2 + 1, size_y // 4, 4, SUB, lanes), f32),
            pltpu.VMEM((num_g // 4, SUB, lanes), f32),
            pltpu.SemaphoreType.DMA((slots + 1,)),
            pltpu.SemaphoreType.DMA((3,)),
        ],
        compiler_params=pltpu.CompilerParams(vmem_limit_bytes=VMEM_BYTES),
        name="transform",
    )(col, phase, val, cond, dz, dy, dyr, cs)


def split_lanes(block):
    high = block.astype(bf16)
    low = (block - high.astype(f32)).astype(bf16)
    return high, low


def fill_left(w_ref, own_ref, left_scr):
    freqs = w_ref.shape[0]
    rows, pairs2 = own_ref.shape

    def fill(w, carry):
        row = w_ref[pl.ds(w, 1), :]
        high, low = split_lanes(own_ref[...] * jnp.concatenate([row, row], axis=1))
        at = pl.ds(pl.multiple_of(w * rows, rows), rows)
        left_scr[at, :pairs2] = high
        left_scr[at, pairs2 : 2 * pairs2] = high
        left_scr[at, 2 * pairs2 :] = low
        return carry

    lax.fori_loop(0, freqs, fill, 0)


def chi_tile(block, left_scr, real_ref, imag_ref):
    freqs, rows, _ = real_ref.shape
    pairs = block.shape[1] // 2
    turned = jnp.concatenate([-block[:, pairs:], block[:, :pairs]], axis=1)
    for value, out_ref in ((block, real_ref), (turned, imag_ref)):
        high, low = split_lanes(value)
        right = jnp.concatenate([high, low, high], axis=1)
        got = lax.dot_general(
            left_scr[...], right, (((1,), (1,)), ((), ())), preferred_element_type=f32
        )
        out_ref[...] = got.reshape(freqs, rows, -1)


def chi_kernel(w_ref, own_ref, all_ref, real_ref, imag_ref, left_scr):
    @pl.when(pl.program_id(0) == 0)
    def _():
        fill_left(w_ref, own_ref, left_scr)

    chi_tile(all_ref[...], left_scr, real_ref, imag_ref)


def chi(weights, own, everyone):
    freqs, pairs = weights.shape
    rows = own.shape[0]
    num_g = everyone.shape[0]
    tile = min(num_g, 4 * LANES)
    out = jax.ShapeDtypeStruct((freqs, rows, num_g), f32)
    out_spec = pl.BlockSpec((freqs, rows, tile), lambda t: (0, 0, t))
    return pl.pallas_call(
        chi_kernel,
        grid=(num_g // tile,),
        out_shape=(out, out),
        in_specs=[
            pl.BlockSpec((freqs, pairs), lambda t: (0, 0)),
            pl.BlockSpec((rows, 2 * pairs), lambda t: (0, 0)),
            pl.BlockSpec((tile, 2 * pairs), lambda t: (t, 0)),
        ],
        out_specs=(out_spec, out_spec),
        scratch_shapes=[pltpu.VMEM((freqs * rows, 6 * pairs), bf16)],
        name="chi",
    )(weights, own, everyone)


def chi_group_kernel(counts, with_old, *refs):
    total = sum(counts)
    n = len(counts)
    _, w_ref, own_ref = refs[:3]
    pieces = refs[3 : 3 + total]
    rest = refs[3 + total + (2 if with_old else 0) :]
    real_ref, imag_ref, left_scr, got_scr, sems = rest
    step = pl.program_id(0)

    def copies(i):
        at, first = 0, sum(counts[:i])
        for j in range(counts[i]):
            ref = pieces[first + j]
            yield pltpu.make_async_copy(
                ref, got_scr.at[i, pl.ds(at, ref.shape[0])], sems.at[first + j]
            )
            at += ref.shape[0]

    @pl.when(step == 0)
    def _():
        for i in range(n):
            for copy in copies(i):
                copy.start()
        fill_left(w_ref, own_ref, left_scr)

    for i in range(n):

        @pl.when(step == i)
        def _(i=i):
            for copy in copies(i):
                copy.wait()

    chi_tile(got_scr[step], left_scr, real_ref, imag_ref)


def chi_group(weights, own, blocks, ids, first, num_g, old):
    freqs, pairs = weights.shape
    rows = own.shape[0]
    counts = tuple(len(b) for b in blocks)
    pieces = [p for b in blocks for p in b]
    out = jax.ShapeDtypeStruct((freqs, rows, num_g), f32)
    out_spec = pl.BlockSpec((freqs, rows, rows), lambda t, ids: (0, 0, ids[first + t]))
    hbm = pl.BlockSpec(memory_space=pl.ANY)
    olds = () if old is None else old
    return pl.pallas_call(
        functools.partial(chi_group_kernel, counts, old is not None),
        grid_spec=pltpu.PrefetchScalarGridSpec(
            num_scalar_prefetch=1,
            grid=(len(blocks),),
            in_specs=[
                pl.BlockSpec((freqs, pairs), lambda t, ids: (0, 0)),
                pl.BlockSpec((rows, 2 * pairs), lambda t, ids: (0, 0)),
            ]
            + [hbm] * (len(pieces) + len(olds)),
            out_specs=(out_spec, out_spec),
            scratch_shapes=[
                pltpu.VMEM((freqs * rows, 6 * pairs), bf16),
                pltpu.VMEM((len(blocks), rows, 2 * pairs), f32),
                pltpu.SemaphoreType.DMA((len(pieces),)),
            ],
        ),
        out_shape=(out, out),
        input_output_aliases={3 + len(pieces) + i: i for i in range(len(olds))},
        compiler_params=pltpu.CompilerParams(vmem_limit_bytes=VMEM_BYTES),
        name="chi",
    )(ids, weights, own, *pieces, *olds)


GROUPS = (((0, 0),), ((1, 0), (0, 3)), ((0, 1), (1, 3)), ((0, 2), (1, 1)), ((1, 2),))
RING = (0, 2, 3, 1)


class Links:
    def __init__(self, count):
        def place(i):
            return i // 4, i // 2 % 2, i % 2

        def at(z, y, core):
            return z * 4 + y * 2 + core

        def turn(i, by):
            z, y, core = place(i)
            return at(RING[(RING.index(z) + by) % 4], y, core)

        every = range(count)
        self.core = [(i, i ^ 1) for i in every]
        self.y = [(i, i ^ 2) for i in every]
        self.cw = [(i, turn(i, 1)) for i in every]
        self.ccw = [(i, turn(i, -1)) for i in every]
        self.near = np.array(
            [
                [[[turn(i ^ (2 * b) ^ a, r) for r in range(4)] for b in range(2)] for a in range(2)]
                for i in every
            ],
            dtype=np.int32,
        )
        whole = np.arange(2 * count).reshape(count, 2)[self.near]
        first = whole[..., 0].reshape(count, 2, -1)
        second = whole[..., 1].swapaxes(2, 3).reshape(count, 2, -1)
        self.whole = whole.reshape(count, -1)
        self.halved = np.concatenate([first, second], axis=2).reshape(count, -1)
        self.order = np.stack([self.near[:, :, b, r] for g in GROUPS for b, r in g], axis=1)

    @staticmethod
    def fits(count):
        return count == len(RING) * 4


def send(value, pairs):
    return lax.ppermute(value, "blk", pairs)


def ring(near, links):
    block = near.shape[0] // 4
    part = block // 2
    to_cw, to_ccw, near = lax.optimization_barrier(
        (near[2 * block : 2 * block + part], near[2 * block + part : 3 * block], near)
    )
    cw = send(to_cw, links.cw)
    ccw = send(to_ccw, links.ccw)
    to_cw = jnp.concatenate([near[block : block + part] + cw, near[block + part : 2 * block]])
    to_ccw = jnp.concatenate([near[3 * block : 3 * block + part], near[3 * block + part :] + ccw])
    from_cw = send(to_cw, links.cw)
    from_ccw = send(to_ccw, links.ccw)
    return near[:block], from_cw, from_ccw


def reduce_scatter(keep, other, links):
    half = keep.shape[0] // 2
    got = send(other, links.core)
    far = send(keep[half:] + got[half:], links.y)
    return ring(keep[:half] + got[:half] + far, links)


def reduce_scatter_halves(keep, other, links):
    half = keep.shape[0] // 2
    part = half // 2
    got = send(other, links.core)
    far = send(keep[part:half] + got[part:half], links.y)
    mine, cw, ccw = ring(keep[half:] + got[half:], links)
    last = mine.shape[0] // 2
    late = send(mine[last:] + cw[last:] + ccw[last:], links.y)
    first = sum(ring(keep[:part] + got[:part] + far, links))
    return jnp.concatenate([first, mine[:last] + cw[:last] + ccw[:last] + late])


def gather_and_chi(weights, own, links, ids, num_g):
    part = own.shape[0] // 2

    def over(pieces, pairs):
        return [send(p, pairs) for p in pieces]

    cw = send(own, links.cw)
    later, cw = lax.optimization_barrier((own, cw))
    ccw = send(later, links.ccw)
    cw_later, ccw = lax.optimization_barrier((cw, ccw))
    mine = {(0, 0): [own], (0, 3): [cw], (0, 1): [ccw]}
    mine[0, 2] = [send(cw_later[:part], links.cw), send(ccw[part:], links.ccw)]
    for r in range(4):
        mine[1, r] = over(mine[0, r], links.y)
    old = None
    first = 0
    for group in GROUPS:
        blocks = []
        for b, r in group:
            blocks += [mine[b, r], over(mine[b, r], links.core)]
        old = chi_group(weights, own, blocks, ids, first, num_g, old)
        first += len(blocks)
    return old


def phase_table(size_x, first, planes, norm):
    x = first + jnp.arange(SLOTS, dtype=jnp.int32)
    k = jnp.arange(size_x, dtype=jnp.int32)
    ang = (k[:, None] * x[None, :] % size_x).astype(f32) * (2.0 * math.pi / size_x)
    live = (jnp.arange(SLOTS) < planes).astype(f32) * norm
    cos_t, sin_t = jnp.cos(ang) * live, jnp.sin(ang) * live
    plain = jnp.stack(
        [jnp.concatenate([cos_t, cos_t], 1), jnp.concatenate([sin_t, -sin_t], 1)]
    )
    mirror = jnp.stack(
        [jnp.concatenate([cos_t, -cos_t], 1), jnp.concatenate([-sin_t, -sin_t], 1)]
    )
    table = jnp.concatenate([plain, mirror], axis=1)
    return jnp.broadcast_to(table.reshape(2, -1, 1), (2, table[0].size, LANES))


def polarizability(psi_val, psi_cond, e_val, e_cond, occ, freq, gmap):
    num_val, planes, size_y, size_z = psi_val.shape
    num_cond = psi_cond.shape[0]
    num_g = gmap.shape[0]
    pairs = num_val * num_cond
    size_x = planes * lax.axis_size("blk")
    norm = 1.0 / math.sqrt(size_x * size_y * size_z)

    val = jnp.transpose(psi_val, (1, 2, 3, 0))
    cond = jnp.transpose(
        psi_cond.reshape(num_cond, planes, size_y // SUB, SUB, size_z), (0, 1, 2, 4, 3)
    )
    if planes < SLOTS:
        val = jnp.pad(val, ((0, SLOTS - planes), (0, 0), (0, 0), (0, 0)))
        cond = jnp.pad(cond, ((0, 0), (0, SLOTS - planes), (0, 0), (0, 0), (0, 0)))

    kz = gmap % size_z
    ky = gmap // size_z % size_y
    kx = gmap // (size_z * size_y)
    mirrored = kz > size_z // 2
    col = jnp.where(mirrored, size_z - kz, kz) * size_y + jnp.where(
        mirrored, (size_y - ky) % size_y, ky
    )
    pick = jnp.stack([col, kx + jnp.where(mirrored, size_x, 0)]) * SUB
    cs = phase_table(size_x, lax.axis_index("blk") * planes, planes, norm)

    count = lax.axis_size("blk")
    links = Links(count) if Links.fits(count) else None
    if links is not None:
        tables = np.concatenate([links.whole, links.halved, links.order.reshape(count, -1)], axis=1)
        table = jnp.asarray(tables)[lax.axis_index("blk")]
        picks = pick.reshape(2, 2 * count, -1)[:, table[: 4 * count]].reshape(2, 2, -1)
        ids = table[4 * count :]
    owned = []
    for c in range(num_cond):
        last = c == num_cond - 1
        chosen = pick if links is None else picks[:, int(last)]
        keep, other = transform(chosen[0], chosen[1], val, cond[c], cs, num_g)
        if links is None:
            whole = jnp.concatenate([keep, other])
            owned.append((lax.psum_scatter(whole, "blk", scatter_dimension=0, tiled=True),))
        elif last:
            owned.append((reduce_scatter_halves(keep, other, links),))
        else:
            owned.append(reduce_scatter(keep, other, links))
    for c, parts in enumerate(owned):
        owned[c] = sum(parts[1:], parts[0])
    own = jnp.stack(owned).reshape(num_cond, -1, 2, 4, num_val)
    own = jnp.transpose(own, (1, 3, 2, 0, 4)).reshape(-1, 2 * pairs)

    gaps = e_val[None, :] - e_cond[:, None]
    gaps = gaps.reshape(1, pairs)
    occ_row = jnp.broadcast_to(occ.astype(f32)[None, :], (num_cond, num_val)).reshape(1, pairs)
    weights = occ_row * gaps / (gaps * gaps + (freq * freq)[:, None]) / math.sqrt(pairs)

    if links is not None:
        return gather_and_chi(weights, own, links, ids, num_g)
    return chi(weights, own, lax.all_gather(own, "blk", axis=0, tiled=True))


def solution(mesh):
    step = jax.shard_map(
        polarizability,
        mesh=mesh,
        in_specs=(
            P("cell", "blk", None, None),
            P("cell", "blk", None, None),
            P("cell"),
            P("cell"),
            P("cell"),
            P("cell"),
            P("cell"),
        ),
        out_specs=(P("cell", "blk", None), P("cell", "blk", None)),
        check_vma=False,
    )
    if not Links.fits(mesh.shape["blk"]):
        return step
    return step
```

```python
import functools
import math

import jax
import jax.numpy as jnp
import ml_dtypes
import numpy as np
from jax import lax
from jax.experimental import pallas as pl
from jax.experimental.pallas import tpu as pltpu
from jax.sharding import PartitionSpec as P


VMEM_BYTES = 64 * 2**20
LANES = 128
SUB = 8
SLOTS = 4
f32 = jnp.float32
bf16 = jnp.bfloat16


def split_np(table):
    high = table.astype(ml_dtypes.bfloat16)
    low = (table - high.astype(np.float64)).astype(ml_dtypes.bfloat16)
    return np.concatenate([high, high, low], axis=1)


def split3(block):
    high = block.astype(bf16)
    low = (block - high.astype(f32)).astype(bf16)
    return jnp.concatenate([high, low, high], axis=0)


def z_table(size_z):
    half = size_z // 2
    z = np.arange(size_z)
    cos_rows = np.cos(2 * np.pi * ((np.arange(half + 1)[:, None] * z) % size_z) / size_z)
    sin_rows = -np.sin(2 * np.pi * ((np.arange(1, half)[:, None] * z) % size_z) / size_z)
    return np.concatenate([cos_rows, sin_rows], axis=0)


def y_tables(size_y):
    k = np.arange(size_y)
    ang = 2 * np.pi * ((k[:, None] * k[None, :]) % size_y) / size_y
    cos_t, sin_t = np.cos(ang), np.sin(ang)
    real_rows = np.concatenate([cos_t, sin_t], axis=1)
    imag_rows = np.concatenate([-sin_t, cos_t], axis=1)
    full = np.stack([real_rows, imag_rows], axis=0).reshape(2, size_y // 4, 4, 2 * size_y)
    full = full.transpose(1, 0, 2, 3).reshape(2 * size_y, 2 * size_y)
    return full, full[:, :size_y]


def roll_sub(x, shift):
    return pltpu.roll(x, shift % SUB, axis=x.ndim - 2)


def in_steps(count, at_once, step):
    def several(i, carry):
        for u in range(at_once):
            step(i * at_once + u)
        return carry

    lax.fori_loop(0, count // at_once, several, 0)
    for i in range(count // at_once * at_once, count):
        step(i)


def transform_kernel(
    col_ref,
    phase_ref,
    val_hbm,
    cond_ref,
    dz_ref,
    dy_ref,
    dyr_ref,
    cs_hbm,
    keep_hbm,
    send_hbm,
    val_scr,
    cs_scr,
    z_scr,
    tab_scr,
    out_scr,
    in_sems,
    out_sems,
):
    slots, size_y, size_z, lanes = val_hbm.shape
    half = size_z // 2
    groups_y = size_y // SUB
    pitch = size_z + SUB

    def plane(x):
        return pltpu.make_async_copy(val_hbm.at[x], val_scr.at[x], in_sems.at[x])

    phases = pltpu.make_async_copy(cs_hbm, cs_scr, in_sems.at[slots])
    for x in range(slots):
        plane(x).start()
    phases.start()

    def z_stage(x, yg):
        cond = cond_ref[x, yg]
        parts = []
        for j in range(SUB):
            block = val_scr[x, yg * SUB + j]
            parts.append(block * jnp.broadcast_to(cond[:, j : j + 1], (size_z, lanes)))
        rhs = split3(jnp.concatenate(parts, axis=1))
        got = jnp.dot(dz_ref[...], rhs, preferred_element_type=f32)
        for j in range(SUB):
            at = pl.multiple_of((yg * SUB + j) * pitch, SUB)
            z_scr[x, pl.ds(at, size_z), :] = got[:, j * lanes : (j + 1) * lanes]

    def z_plane(x, carry):
        plane(x).wait()
        in_steps(groups_y, 4, functools.partial(z_stage, x))
        return carry

    lax.fori_loop(0, slots, z_plane, 0)

    shape = (size_y // 4, SUB, lanes)
    sub = lax.broadcasted_iota(jnp.int32, shape, 1)
    low2 = (sub % 4) < 2
    low1 = (sub % 2) == 0

    def put(kz, got):
        a = [got[:, x * lanes : (x + 1) * lanes].reshape(shape) for x in range(slots)]
        p0 = jnp.where(low2, a[0], roll_sub(a[2], 2))
        p2 = jnp.where(low2, roll_sub(a[0], -2), a[2])
        p1 = jnp.where(low2, a[1], roll_sub(a[3], 2))
        p3 = jnp.where(low2, roll_sub(a[1], -2), a[3])
        tab_scr[kz, :, 0] = jnp.where(low1, p0, roll_sub(p1, 1))
        tab_scr[kz, :, 1] = jnp.where(low1, roll_sub(p0, -1), p1)
        tab_scr[kz, :, 2] = jnp.where(low1, p2, roll_sub(p3, 1))
        tab_scr[kz, :, 3] = jnp.where(low1, roll_sub(p2, -1), p3)

    def rows(k):
        return jnp.concatenate(
            [z_scr[x, pl.ds(k, size_y, stride=pitch), :] for x in range(slots)], axis=1
        )

    for kz in (0, half):
        put(kz, jnp.dot(dyr_ref[...], split3(rows(kz)), preferred_element_type=f32))

    def y_stage(step):
        kz = step + 1
        block = jnp.concatenate([rows(kz), rows(half + kz)], axis=0)
        put(kz, jnp.dot(dy_ref[...], split3(block), preferred_element_type=f32))

    in_steps(half - 1, 3, y_stage)

    sub1 = lax.broadcasted_iota(jnp.int32, (SUB, lanes), 0)
    m2 = (sub1 % 4) < 2
    m1 = (sub1 % 2) == 0
    kzs, kyq, _, _, _ = tab_scr.shape
    tab = tab_scr.reshape(kzs * kyq * 4 * SUB, lanes)
    quads = keep_hbm.shape[0]
    phases.wait()

    def quad(q):
        t = []
        for i in range(4):
            d = tab[pl.ds(pl.multiple_of(col_ref[q * 4 + i], SUB), SUB), :]
            at = pl.ds(pl.multiple_of(phase_ref[q * 4 + i], SUB), SUB)
            t.append(d * cs_scr[0, at, :] + roll_sub(d, 4) * cs_scr[1, at, :])
        v0 = jnp.where(m2, t[0], roll_sub(t[2], 2)) + jnp.where(m2, roll_sub(t[0], -2), t[2])
        v1 = jnp.where(m2, t[1], roll_sub(t[3], 2)) + jnp.where(m2, roll_sub(t[1], -2), t[3])
        out_scr[q] = jnp.where(m1, v0, roll_sub(v1, 1)) + jnp.where(m1, roll_sub(v0, -1), v1)

    at_once = math.gcd(quads // 2, SUB)
    copies = []
    for n, (out_hbm, first, at, size) in enumerate(
        (
            (send_hbm, quads, 0, quads),
            (keep_hbm, 0, 0, quads // 2),
            (keep_hbm, 0, quads // 2, quads // 2),
        )
    ):
        in_steps(size, at_once, lambda q, start=first + at: quad(start + q))
        copies.append(
            pltpu.make_async_copy(
                out_scr.at[pl.ds(first + at, size)], out_hbm.at[pl.ds(at, size)], out_sems.at[n]
            )
        )
        copies[-1].start()
    for copy in copies:
        copy.wait()


def transform(col, phase, val, cond, cs, num_g):
    slots, size_y, size_z, lanes = val.shape
    dz = jnp.asarray(split_np(z_table(size_z)))
    full, real_only = y_tables(size_y)
    dy, dyr = jnp.asarray(split_np(full)), jnp.asarray(split_np(real_only))
    vmem = pl.BlockSpec(memory_space=pltpu.VMEM)
    smem = pl.BlockSpec(memory_space=pltpu.SMEM)
    hbm = pl.BlockSpec(memory_space=pl.ANY)
    return pl.pallas_call(
        transform_kernel,
        out_shape=(jax.ShapeDtypeStruct((num_g // 8, SUB, lanes), f32),) * 2,
        in_specs=[smem, smem, hbm, vmem, vmem, vmem, vmem, hbm],
        out_specs=(hbm, hbm),
        scratch_shapes=[
            pltpu.VMEM(val.shape, f32),
            pltpu.VMEM(cs.shape, f32),
            pltpu.VMEM((slots, (size_z + SUB) * size_y, lanes), f32),
            pltpu.VMEM((size_z // 2 + 1, size_y // 4, 4, SUB, lanes), f32),
            pltpu.VMEM((num_g // 4, SUB, lanes), f32),
            pltpu.SemaphoreType.DMA((slots + 1,)),
            pltpu.SemaphoreType.DMA((3,)),
        ],
        compiler_params=pltpu.CompilerParams(vmem_limit_bytes=VMEM_BYTES),
        name="transform",
    )(col, phase, val, cond, dz, dy, dyr, cs)


def split_lanes(block):
    high = block.astype(bf16)
    low = (block - high.astype(f32)).astype(bf16)
    return high, low


def fill_left(w_ref, own_ref, left_scr):
    freqs = w_ref.shape[0]
    rows, pairs2 = own_ref.shape

    def fill(w, carry):
        row = w_ref[pl.ds(w, 1), :]
        high, low = split_lanes(own_ref[...] * jnp.concatenate([row, row], axis=1))
        at = pl.ds(pl.multiple_of(w * rows, rows), rows)
        left_scr[at, :pairs2] = high
        left_scr[at, pairs2 : 2 * pairs2] = high
        left_scr[at, 2 * pairs2 :] = low
        return carry

    lax.fori_loop(0, freqs, fill, 0)


def chi_tile(block, left_scr, real_ref, imag_ref):
    freqs, rows, _ = real_ref.shape
    pairs = block.shape[1] // 2
    turned = jnp.concatenate([-block[:, pairs:], block[:, :pairs]], axis=1)
    for value, out_ref in ((block, real_ref), (turned, imag_ref)):
        high, low = split_lanes(value)
        right = jnp.concatenate([high, low, high], axis=1)
        got = lax.dot_general(
            left_scr[...], right, (((1,), (1,)), ((), ())), preferred_element_type=f32
        )
        out_ref[...] = got.reshape(freqs, rows, -1)


def chi_kernel(w_ref, own_ref, all_ref, real_ref, imag_ref, left_scr):
    @pl.when(pl.program_id(0) == 0)
    def _():
        fill_left(w_ref, own_ref, left_scr)

    chi_tile(all_ref[...], left_scr, real_ref, imag_ref)


def chi(weights, own, everyone):
    freqs, pairs = weights.shape
    rows = own.shape[0]
    num_g = everyone.shape[0]
    tile = min(num_g, 4 * LANES)
    out = jax.ShapeDtypeStruct((freqs, rows, num_g), f32)
    out_spec = pl.BlockSpec((freqs, rows, tile), lambda t: (0, 0, t))
    return pl.pallas_call(
        chi_kernel,
        grid=(num_g // tile,),
        out_shape=(out, out),
        in_specs=[
            pl.BlockSpec((freqs, pairs), lambda t: (0, 0)),
            pl.BlockSpec((rows, 2 * pairs), lambda t: (0, 0)),
            pl.BlockSpec((tile, 2 * pairs), lambda t: (t, 0)),
        ],
        out_specs=(out_spec, out_spec),
        scratch_shapes=[pltpu.VMEM((freqs * rows, 6 * pairs), bf16)],
        name="chi",
    )(weights, own, everyone)


def chi_group_kernel(n, first, ids_ref, w_ref, own_ref, *refs):
    pieces = refs[:n]
    outs = refs[-7:-5]
    left_scr, got_scr, out_scr, in_sems, out_sems = refs[-5:]
    rows, pairs2 = own_ref.shape
    freqs = w_ref.shape[0]

    def piece(i):
        return pltpu.make_async_copy(pieces[i], got_scr.at[i], in_sems.at[i])

    def result(i, half):
        at = pl.ds(pl.multiple_of(ids_ref[first + i] * rows, rows), rows)
        slot = i % 2
        return pltpu.make_async_copy(
            out_scr.at[slot, half], outs[half].at[:, :, at], out_sems.at[slot, half]
        )

    for i in range(n):
        piece(i).start()
    fill_left(w_ref, own_ref, left_scr)
    for i in range(n):
        piece(i).wait()

    def block(i, carry):
        value = got_scr[i]
        turned = jnp.concatenate([-value[:, pairs2 // 2 :], value[:, : pairs2 // 2]], axis=1)
        for half, side in enumerate((value, turned)):
            high, low = split_lanes(side)
            right = jnp.concatenate([high, low, high], axis=1)

            @pl.when(i >= 2)
            def _(half=half):
                result(i - 2, half).wait()

            got = lax.dot_general(
                left_scr[...], right, (((1,), (1,)), ((), ())), preferred_element_type=f32
            )
            out_scr[i % 2, half] = got.reshape(freqs, rows, rows)
            result(i, half).start()
        return carry

    lax.fori_loop(0, n, block, 0)
    for i in range(max(n - 2, 0), n):
        for half in range(2):
            result(i, half).wait()


def chi_group(weights, own, blocks, ids, first, num_g, old):
    freqs, pairs = weights.shape
    rows = own.shape[0]
    n = len(blocks)
    out = jax.ShapeDtypeStruct((freqs, rows, num_g), f32)
    hbm = pl.BlockSpec(memory_space=pl.ANY)
    vmem = pl.BlockSpec(memory_space=pltpu.VMEM)
    olds = () if old is None else old
    return pl.pallas_call(
        functools.partial(chi_group_kernel, n, first),
        in_specs=[pl.BlockSpec(memory_space=pltpu.SMEM), vmem, vmem] + [hbm] * (n + len(olds)),
        out_specs=(hbm, hbm),
        scratch_shapes=[
            pltpu.VMEM((freqs * rows, 6 * pairs), bf16),
            pltpu.VMEM((n, rows, 2 * pairs), f32),
            pltpu.VMEM((2, 2, freqs, rows, rows), f32),
            pltpu.SemaphoreType.DMA((n,)),
            pltpu.SemaphoreType.DMA((2, 2)),
        ],
        out_shape=(out, out),
        input_output_aliases={3 + n + i: i for i in range(len(olds))},
        compiler_params=pltpu.CompilerParams(vmem_limit_bytes=VMEM_BYTES),
        name="chi",
    )(ids, weights, own, *blocks, *olds)


GROUPS = (((0, 0),), ((1, 0), (0, 3)), ((0, 1), (1, 3)), ((0, 2), (1, 1)), ((1, 2),))
RING = (0, 2, 3, 1)


class Links:
    def __init__(self, count):
        def place(i):
            return i // 4, i // 2 % 2, i % 2

        def at(z, y, core):
            return z * 4 + y * 2 + core

        def turn(i, by):
            z, y, core = place(i)
            return at(RING[(RING.index(z) + by) % 4], y, core)

        every = range(count)
        self.core = [(i, i ^ 1) for i in every]
        self.y = [(i, i ^ 2) for i in every]
        self.cw = [(i, turn(i, 1)) for i in every]
        self.ccw = [(i, turn(i, -1)) for i in every]
        self.near = np.array(
            [
                [[[turn(i ^ (2 * b) ^ a, r) for r in range(4)] for b in range(2)] for a in range(2)]
                for i in every
            ],
            dtype=np.int32,
        )
        self.order = np.stack([self.near[:, :, b, r] for g in GROUPS for b, r in g], axis=1)

    @staticmethod
    def fits(count):
        return count == len(RING) * 4


def send(value, pairs):
    return lax.ppermute(value, "blk", pairs)


def reduce_scatter(keep, other, links, before):
    half = keep.shape[0] // 2
    got = send(other, links.core)
    far = send(keep[half:] + got[half:], links.y)
    if before:
        far, *_ = lax.optimization_barrier((far, *before))
    near = keep[:half] + got[:half] + far
    block = half // 4
    to_cw, to_ccw, next_cw, mine = lax.optimization_barrier(
        tuple(near[i * block : (i + 1) * block] for i in (2, 3, 1, 0))
    )
    two_back = send(to_cw, links.cw)
    ahead = send(to_ccw, links.ccw)
    next_cw = next_cw + two_back
    back = send(next_cw, links.cw)
    return mine, ahead, back


def gather_and_chi(weights, own, links, ids, num_g):
    cw = send(own, links.cw)
    later, cw = lax.optimization_barrier((own, cw))
    ccw = send(later, links.ccw)
    cw_later, ccw = lax.optimization_barrier((cw, ccw))
    mine = {(0, 0): own, (0, 3): cw, (0, 1): ccw, (0, 2): send(cw_later, links.cw)}
    for r in range(4):
        mine[1, r] = send(mine[0, r], links.y)
    old = None
    first = 0
    for group in GROUPS:
        blocks = []
        for b, r in group:
            blocks += [mine[b, r], send(mine[b, r], links.core)]
        old = chi_group(weights, own, blocks, ids, first, num_g, old)
        first += len(blocks)
    return old


def phase_table(size_x, first, planes, norm):
    x = first + jnp.arange(SLOTS, dtype=jnp.int32)
    k = jnp.arange(size_x, dtype=jnp.int32)
    ang = (k[:, None] * x[None, :] % size_x).astype(f32) * (2.0 * math.pi / size_x)
    live = (jnp.arange(SLOTS) < planes).astype(f32) * norm
    cos_t, sin_t = jnp.cos(ang) * live, jnp.sin(ang) * live
    plain = jnp.stack(
        [jnp.concatenate([cos_t, cos_t], 1), jnp.concatenate([sin_t, -sin_t], 1)]
    )
    mirror = jnp.stack(
        [jnp.concatenate([cos_t, -cos_t], 1), jnp.concatenate([-sin_t, -sin_t], 1)]
    )
    table = jnp.concatenate([plain, mirror], axis=1)
    return jnp.broadcast_to(table.reshape(2, -1, 1), (2, table[0].size, LANES))


def polarizability(psi_val, psi_cond, e_val, e_cond, occ, freq, gmap):
    num_val, planes, size_y, size_z = psi_val.shape
    num_cond = psi_cond.shape[0]
    num_g = gmap.shape[0]
    pairs = num_val * num_cond
    size_x = planes * lax.axis_size("blk")
    norm = 1.0 / math.sqrt(size_x * size_y * size_z)

    val = jnp.transpose(psi_val, (1, 2, 3, 0))
    cond = jnp.transpose(
        psi_cond.reshape(num_cond, planes, size_y // SUB, SUB, size_z), (0, 1, 2, 4, 3)
    )
    if planes < SLOTS:
        val = jnp.pad(val, ((0, SLOTS - planes), (0, 0), (0, 0), (0, 0)))
        cond = jnp.pad(cond, ((0, 0), (0, SLOTS - planes), (0, 0), (0, 0), (0, 0)))

    kz = gmap % size_z
    ky = gmap // size_z % size_y
    kx = gmap // (size_z * size_y)
    mirrored = kz > size_z // 2
    col = jnp.where(mirrored, size_z - kz, kz) * size_y + jnp.where(
        mirrored, (size_y - ky) % size_y, ky
    )
    pick = jnp.stack([col, kx + jnp.where(mirrored, size_x, 0)]) * SUB
    cs = phase_table(size_x, lax.axis_index("blk") * planes, planes, norm)

    count = lax.axis_size("blk")
    links = Links(count) if Links.fits(count) else None
    if links is not None:
        tables = np.concatenate([x.reshape(count, -1) for x in (links.near, links.order)], axis=1)
        table = jnp.asarray(tables)[lax.axis_index("blk")]
        pick = pick.reshape(2, count, -1)[:, table[:count]].reshape(2, -1)
        ids = table[count:]
    owned = []
    for c in range(num_cond):
        keep, other = transform(pick[0], pick[1], val, cond[c], cs, num_g)
        if links is None:
            whole = jnp.concatenate([keep, other])
            owned.append((lax.psum_scatter(whole, "blk", scatter_dimension=0, tiled=True),))
        else:
            before = owned[-1][1:] if c == num_cond - 1 else ()
            owned.append(reduce_scatter(keep, other, links, before))
    for c, parts in enumerate(owned):
        owned[c] = sum(parts[1:], parts[0])
    own = jnp.stack(owned).reshape(num_cond, -1, 2, 4, num_val)
    own = jnp.transpose(own, (1, 3, 2, 0, 4)).reshape(-1, 2 * pairs)

    gaps = e_val[None, :] - e_cond[:, None]
    gaps = gaps.reshape(1, pairs)
    occ_row = jnp.broadcast_to(occ.astype(f32)[None, :], (num_cond, num_val)).reshape(1, pairs)
    weights = occ_row * gaps / (gaps * gaps + (freq * freq)[:, None]) / math.sqrt(pairs)

    if links is not None:
        return gather_and_chi(weights, own, links, ids, num_g)
    return chi(weights, own, lax.all_gather(own, "blk", axis=0, tiled=True))


def solution(mesh):
    step = jax.shard_map(
        polarizability,
        mesh=mesh,
        in_specs=(
            P("cell", "blk", None, None),
            P("cell", "blk", None, None),
            P("cell"),
            P("cell"),
            P("cell"),
            P("cell"),
            P("cell"),
        ),
        out_specs=(P("cell", "blk", None), P("cell", "blk", None)),
        check_vma=False,
    )
    if not Links.fits(mesh.shape["blk"]):
        return step
    return step
```

```python
import functools
import math

import jax
import jax.numpy as jnp
import ml_dtypes
import numpy as np
from jax import lax
from jax.experimental import pallas as pl
from jax.experimental.pallas import tpu as pltpu
from jax.sharding import PartitionSpec as P


VMEM_BYTES = 64 * 2**20
LANES = 128
SUB = 8
SLOTS = 4
f32 = jnp.float32
bf16 = jnp.bfloat16


def split_np(table):
    high = table.astype(ml_dtypes.bfloat16)
    low = (table - high.astype(np.float64)).astype(ml_dtypes.bfloat16)
    return np.concatenate([high, high, low], axis=1)


def split3(block):
    high = block.astype(bf16)
    low = (block - high.astype(f32)).astype(bf16)
    return jnp.concatenate([high, low, high], axis=0)


def z_table(size_z):
    half = size_z // 2
    z = np.arange(size_z)
    cos_rows = np.cos(2 * np.pi * ((np.arange(half + 1)[:, None] * z) % size_z) / size_z)
    sin_rows = -np.sin(2 * np.pi * ((np.arange(1, half)[:, None] * z) % size_z) / size_z)
    return np.concatenate([cos_rows, sin_rows], axis=0)


def y_tables(size_y):
    k = np.arange(size_y)
    ang = 2 * np.pi * ((k[:, None] * k[None, :]) % size_y) / size_y
    cos_t, sin_t = np.cos(ang), np.sin(ang)
    real_rows = np.concatenate([cos_t, sin_t], axis=1)
    imag_rows = np.concatenate([-sin_t, cos_t], axis=1)
    full = np.stack([real_rows, imag_rows], axis=0).reshape(2, size_y // 4, 4, 2 * size_y)
    full = full.transpose(1, 0, 2, 3).reshape(2 * size_y, 2 * size_y)
    return full, full[:, :size_y]


def roll_sub(x, shift):
    return pltpu.roll(x, shift % SUB, axis=x.ndim - 2)


def in_steps(count, at_once, step):
    def several(i, carry):
        for u in range(at_once):
            step(i * at_once + u)
        return carry

    lax.fori_loop(0, count // at_once, several, 0)
    for i in range(count // at_once * at_once, count):
        step(i)


def transform_kernel(
    col_ref,
    phase_ref,
    val_hbm,
    cond_ref,
    dz_ref,
    dy_ref,
    dyr_ref,
    cs_hbm,
    keep_hbm,
    send_hbm,
    val_scr,
    cs_scr,
    z_scr,
    tab_scr,
    out_scr,
    in_sems,
    out_sems,
):
    slots, size_y, size_z, lanes = val_hbm.shape
    half = size_z // 2
    groups_y = size_y // SUB
    pitch = size_z + SUB

    def plane(x):
        return pltpu.make_async_copy(val_hbm.at[x], val_scr.at[x], in_sems.at[x])

    phases = pltpu.make_async_copy(cs_hbm, cs_scr, in_sems.at[slots])
    for x in range(slots):
        plane(x).start()
    phases.start()

    def z_stage(x, yg):
        cond = cond_ref[x, yg]
        parts = []
        for j in range(SUB):
            block = val_scr[x, yg * SUB + j]
            parts.append(block * jnp.broadcast_to(cond[:, j : j + 1], (size_z, lanes)))
        rhs = split3(jnp.concatenate(parts, axis=1))
        got = jnp.dot(dz_ref[...], rhs, preferred_element_type=f32)
        for j in range(SUB):
            at = pl.multiple_of((yg * SUB + j) * pitch, SUB)
            z_scr[x, pl.ds(at, size_z), :] = got[:, j * lanes : (j + 1) * lanes]

    def z_plane(x, carry):
        plane(x).wait()
        in_steps(groups_y, 4, functools.partial(z_stage, x))
        return carry

    lax.fori_loop(0, slots, z_plane, 0)

    shape = (size_y // 4, SUB, lanes)
    sub = lax.broadcasted_iota(jnp.int32, shape, 1)
    low2 = (sub % 4) < 2
    low1 = (sub % 2) == 0

    def put(kz, got):
        a = [got[:, x * lanes : (x + 1) * lanes].reshape(shape) for x in range(slots)]
        p0 = jnp.where(low2, a[0], roll_sub(a[2], 2))
        p2 = jnp.where(low2, roll_sub(a[0], -2), a[2])
        p1 = jnp.where(low2, a[1], roll_sub(a[3], 2))
        p3 = jnp.where(low2, roll_sub(a[1], -2), a[3])
        tab_scr[kz, :, 0] = jnp.where(low1, p0, roll_sub(p1, 1))
        tab_scr[kz, :, 1] = jnp.where(low1, roll_sub(p0, -1), p1)
        tab_scr[kz, :, 2] = jnp.where(low1, p2, roll_sub(p3, 1))
        tab_scr[kz, :, 3] = jnp.where(low1, roll_sub(p2, -1), p3)

    def rows(k):
        return jnp.concatenate(
            [z_scr[x, pl.ds(k, size_y, stride=pitch), :] for x in range(slots)], axis=1
        )

    for kz in (0, half):
        put(kz, jnp.dot(dyr_ref[...], split3(rows(kz)), preferred_element_type=f32))

    def y_stage(step):
        kz = step + 1
        block = jnp.concatenate([rows(kz), rows(half + kz)], axis=0)
        put(kz, jnp.dot(dy_ref[...], split3(block), preferred_element_type=f32))

    in_steps(half - 1, 3, y_stage)

    sub1 = lax.broadcasted_iota(jnp.int32, (SUB, lanes), 0)
    m2 = (sub1 % 4) < 2
    m1 = (sub1 % 2) == 0
    kzs, kyq, _, _, _ = tab_scr.shape
    tab = tab_scr.reshape(kzs * kyq * 4 * SUB, lanes)
    quads = keep_hbm.shape[0]
    phases.wait()

    def quad(q):
        t = []
        for i in range(4):
            d = tab[pl.ds(pl.multiple_of(col_ref[q * 4 + i], SUB), SUB), :]
            at = pl.ds(pl.multiple_of(phase_ref[q * 4 + i], SUB), SUB)
            t.append(d * cs_scr[0, at, :] + roll_sub(d, 4) * cs_scr[1, at, :])
        v0 = jnp.where(m2, t[0], roll_sub(t[2], 2)) + jnp.where(m2, roll_sub(t[0], -2), t[2])
        v1 = jnp.where(m2, t[1], roll_sub(t[3], 2)) + jnp.where(m2, roll_sub(t[1], -2), t[3])
        out_scr[q] = jnp.where(m1, v0, roll_sub(v1, 1)) + jnp.where(m1, roll_sub(v0, -1), v1)

    at_once = math.gcd(quads // 2, SUB)
    copies = []
    for n, (out_hbm, first, at, size) in enumerate(
        (
            (send_hbm, quads, 0, quads),
            (keep_hbm, 0, 0, quads // 2),
            (keep_hbm, 0, quads // 2, quads // 2),
        )
    ):
        in_steps(size, at_once, lambda q, start=first + at: quad(start + q))
        copies.append(
            pltpu.make_async_copy(
                out_scr.at[pl.ds(first + at, size)], out_hbm.at[pl.ds(at, size)], out_sems.at[n]
            )
        )
        copies[-1].start()
    for copy in copies:
        copy.wait()


def transform(col, phase, val, cond, cs, num_g):
    slots, size_y, size_z, lanes = val.shape
    dz = jnp.asarray(split_np(z_table(size_z)))
    full, real_only = y_tables(size_y)
    dy, dyr = jnp.asarray(split_np(full)), jnp.asarray(split_np(real_only))
    vmem = pl.BlockSpec(memory_space=pltpu.VMEM)
    smem = pl.BlockSpec(memory_space=pltpu.SMEM)
    hbm = pl.BlockSpec(memory_space=pl.ANY)
    return pl.pallas_call(
        transform_kernel,
        out_shape=(jax.ShapeDtypeStruct((num_g // 8, SUB, lanes), f32),) * 2,
        in_specs=[smem, smem, hbm, vmem, vmem, vmem, vmem, hbm],
        out_specs=(hbm, hbm),
        scratch_shapes=[
            pltpu.VMEM(val.shape, f32),
            pltpu.VMEM(cs.shape, f32),
            pltpu.VMEM((slots, (size_z + SUB) * size_y, lanes), f32),
            pltpu.VMEM((size_z // 2 + 1, size_y // 4, 4, SUB, lanes), f32),
            pltpu.VMEM((num_g // 4, SUB, lanes), f32),
            pltpu.SemaphoreType.DMA((slots + 1,)),
            pltpu.SemaphoreType.DMA((3,)),
        ],
        compiler_params=pltpu.CompilerParams(vmem_limit_bytes=VMEM_BYTES),
        name="transform",
    )(col, phase, val, cond, dz, dy, dyr, cs)


def split_lanes(block):
    high = block.astype(bf16)
    low = (block - high.astype(f32)).astype(bf16)
    return high, low


def fill_left(w_ref, own_ref, left_scr):
    freqs = w_ref.shape[0]
    rows, pairs2 = own_ref.shape

    def fill(w, carry):
        row = w_ref[pl.ds(w, 1), :]
        high, low = split_lanes(own_ref[...] * jnp.concatenate([row, row], axis=1))
        at = pl.ds(pl.multiple_of(w * rows, rows), rows)
        left_scr[at, :pairs2] = high
        left_scr[at, pairs2 : 2 * pairs2] = high
        left_scr[at, 2 * pairs2 :] = low
        return carry

    lax.fori_loop(0, freqs, fill, 0)


def chi_tile(block, left_scr, real_ref, imag_ref):
    freqs, rows, _ = real_ref.shape
    pairs = block.shape[1] // 2
    turned = jnp.concatenate([-block[:, pairs:], block[:, :pairs]], axis=1)
    for value, out_ref in ((block, real_ref), (turned, imag_ref)):
        high, low = split_lanes(value)
        right = jnp.concatenate([high, low, high], axis=1)
        got = lax.dot_general(
            left_scr[...], right, (((1,), (1,)), ((), ())), preferred_element_type=f32
        )
        out_ref[...] = got.reshape(freqs, rows, -1)


def chi_kernel(w_ref, own_ref, all_ref, real_ref, imag_ref, left_scr):
    @pl.when(pl.program_id(0) == 0)
    def _():
        fill_left(w_ref, own_ref, left_scr)

    chi_tile(all_ref[...], left_scr, real_ref, imag_ref)


def chi(weights, own, everyone):
    freqs, pairs = weights.shape
    rows = own.shape[0]
    num_g = everyone.shape[0]
    tile = min(num_g, 4 * LANES)
    out = jax.ShapeDtypeStruct((freqs, rows, num_g), f32)
    out_spec = pl.BlockSpec((freqs, rows, tile), lambda t: (0, 0, t))
    return pl.pallas_call(
        chi_kernel,
        grid=(num_g // tile,),
        out_shape=(out, out),
        in_specs=[
            pl.BlockSpec((freqs, pairs), lambda t: (0, 0)),
            pl.BlockSpec((rows, 2 * pairs), lambda t: (0, 0)),
            pl.BlockSpec((tile, 2 * pairs), lambda t: (t, 0)),
        ],
        out_specs=(out_spec, out_spec),
        scratch_shapes=[pltpu.VMEM((freqs * rows, 6 * pairs), bf16)],
        name="chi",
    )(weights, own, everyone)


def chi_group_kernel(counts, with_old, *refs):
    total = sum(counts)
    n = len(counts)
    _, w_ref, own_ref = refs[:3]
    pieces = refs[3 : 3 + total]
    rest = refs[3 + total + (2 if with_old else 0) :]
    real_ref, imag_ref, left_scr, got_scr, sems = rest
    step = pl.program_id(0)

    def copies(i):
        at, first = 0, sum(counts[:i])
        for j in range(counts[i]):
            ref = pieces[first + j]
            yield pltpu.make_async_copy(
                ref, got_scr.at[i, pl.ds(at, ref.shape[0])], sems.at[first + j]
            )
            at += ref.shape[0]

    @pl.when(step == 0)
    def _():
        for i in range(n):
            for copy in copies(i):
                copy.start()
        fill_left(w_ref, own_ref, left_scr)

    for i in range(n):

        @pl.when(step == i)
        def _(i=i):
            for copy in copies(i):
                copy.wait()

    chi_tile(got_scr[step], left_scr, real_ref, imag_ref)


def chi_group(weights, own, blocks, ids, first, num_g, old):
    freqs, pairs = weights.shape
    rows = own.shape[0]
    counts = tuple(len(b) for b in blocks)
    pieces = [p for b in blocks for p in b]
    out = jax.ShapeDtypeStruct((freqs, rows, num_g), f32)
    out_spec = pl.BlockSpec((freqs, rows, rows), lambda t, ids: (0, 0, ids[first + t]))
    hbm = pl.BlockSpec(memory_space=pl.ANY)
    olds = () if old is None else old
    return pl.pallas_call(
        functools.partial(chi_group_kernel, counts, old is not None),
        grid_spec=pltpu.PrefetchScalarGridSpec(
            num_scalar_prefetch=1,
            grid=(len(blocks),),
            in_specs=[
                pl.BlockSpec((freqs, pairs), lambda t, ids: (0, 0)),
                pl.BlockSpec((rows, 2 * pairs), lambda t, ids: (0, 0)),
            ]
            + [hbm] * (len(pieces) + len(olds)),
            out_specs=(out_spec, out_spec),
            scratch_shapes=[
                pltpu.VMEM((freqs * rows, 6 * pairs), bf16),
                pltpu.VMEM((len(blocks), rows, 2 * pairs), f32),
                pltpu.SemaphoreType.DMA((len(pieces),)),
            ],
        ),
        out_shape=(out, out),
        input_output_aliases={3 + len(pieces) + i: i for i in range(len(olds))},
        compiler_params=pltpu.CompilerParams(vmem_limit_bytes=VMEM_BYTES),
        name="chi",
    )(ids, weights, own, *pieces, *olds)


GROUPS = (((0, 0),), ((1, 0), (0, 3)), ((0, 1), (1, 3)), ((0, 2), (1, 1)), ((1, 2),))
RING = (0, 2, 3, 1)


class Links:
    def __init__(self, count):
        def place(i):
            return i // 4, i // 2 % 2, i % 2

        def at(z, y, core):
            return z * 4 + y * 2 + core

        def turn(i, by):
            z, y, core = place(i)
            return at(RING[(RING.index(z) + by) % 4], y, core)

        every = range(count)
        self.core = [(i, i ^ 1) for i in every]
        self.y = [(i, i ^ 2) for i in every]
        self.cw = [(i, turn(i, 1)) for i in every]
        self.ccw = [(i, turn(i, -1)) for i in every]
        self.near = np.array(
            [
                [[[turn(i ^ (2 * b) ^ a, r) for r in range(4)] for b in range(2)] for a in range(2)]
                for i in every
            ],
            dtype=np.int32,
        )
        self.order = np.stack([self.near[:, :, b, r] for g in GROUPS for b, r in g], axis=1)

    @staticmethod
    def fits(count):
        return count == len(RING) * 4


def send(value, pairs):
    return lax.ppermute(value, "blk", pairs)


def reduce_scatter(keep, other, links, before):
    half = keep.shape[0] // 2
    got = send(other, links.core)
    far = send(keep[half:] + got[half:], links.y)
    if before:
        far, *_ = lax.optimization_barrier((far, *before))
    near = keep[:half] + got[:half] + far
    block = half // 4
    to_cw, to_ccw, next_cw, mine = lax.optimization_barrier(
        tuple(near[i * block : (i + 1) * block] for i in (2, 3, 1, 0))
    )
    two_back = send(to_cw, links.cw)
    ahead = send(to_ccw, links.ccw)
    next_cw = next_cw + two_back
    back = send(next_cw, links.cw)
    return mine, ahead, back


def gather_and_chi(weights, own, links, ids, num_g):
    cw = send(own, links.cw)
    later, cw = lax.optimization_barrier((own, cw))
    ccw = send(later, links.ccw)
    cw_later, ccw = lax.optimization_barrier((cw, ccw))
    mine = {(0, 0): own, (0, 3): cw, (0, 1): ccw, (0, 2): send(cw_later, links.cw)}
    for r in range(4):
        mine[1, r] = send(mine[0, r], links.y)
    old = None
    first = 0
    for group in GROUPS:
        blocks = []
        for b, r in group:
            blocks += [[mine[b, r]], [send(mine[b, r], links.core)]]
        old = chi_group(weights, own, blocks, ids, first, num_g, old)
        first += len(blocks)
    return old


def phase_table(size_x, first, planes, norm):
    x = first + jnp.arange(SLOTS, dtype=jnp.int32)
    k = jnp.arange(size_x, dtype=jnp.int32)
    ang = (k[:, None] * x[None, :] % size_x).astype(f32) * (2.0 * math.pi / size_x)
    live = (jnp.arange(SLOTS) < planes).astype(f32) * norm
    cos_t, sin_t = jnp.cos(ang) * live, jnp.sin(ang) * live
    plain = jnp.stack(
        [jnp.concatenate([cos_t, cos_t], 1), jnp.concatenate([sin_t, -sin_t], 1)]
    )
    mirror = jnp.stack(
        [jnp.concatenate([cos_t, -cos_t], 1), jnp.concatenate([-sin_t, -sin_t], 1)]
    )
    table = jnp.concatenate([plain, mirror], axis=1)
    return jnp.broadcast_to(table.reshape(2, -1, 1), (2, table[0].size, LANES))


def polarizability(psi_val, psi_cond, e_val, e_cond, occ, freq, gmap):
    num_val, planes, size_y, size_z = psi_val.shape
    num_cond = psi_cond.shape[0]
    num_g = gmap.shape[0]
    pairs = num_val * num_cond
    size_x = planes * lax.axis_size("blk")
    norm = 1.0 / math.sqrt(size_x * size_y * size_z)

    val = jnp.transpose(psi_val, (1, 2, 3, 0))
    cond = jnp.transpose(
        psi_cond.reshape(num_cond, planes, size_y // SUB, SUB, size_z), (0, 1, 2, 4, 3)
    )
    if planes < SLOTS:
        val = jnp.pad(val, ((0, SLOTS - planes), (0, 0), (0, 0), (0, 0)))
        cond = jnp.pad(cond, ((0, 0), (0, SLOTS - planes), (0, 0), (0, 0), (0, 0)))

    kz = gmap % size_z
    ky = gmap // size_z % size_y
    kx = gmap // (size_z * size_y)
    mirrored = kz > size_z // 2
    col = jnp.where(mirrored, size_z - kz, kz) * size_y + jnp.where(
        mirrored, (size_y - ky) % size_y, ky
    )
    pick = jnp.stack([col, kx + jnp.where(mirrored, size_x, 0)]) * SUB
    cs = phase_table(size_x, lax.axis_index("blk") * planes, planes, norm)

    count = lax.axis_size("blk")
    links = Links(count) if Links.fits(count) else None
    if links is not None:
        tables = np.concatenate([x.reshape(count, -1) for x in (links.near, links.order)], axis=1)
        table = jnp.asarray(tables)[lax.axis_index("blk")]
        pick = pick.reshape(2, count, -1)[:, table[:count]].reshape(2, -1)
        ids = table[count:]
    owned = []
    for c in range(num_cond):
        keep, other = transform(pick[0], pick[1], val, cond[c], cs, num_g)
        if links is None:
            whole = jnp.concatenate([keep, other])
            owned.append((lax.psum_scatter(whole, "blk", scatter_dimension=0, tiled=True),))
        else:
            before = owned[-1][1:] if c == num_cond - 1 else ()
            owned.append(reduce_scatter(keep, other, links, before))
    for c, parts in enumerate(owned):
        owned[c] = sum(parts[1:], parts[0])
    own = jnp.stack(owned).reshape(num_cond, -1, 2, 4, num_val)
    own = jnp.transpose(own, (1, 3, 2, 0, 4)).reshape(-1, 2 * pairs)

    gaps = e_val[None, :] - e_cond[:, None]
    gaps = gaps.reshape(1, pairs)
    occ_row = jnp.broadcast_to(occ.astype(f32)[None, :], (num_cond, num_val)).reshape(1, pairs)
    weights = occ_row * gaps / (gaps * gaps + (freq * freq)[:, None]) / math.sqrt(pairs)

    if links is not None:
        return gather_and_chi(weights, own, links, ids, num_g)
    return chi(weights, own, lax.all_gather(own, "blk", axis=0, tiled=True))


def solution(mesh):
    step = jax.shard_map(
        polarizability,
        mesh=mesh,
        in_specs=(
            P("cell", "blk", None, None),
            P("cell", "blk", None, None),
            P("cell"),
            P("cell"),
            P("cell"),
            P("cell"),
            P("cell"),
        ),
        out_specs=(P("cell", "blk", None), P("cell", "blk", None)),
        check_vma=False,
    )
    if not Links.fits(mesh.shape["blk"]):
        return step
    return step
```

```python
import functools
import math

import jax
import jax.numpy as jnp
import ml_dtypes
import numpy as np
from jax import lax
from jax.experimental import pallas as pl
from jax.experimental.pallas import tpu as pltpu
from jax.sharding import PartitionSpec as P


VMEM_BYTES = 64 * 2**20
LANES = 128
SUB = 8
PARTS = 4
SLOTS = 4
f32 = jnp.float32
bf16 = jnp.bfloat16


def split_np(table):
    high = table.astype(ml_dtypes.bfloat16)
    low = (table - high.astype(np.float64)).astype(ml_dtypes.bfloat16)
    return np.concatenate([high, high, low], axis=1)


def split3(block):
    high = block.astype(bf16)
    low = (block - high.astype(f32)).astype(bf16)
    return jnp.concatenate([high, low, high], axis=0)


def z_table(size_z):
    half = size_z // 2
    z = np.arange(size_z)
    cos_rows = np.cos(2 * np.pi * ((np.arange(half + 1)[:, None] * z) % size_z) / size_z)
    sin_rows = -np.sin(2 * np.pi * ((np.arange(1, half)[:, None] * z) % size_z) / size_z)
    return np.concatenate([cos_rows, sin_rows], axis=0)


def y_tables(size_y):
    k = np.arange(size_y)
    ang = 2 * np.pi * ((k[:, None] * k[None, :]) % size_y) / size_y
    cos_t, sin_t = np.cos(ang), np.sin(ang)
    real_rows = np.concatenate([cos_t, sin_t], axis=1)
    imag_rows = np.concatenate([-sin_t, cos_t], axis=1)
    full = np.stack([real_rows, imag_rows], axis=0).reshape(2, size_y // 4, 4, 2 * size_y)
    full = full.transpose(1, 0, 2, 3).reshape(2 * size_y, 2 * size_y)
    return full, full[:, :size_y]


def roll_sub(x, shift):
    return pltpu.roll(x, shift % SUB, axis=x.ndim - 2)


def in_steps(count, at_once, step):
    def several(i, carry):
        for u in range(at_once):
            step(i * at_once + u)
        return carry

    lax.fori_loop(0, count // at_once, several, 0)
    for i in range(count // at_once * at_once, count):
        step(i)


def transform_kernel(
    col_ref,
    phase_ref,
    val_hbm,
    cond_ref,
    dz_ref,
    dy_ref,
    dyr_ref,
    cs_hbm,
    *refs,
):
    outs, scratch = refs[:PARTS], refs[PARTS:]
    transform_parts(
        col_ref, phase_ref, val_hbm, cond_ref, dz_ref, dy_ref, dyr_ref, cs_hbm, outs, *scratch
    )


def transform_parts(
    col_ref,
    phase_ref,
    val_hbm,
    cond_ref,
    dz_ref,
    dy_ref,
    dyr_ref,
    cs_hbm,
    outs,
    val_scr,
    cs_scr,
    z_scr,
    tab_scr,
    out_scr,
    in_sems,
    out_sems,
):
    slots, size_y, size_z, lanes = val_hbm.shape
    half = size_z // 2
    groups_y = size_y // SUB
    pitch = size_z + SUB

    def plane(x):
        return pltpu.make_async_copy(val_hbm.at[x], val_scr.at[x], in_sems.at[x])

    phases = pltpu.make_async_copy(cs_hbm, cs_scr, in_sems.at[slots])
    for x in range(slots):
        plane(x).start()
    phases.start()

    def z_stage(x, yg):
        cond = cond_ref[x, yg]
        parts = []
        for j in range(SUB):
            block = val_scr[x, yg * SUB + j]
            parts.append(block * jnp.broadcast_to(cond[:, j : j + 1], (size_z, lanes)))
        rhs = split3(jnp.concatenate(parts, axis=1))
        got = jnp.dot(dz_ref[...], rhs, preferred_element_type=f32)
        for j in range(SUB):
            at = pl.multiple_of((yg * SUB + j) * pitch, SUB)
            z_scr[x, pl.ds(at, size_z), :] = got[:, j * lanes : (j + 1) * lanes]

    def z_plane(x, carry):
        plane(x).wait()
        in_steps(groups_y, 4, functools.partial(z_stage, x))
        return carry

    lax.fori_loop(0, slots, z_plane, 0)

    shape = (size_y // 4, SUB, lanes)
    sub = lax.broadcasted_iota(jnp.int32, shape, 1)
    low2 = (sub % 4) < 2
    low1 = (sub % 2) == 0

    def put(kz, got):
        a = [got[:, x * lanes : (x + 1) * lanes].reshape(shape) for x in range(slots)]
        p0 = jnp.where(low2, a[0], roll_sub(a[2], 2))
        p2 = jnp.where(low2, roll_sub(a[0], -2), a[2])
        p1 = jnp.where(low2, a[1], roll_sub(a[3], 2))
        p3 = jnp.where(low2, roll_sub(a[1], -2), a[3])
        tab_scr[kz, :, 0] = jnp.where(low1, p0, roll_sub(p1, 1))
        tab_scr[kz, :, 1] = jnp.where(low1, roll_sub(p0, -1), p1)
        tab_scr[kz, :, 2] = jnp.where(low1, p2, roll_sub(p3, 1))
        tab_scr[kz, :, 3] = jnp.where(low1, roll_sub(p2, -1), p3)

    def rows(k):
        return jnp.concatenate(
            [z_scr[x, pl.ds(k, size_y, stride=pitch), :] for x in range(slots)], axis=1
        )

    for kz in (0, half):
        put(kz, jnp.dot(dyr_ref[...], split3(rows(kz)), preferred_element_type=f32))

    def y_stage(step):
        kz = step + 1
        block = jnp.concatenate([rows(kz), rows(half + kz)], axis=0)
        put(kz, jnp.dot(dy_ref[...], split3(block), preferred_element_type=f32))

    in_steps(half - 1, 3, y_stage)

    sub1 = lax.broadcasted_iota(jnp.int32, (SUB, lanes), 0)
    m2 = (sub1 % 4) < 2
    m1 = (sub1 % 2) == 0
    kzs, kyq, _, _, _ = tab_scr.shape
    tab = tab_scr.reshape(kzs * kyq * 4 * SUB, lanes)
    quads = outs[0].shape[0]
    low4 = sub1 < 4
    phases.wait()

    def quad(q):
        t = []
        for i in range(4):
            d = tab[pl.ds(pl.multiple_of(col_ref[q * 4 + i], SUB), SUB), :]
            at = pl.ds(pl.multiple_of(phase_ref[q * 4 + i], SUB), SUB)
            p = cs_scr[at, :]
            turned = roll_sub(p, 4)
            t.append(d * jnp.where(low4, p, turned) + roll_sub(d, 4) * jnp.where(low4, turned, -p))
        v0 = jnp.where(m2, t[0], roll_sub(t[2], 2)) + jnp.where(m2, roll_sub(t[0], -2), t[2])
        v1 = jnp.where(m2, t[1], roll_sub(t[3], 2)) + jnp.where(m2, roll_sub(t[1], -2), t[3])
        out_scr[q] = jnp.where(m1, v0, roll_sub(v1, 1)) + jnp.where(m1, roll_sub(v0, -1), v1)

    copies = []
    for n in reversed(range(PARTS)):
        first = n * quads
        in_steps(quads, math.gcd(quads, SUB), lambda q, first=first: quad(first + q))
        copies.append(
            pltpu.make_async_copy(out_scr.at[pl.ds(first, quads)], outs[n], out_sems.at[n])
        )
        copies[-1].start()
    for copy in copies:
        copy.wait()


def transform(col, phase, val, cond, c, cs, num_g):
    slots, size_y, size_z, lanes = val.shape
    dz = jnp.asarray(split_np(z_table(size_z)))
    full, real_only = y_tables(size_y)
    dy, dyr = jnp.asarray(split_np(full)), jnp.asarray(split_np(real_only))
    vmem = pl.BlockSpec(memory_space=pltpu.VMEM)
    smem = pl.BlockSpec(memory_space=pltpu.SMEM)
    hbm = pl.BlockSpec(memory_space=pl.ANY)
    return pl.pallas_call(
        transform_kernel,
        grid=(1,),
        out_shape=(jax.ShapeDtypeStruct((num_g // 4 // PARTS, SUB, lanes), f32),) * PARTS,
        in_specs=[
            smem,
            smem,
            hbm,
            pl.BlockSpec((None,) + cond.shape[1:], lambda i: (c, 0, 0, 0, 0)),
            vmem,
            vmem,
            vmem,
            hbm,
        ],
        out_specs=(hbm,) * PARTS,
        scratch_shapes=[
            pltpu.VMEM(val.shape, f32),
            pltpu.VMEM(cs.shape, f32),
            pltpu.VMEM((slots, (size_z + SUB) * size_y, lanes), f32),
            pltpu.VMEM((size_z // 2 + 1, size_y // 4, 4, SUB, lanes), f32),
            pltpu.VMEM((num_g // 4, SUB, lanes), f32),
            pltpu.SemaphoreType.DMA((slots + 1,)),
            pltpu.SemaphoreType.DMA((PARTS,)),
        ],
        compiler_params=pltpu.CompilerParams(vmem_limit_bytes=VMEM_BYTES),
        name="transform",
    )(col, phase, val, cond, dz, dy, dyr, cs)


def split_lanes(block):
    high = block.astype(bf16)
    low = (block - high.astype(f32)).astype(bf16)
    return high, low


def fill_left(w_ref, own_ref, left_scr):
    freqs = w_ref.shape[0]
    rows, pairs2 = own_ref.shape
    pairs = pairs2 // 2

    def fill(w, carry):
        row = w_ref[pl.ds(w, 1), :]
        a = own_ref[:, :pairs] * row
        b = own_ref[:, pairs:] * row
        at = pl.ds(pl.multiple_of(w * rows, rows), rows)
        for n, side in enumerate((a + b, a, b)):
            high, low = split_lanes(side)
            left_scr[at, (3 * n) * pairs : (3 * n + 1) * pairs] = high
            left_scr[at, (3 * n + 1) * pairs : (3 * n + 2) * pairs] = high
            left_scr[at, (3 * n + 2) * pairs : (3 * n + 3) * pairs] = low
        return carry

    lax.fori_loop(0, freqs, fill, 0)


def chi_tile(block, left_scr, real_ref, imag_ref):
    freqs, rows, _ = real_ref.shape
    pairs = block.shape[1] // 2
    c, d = block[:, :pairs], block[:, pairs:]
    got = []
    for n, side in enumerate((c, c + d, c - d)):
        high, low = split_lanes(side)
        right = jnp.concatenate([high, low, high], axis=1)
        got.append(
            lax.dot_general(
                left_scr[:, 3 * n * pairs : 3 * (n + 1) * pairs],
                right,
                (((1,), (1,)), ((), ())),
                preferred_element_type=f32,
            )
        )
    real_ref[...] = (got[0] - got[2]).reshape(freqs, rows, -1)
    imag_ref[...] = (got[0] - got[1]).reshape(freqs, rows, -1)


def chi_kernel(w_ref, own_ref, all_ref, real_ref, imag_ref, left_scr):
    @pl.when(pl.program_id(0) == 0)
    def _():
        fill_left(w_ref, own_ref, left_scr)

    chi_tile(all_ref[...], left_scr, real_ref, imag_ref)


def chi(weights, own, everyone):
    freqs, pairs = weights.shape
    rows = own.shape[0]
    num_g = everyone.shape[0]
    tile = min(num_g, 4 * LANES)
    out = jax.ShapeDtypeStruct((freqs, rows, num_g), f32)
    out_spec = pl.BlockSpec((freqs, rows, tile), lambda t: (0, 0, t))
    return pl.pallas_call(
        chi_kernel,
        grid=(num_g // tile,),
        out_shape=(out, out),
        in_specs=[
            pl.BlockSpec((freqs, pairs), lambda t: (0, 0)),
            pl.BlockSpec((rows, 2 * pairs), lambda t: (0, 0)),
            pl.BlockSpec((tile, 2 * pairs), lambda t: (t, 0)),
        ],
        out_specs=(out_spec, out_spec),
        scratch_shapes=[pltpu.VMEM((freqs * rows, 9 * pairs), bf16)],
        name="chi",
    )(weights, own, everyone)


def chi_group_kernel(counts, with_old, *refs):
    total = sum(counts)
    n = len(counts)
    _, w_ref, own_ref = refs[:3]
    pieces = refs[3 : 3 + total]
    rest = refs[3 + total + (2 if with_old else 0) :]
    real_ref, imag_ref, left_scr, got_scr, sems = rest
    step = pl.program_id(0)

    def copies(i):
        at, first = 0, sum(counts[:i])
        for j in range(counts[i]):
            ref = pieces[first + j]
            yield pltpu.make_async_copy(
                ref, got_scr.at[i, pl.ds(at, ref.shape[0])], sems.at[first + j]
            )
            at += ref.shape[0]

    @pl.when(step == 0)
    def _():
        for i in range(n):
            for copy in copies(i):
                copy.start()
        fill_left(w_ref, own_ref, left_scr)

    for i in range(n):

        @pl.when(step == i)
        def _(i=i):
            for copy in copies(i):
                copy.wait()

    chi_tile(got_scr[step], left_scr, real_ref, imag_ref)


def chi_group(weights, own, blocks, ids, first, num_g, old):
    freqs, pairs = weights.shape
    rows = own.shape[0]
    counts = tuple(len(b) for b in blocks)
    pieces = [p for b in blocks for p in b]
    out = jax.ShapeDtypeStruct((freqs, rows, num_g), f32)
    out_spec = pl.BlockSpec((freqs, rows, rows), lambda t, ids: (0, 0, ids[first + t]))
    hbm = pl.BlockSpec(memory_space=pl.ANY)
    olds = () if old is None else old
    return pl.pallas_call(
        functools.partial(chi_group_kernel, counts, old is not None),
        grid_spec=pltpu.PrefetchScalarGridSpec(
            num_scalar_prefetch=1,
            grid=(len(blocks),),
            in_specs=[
                pl.BlockSpec((freqs, pairs), lambda t, ids: (0, 0)),
                pl.BlockSpec((rows, 2 * pairs), lambda t, ids: (0, 0)),
            ]
            + [hbm] * (len(pieces) + len(olds)),
            out_specs=(out_spec, out_spec),
            scratch_shapes=[
                pltpu.VMEM((freqs * rows, 9 * pairs), bf16),
                pltpu.VMEM((len(blocks), rows, 2 * pairs), f32),
                pltpu.SemaphoreType.DMA((len(pieces),)),
            ],
        ),
        out_shape=(out, out),
        input_output_aliases={3 + len(pieces) + i: i for i in range(len(olds))},
        compiler_params=pltpu.CompilerParams(vmem_limit_bytes=VMEM_BYTES),
        name="chi",
    )(ids, weights, own, *pieces, *olds)


GROUPS = (((0, 0),), ((1, 0), (0, 3)), ((0, 1), (1, 3)), ((0, 2), (1, 1)), ((1, 2),))
RING = (0, 2, 3, 1)


class Links:
    def __init__(self, count):
        def place(i):
            return i // 4, i // 2 % 2, i % 2

        def at(z, y, core):
            return z * 4 + y * 2 + core

        def turn(i, by):
            z, y, core = place(i)
            return at(RING[(RING.index(z) + by) % 4], y, core)

        every = range(count)
        self.core = [(i, i ^ 1) for i in every]
        self.y = [(i, i ^ 2) for i in every]
        self.cw = [(i, turn(i, 1)) for i in every]
        self.ccw = [(i, turn(i, -1)) for i in every]
        self.near = np.array(
            [
                [[[turn(i ^ (2 * b) ^ a, r) for r in range(4)] for b in range(2)] for a in range(2)]
                for i in every
            ],
            dtype=np.int32,
        )
        self.order = np.stack([self.near[:, :, b, r] for g in GROUPS for b, r in g], axis=1)

    @staticmethod
    def fits(count):
        return count == len(RING) * 4


def send(value, pairs):
    return lax.ppermute(value, "blk", pairs)


def reduce_scatter(near, far, near_other, far_other, links, before):
    far = far + send(far_other, links.core)
    got = send(near_other, links.core)
    far = send(far, links.y)
    if before:
        far, *_ = lax.optimization_barrier((far, *before))
    near = near + got + far
    block = near.shape[0] // 4
    to_cw, to_ccw, next_cw, mine = lax.optimization_barrier(
        tuple(near[i * block : (i + 1) * block] for i in (2, 3, 1, 0))
    )
    two_back = send(to_cw, links.cw)
    ahead = send(to_ccw, links.ccw)
    next_cw = next_cw + two_back
    back = send(next_cw, links.cw)
    return mine, ahead, back


def gather_and_chi(weights, own, links, ids, num_g):
    cw = send(own, links.cw)
    later, cw = lax.optimization_barrier((own, cw))
    ccw = send(later, links.ccw)
    cw_later, ccw = lax.optimization_barrier((cw, ccw))
    mine = {(0, 0): own, (0, 3): cw, (0, 1): ccw, (0, 2): send(cw_later, links.cw)}
    for r in range(4):
        mine[1, r] = send(mine[0, r], links.y)
    old = None
    first = 0
    for group in GROUPS:
        blocks = []
        for b, r in group:
            blocks += [[mine[b, r]], [send(mine[b, r], links.core)]]
        old = chi_group(weights, own, blocks, ids, first, num_g, old)
        first += len(blocks)
    return old


def phase_table(size_x, first, planes, norm):
    x = first + jnp.arange(SLOTS, dtype=jnp.int32)
    k = jnp.arange(size_x, dtype=jnp.int32)
    ang = (k[:, None] * x[None, :] % size_x).astype(f32) * (2.0 * math.pi / size_x)
    live = (jnp.arange(SLOTS) < planes).astype(f32) * norm
    cos_t, sin_t = jnp.cos(ang) * live, jnp.sin(ang) * live
    table = jnp.stack(
        [jnp.concatenate([cos_t, sin_t], axis=1), jnp.concatenate([cos_t, -sin_t], axis=1)]
    )
    return jnp.broadcast_to(table.reshape(-1, 1), (table.size, LANES))


def polarizability(psi_val, psi_cond, e_val, e_cond, occ, freq, gmap):
    num_val, planes, size_y, size_z = psi_val.shape
    num_cond = psi_cond.shape[0]
    num_g = gmap.shape[0]
    pairs = num_val * num_cond
    size_x = planes * lax.axis_size("blk")
    norm = 1.0 / math.sqrt(size_x * size_y * size_z)

    val = jnp.transpose(psi_val, (1, 2, 3, 0))
    cond = jnp.transpose(
        psi_cond.reshape(num_cond, planes, size_y // SUB, SUB, size_z), (0, 1, 2, 4, 3)
    )
    if planes < SLOTS:
        val = jnp.pad(val, ((0, SLOTS - planes), (0, 0), (0, 0), (0, 0)))
        cond = jnp.pad(cond, ((0, 0), (0, SLOTS - planes), (0, 0), (0, 0), (0, 0)))

    kz = gmap % size_z
    ky = gmap // size_z % size_y
    kx = gmap // (size_z * size_y)
    mirrored = kz > size_z // 2
    col = jnp.where(mirrored, size_z - kz, kz) * size_y + jnp.where(
        mirrored, (size_y - ky) % size_y, ky
    )
    pick = jnp.stack([col, kx + jnp.where(mirrored, size_x, 0)]) * SUB
    cs = phase_table(size_x, lax.axis_index("blk") * planes, planes, norm)

    count = lax.axis_size("blk")
    links = Links(count) if Links.fits(count) else None
    if links is not None:
        tables = np.concatenate([x.reshape(count, -1) for x in (links.near, links.order)], axis=1)
        table = jnp.asarray(tables)[lax.axis_index("blk")]
        pick = pick.reshape(2, count, -1)[:, table[:count]].reshape(2, -1)
        ids = table[count:]
    owned = []
    for c in range(num_cond):
        made = transform(pick[0], pick[1], val, cond, c, cs, num_g)
        if links is None:
            whole = jnp.concatenate(made)
            owned.append((lax.psum_scatter(whole, "blk", scatter_dimension=0, tiled=True),))
        else:
            before = owned[-1][1:] if c == num_cond - 1 else ()
            owned.append(reduce_scatter(*made, links, before))
    for c, parts in enumerate(owned):
        owned[c] = sum(parts[1:], parts[0])
    own = jnp.stack(owned).reshape(num_cond, -1, 2, 4, num_val)
    rows = own.shape[1] * 4
    turned = lax.dynamic_slice_in_dim(mirrored, lax.axis_index("blk") * rows, rows)
    sign = jnp.where(turned, -1.0, 1.0).astype(f32)
    signs = jnp.stack([jnp.ones_like(sign), sign], axis=1).reshape(-1, 4, 2, 1, 1)
    own = (jnp.transpose(own, (1, 3, 2, 0, 4)) * signs).reshape(-1, 2 * pairs)

    gaps = e_val[None, :] - e_cond[:, None]
    gaps = gaps.reshape(1, pairs)
    occ_row = jnp.broadcast_to(occ.astype(f32)[None, :], (num_cond, num_val)).reshape(1, pairs)
    weights = occ_row * gaps / (gaps * gaps + (freq * freq)[:, None]) / math.sqrt(pairs)

    if links is not None:
        return gather_and_chi(weights, own, links, ids, num_g)
    return chi(weights, own, lax.all_gather(own, "blk", axis=0, tiled=True))


def solution(mesh):
    step = jax.shard_map(
        polarizability,
        mesh=mesh,
        in_specs=(
            P("cell", "blk", None, None),
            P("cell", "blk", None, None),
            P("cell"),
            P("cell"),
            P("cell"),
            P("cell"),
            P("cell"),
        ),
        out_specs=(P("cell", "blk", None), P("cell", "blk", None)),
        check_vma=False,
    )
    if not Links.fits(mesh.shape["blk"]):
        return step
    return step
```

```python
import functools
import math

import jax
import jax.numpy as jnp
import ml_dtypes
import numpy as np
from jax import lax
from jax.experimental import pallas as pl
from jax.experimental.pallas import tpu as pltpu
from jax.sharding import PartitionSpec as P


VMEM_BYTES = 64 * 2**20
LANES = 128
SUB = 8
PARTS = 4
SLOTS = 4
f32 = jnp.float32
bf16 = jnp.bfloat16


def split_np(table):
    high = table.astype(ml_dtypes.bfloat16)
    low = (table - high.astype(np.float64)).astype(ml_dtypes.bfloat16)
    return np.concatenate([high, high, low], axis=1)


def split3(block):
    high = block.astype(bf16)
    low = (block - high.astype(f32)).astype(bf16)
    return jnp.concatenate([high, low, high], axis=0)


def z_table(size_z):
    half = size_z // 2
    z = np.arange(size_z)
    cos_rows = np.cos(2 * np.pi * ((np.arange(half + 1)[:, None] * z) % size_z) / size_z)
    sin_rows = -np.sin(2 * np.pi * ((np.arange(1, half)[:, None] * z) % size_z) / size_z)
    return np.concatenate([cos_rows, sin_rows], axis=0)


def y_tables(size_y):
    k = np.arange(size_y)
    ang = 2 * np.pi * ((k[:, None] * k[None, :]) % size_y) / size_y
    cos_t, sin_t = np.cos(ang), np.sin(ang)
    real_rows = np.concatenate([cos_t, sin_t], axis=1)
    imag_rows = np.concatenate([-sin_t, cos_t], axis=1)
    full = np.stack([real_rows, imag_rows], axis=0).reshape(2, size_y // 4, 4, 2 * size_y)
    full = full.transpose(1, 0, 2, 3).reshape(2 * size_y, 2 * size_y)
    return full, full[:, :size_y]


def roll_sub(x, shift):
    return pltpu.roll(x, shift % SUB, axis=x.ndim - 2)


def in_steps(count, at_once, step):
    def several(i, carry):
        for u in range(at_once):
            step(i * at_once + u)
        return carry

    lax.fori_loop(0, count // at_once, several, 0)
    for i in range(count // at_once * at_once, count):
        step(i)


def transform_kernel(
    col_ref,
    phase_ref,
    val_hbm,
    cond_ref,
    dz_ref,
    dy_ref,
    dyr_ref,
    cs_hbm,
    *refs,
):
    outs, scratch = refs[:PARTS], refs[PARTS:]
    transform_parts(
        col_ref, phase_ref, val_hbm, cond_ref, dz_ref, dy_ref, dyr_ref, cs_hbm, outs, *scratch
    )


def transform_parts(
    col_ref,
    phase_ref,
    val_hbm,
    cond_ref,
    dz_ref,
    dy_ref,
    dyr_ref,
    cs_hbm,
    outs,
    val_scr,
    cs_scr,
    z_scr,
    tab_scr,
    out_scr,
    in_sems,
    out_sems,
):
    slots, size_y, size_z, lanes = val_hbm.shape
    half = size_z // 2
    groups_y = size_y // SUB
    pitch = size_z + SUB

    def plane(x):
        return pltpu.make_async_copy(val_hbm.at[x], val_scr.at[x], in_sems.at[x])

    phases = pltpu.make_async_copy(cs_hbm, cs_scr, in_sems.at[slots])
    for x in range(slots):
        plane(x).start()
    phases.start()

    def z_stage(x, yg):
        cond = cond_ref[x]
        parts = []
        for j in range(SUB):
            block = val_scr[x, yg * SUB + j]
            y = yg * SUB + j
            parts.append(block * jnp.broadcast_to(cond[:, y : y + 1], (size_z, lanes)))
        rhs = split3(jnp.concatenate(parts, axis=1))
        got = jnp.dot(dz_ref[...], rhs, preferred_element_type=f32)
        for j in range(SUB):
            at = pl.multiple_of((yg * SUB + j) * pitch, SUB)
            z_scr[x, pl.ds(at, size_z), :] = got[:, j * lanes : (j + 1) * lanes]

    def z_plane(x, carry):
        plane(x).wait()
        for yg in range(groups_y):
            z_stage(x, yg)
        return carry

    lax.fori_loop(0, slots, z_plane, 0)

    shape = (size_y // 4, SUB, lanes)
    sub = lax.broadcasted_iota(jnp.int32, shape, 1)
    low2 = (sub % 4) < 2
    low1 = (sub % 2) == 0

    def put(kz, got):
        a = [got[:, x * lanes : (x + 1) * lanes].reshape(shape) for x in range(slots)]
        p0 = jnp.where(low2, a[0], roll_sub(a[2], 2))
        p2 = jnp.where(low2, roll_sub(a[0], -2), a[2])
        p1 = jnp.where(low2, a[1], roll_sub(a[3], 2))
        p3 = jnp.where(low2, roll_sub(a[1], -2), a[3])
        tab_scr[kz, :, 0] = jnp.where(low1, p0, roll_sub(p1, 1))
        tab_scr[kz, :, 1] = jnp.where(low1, roll_sub(p0, -1), p1)
        tab_scr[kz, :, 2] = jnp.where(low1, p2, roll_sub(p3, 1))
        tab_scr[kz, :, 3] = jnp.where(low1, roll_sub(p2, -1), p3)

    def rows(k):
        return jnp.concatenate(
            [z_scr[x, pl.ds(k, size_y, stride=pitch), :] for x in range(slots)], axis=1
        )

    for kz in (0, half):
        put(kz, jnp.dot(dyr_ref[...], split3(rows(kz)), preferred_element_type=f32))

    def y_stage(step):
        kz = step + 1
        block = jnp.concatenate([rows(kz), rows(half + kz)], axis=0)
        put(kz, jnp.dot(dy_ref[...], split3(block), preferred_element_type=f32))

    in_steps(half - 1, 5, y_stage)

    sub1 = lax.broadcasted_iota(jnp.int32, (SUB, lanes), 0)
    m2 = (sub1 % 4) < 2
    m1 = (sub1 % 2) == 0
    kzs, kyq, _, _, _ = tab_scr.shape
    tab = tab_scr.reshape(kzs * kyq * 4 * SUB, lanes)
    quads = outs[0].shape[0]
    low4 = sub1 < 4
    phases.wait()

    def quad(q):
        t = []
        for i in range(4):
            d = tab[pl.ds(pl.multiple_of(col_ref[q * 4 + i], SUB), SUB), :]
            at = pl.ds(pl.multiple_of(phase_ref[q * 4 + i], SUB), SUB)
            p = cs_scr[at, :]
            turned = roll_sub(p, 4)
            t.append(d * jnp.where(low4, p, turned) + roll_sub(d, 4) * jnp.where(low4, turned, -p))
        v0 = jnp.where(m2, t[0], roll_sub(t[2], 2)) + jnp.where(m2, roll_sub(t[0], -2), t[2])
        v1 = jnp.where(m2, t[1], roll_sub(t[3], 2)) + jnp.where(m2, roll_sub(t[1], -2), t[3])
        out_scr[q] = jnp.where(m1, v0, roll_sub(v1, 1)) + jnp.where(m1, roll_sub(v0, -1), v1)

    copies = []
    for n in reversed(range(PARTS)):
        first = n * quads
        in_steps(quads, math.gcd(quads, 2 * SUB), lambda q, first=first: quad(first + q))
        copies.append(
            pltpu.make_async_copy(out_scr.at[pl.ds(first, quads)], outs[n], out_sems.at[n])
        )
        copies[-1].start()
    for copy in copies:
        copy.wait()


def transform(col, phase, val, cond, c, cs, num_g):
    slots, size_y, size_z, lanes = val.shape
    dz = jnp.asarray(split_np(z_table(size_z)))
    full, real_only = y_tables(size_y)
    dy, dyr = jnp.asarray(split_np(full)), jnp.asarray(split_np(real_only))
    vmem = pl.BlockSpec(memory_space=pltpu.VMEM)
    smem = pl.BlockSpec(memory_space=pltpu.SMEM)
    hbm = pl.BlockSpec(memory_space=pl.ANY)
    return pl.pallas_call(
        transform_kernel,
        grid=(1,),
        out_shape=(jax.ShapeDtypeStruct((num_g // 4 // PARTS, SUB, lanes), f32),) * PARTS,
        in_specs=[
            smem,
            smem,
            hbm,
            pl.BlockSpec((None,) + cond.shape[1:], lambda i: (c, 0, 0, 0)),
            vmem,
            vmem,
            vmem,
            hbm,
        ],
        out_specs=(hbm,) * PARTS,
        scratch_shapes=[
            pltpu.VMEM(val.shape, f32),
            pltpu.VMEM(cs.shape, f32),
            pltpu.VMEM((slots, (size_z + SUB) * size_y, lanes), f32),
            pltpu.VMEM((size_z // 2 + 1, size_y // 4, 4, SUB, lanes), f32),
            pltpu.VMEM((num_g // 4, SUB, lanes), f32),
            pltpu.SemaphoreType.DMA((slots + 1,)),
            pltpu.SemaphoreType.DMA((PARTS,)),
        ],
        compiler_params=pltpu.CompilerParams(vmem_limit_bytes=VMEM_BYTES),
        name="transform",
    )(col, phase, val, cond, dz, dy, dyr, cs)


def split_lanes(block):
    high = block.astype(bf16)
    low = (block - high.astype(f32)).astype(bf16)
    return high, low


def fill_left(w_ref, own_ref, left_scr):
    freqs = w_ref.shape[0]
    rows, pairs2 = own_ref.shape
    pairs = pairs2 // 2

    def fill(w, carry):
        row = w_ref[pl.ds(w, 1), :]
        a = own_ref[:, :pairs] * row
        b = own_ref[:, pairs:] * row
        at = pl.ds(pl.multiple_of(w * rows, rows), rows)
        for n, side in enumerate((a + b, a, b)):
            high, low = split_lanes(side)
            left_scr[at, (3 * n) * pairs : (3 * n + 1) * pairs] = high
            left_scr[at, (3 * n + 1) * pairs : (3 * n + 2) * pairs] = high
            left_scr[at, (3 * n + 2) * pairs : (3 * n + 3) * pairs] = low
        return carry

    lax.fori_loop(0, freqs, fill, 0)


def chi_tile(block, left_scr, real_ref, imag_ref):
    freqs, rows, _ = real_ref.shape
    pairs = block.shape[1] // 2
    c, d = block[:, :pairs], block[:, pairs:]
    got = []
    for n, side in enumerate((c, c + d, c - d)):
        high, low = split_lanes(side)
        right = jnp.concatenate([high, low, high], axis=1)
        got.append(
            lax.dot_general(
                left_scr[:, 3 * n * pairs : 3 * (n + 1) * pairs],
                right,
                (((1,), (1,)), ((), ())),
                preferred_element_type=f32,
            )
        )
    real_ref[...] = (got[0] - got[2]).reshape(freqs, rows, -1)
    imag_ref[...] = (got[0] - got[1]).reshape(freqs, rows, -1)


def chi_kernel(w_ref, own_ref, all_ref, real_ref, imag_ref, left_scr):
    @pl.when(pl.program_id(0) == 0)
    def _():
        fill_left(w_ref, own_ref, left_scr)

    chi_tile(all_ref[...], left_scr, real_ref, imag_ref)


def chi(weights, own, everyone):
    freqs, pairs = weights.shape
    rows = own.shape[0]
    num_g = everyone.shape[0]
    tile = min(num_g, 4 * LANES)
    out = jax.ShapeDtypeStruct((freqs, rows, num_g), f32)
    out_spec = pl.BlockSpec((freqs, rows, tile), lambda t: (0, 0, t))
    return pl.pallas_call(
        chi_kernel,
        grid=(num_g // tile,),
        out_shape=(out, out),
        in_specs=[
            pl.BlockSpec((freqs, pairs), lambda t: (0, 0)),
            pl.BlockSpec((rows, 2 * pairs), lambda t: (0, 0)),
            pl.BlockSpec((tile, 2 * pairs), lambda t: (t, 0)),
        ],
        out_specs=(out_spec, out_spec),
        scratch_shapes=[pltpu.VMEM((freqs * rows, 9 * pairs), bf16)],
        name="chi",
    )(weights, own, everyone)


def chi_group_kernel(counts, with_old, *refs):
    total = sum(counts)
    n = len(counts)
    _, w_ref, own_ref = refs[:3]
    pieces = refs[3 : 3 + total]
    rest = refs[3 + total + (2 if with_old else 0) :]
    real_ref, imag_ref, left_scr, got_scr, sems = rest
    step = pl.program_id(0)

    def copies(i):
        at, first = 0, sum(counts[:i])
        for j in range(counts[i]):
            ref = pieces[first + j]
            yield pltpu.make_async_copy(
                ref, got_scr.at[i, pl.ds(at, ref.shape[0])], sems.at[first + j]
            )
            at += ref.shape[0]

    @pl.when(step == 0)
    def _():
        for i in range(n):
            for copy in copies(i):
                copy.start()
        fill_left(w_ref, own_ref, left_scr)

    for i in range(n):

        @pl.when(step == i)
        def _(i=i):
            for copy in copies(i):
                copy.wait()

    chi_tile(got_scr[step], left_scr, real_ref, imag_ref)


def chi_group(weights, own, blocks, ids, first, num_g, old):
    freqs, pairs = weights.shape
    rows = own.shape[0]
    counts = tuple(len(b) for b in blocks)
    pieces = [p for b in blocks for p in b]
    out = jax.ShapeDtypeStruct((freqs, rows, num_g), f32)
    out_spec = pl.BlockSpec((freqs, rows, rows), lambda t, ids: (0, 0, ids[first + t]))
    hbm = pl.BlockSpec(memory_space=pl.ANY)
    olds = () if old is None else old
    return pl.pallas_call(
        functools.partial(chi_group_kernel, counts, old is not None),
        grid_spec=pltpu.PrefetchScalarGridSpec(
            num_scalar_prefetch=1,
            grid=(len(blocks),),
            in_specs=[
                pl.BlockSpec((freqs, pairs), lambda t, ids: (0, 0)),
                pl.BlockSpec((rows, 2 * pairs), lambda t, ids: (0, 0)),
            ]
            + [hbm] * (len(pieces) + len(olds)),
            out_specs=(out_spec, out_spec),
            scratch_shapes=[
                pltpu.VMEM((freqs * rows, 9 * pairs), bf16),
                pltpu.VMEM((len(blocks), rows, 2 * pairs), f32),
                pltpu.SemaphoreType.DMA((len(pieces),)),
            ],
        ),
        out_shape=(out, out),
        input_output_aliases={3 + len(pieces) + i: i for i in range(len(olds))},
        compiler_params=pltpu.CompilerParams(vmem_limit_bytes=VMEM_BYTES),
        name="chi",
    )(ids, weights, own, *pieces, *olds)


GROUPS = (((0, 0),), ((1, 0), (0, 3)), ((0, 1), (1, 3)), ((0, 2), (1, 1)), ((1, 2),))
RING = (0, 2, 3, 1)


class Links:
    def __init__(self, count):
        def place(i):
            return i // 4, i // 2 % 2, i % 2

        def at(z, y, core):
            return z * 4 + y * 2 + core

        def turn(i, by):
            z, y, core = place(i)
            return at(RING[(RING.index(z) + by) % 4], y, core)

        every = range(count)
        self.core = [(i, i ^ 1) for i in every]
        self.y = [(i, i ^ 2) for i in every]
        self.cw = [(i, turn(i, 1)) for i in every]
        self.ccw = [(i, turn(i, -1)) for i in every]
        self.near = np.array(
            [
                [[[turn(i ^ (2 * b) ^ a, r) for r in range(4)] for b in range(2)] for a in range(2)]
                for i in every
            ],
            dtype=np.int32,
        )
        self.order = np.stack([self.near[:, :, b, r] for g in GROUPS for b, r in g], axis=1)

    @staticmethod
    def fits(count):
        return count == len(RING) * 4


def send(value, pairs):
    return lax.ppermute(value, "blk", pairs)


def reduce_scatter(near, far, near_other, far_other, links, before):
    block = near.shape[0] // 4
    got_far = send(far_other, links.core)
    got_near = send(near_other, links.core)
    if before:
        cuts = ((2 * block, 4 * block), (0, 2 * block))
        high, low = (send(far[i:j] + got_far[i:j], links.y) for i, j in cuts)
        high, *_ = lax.optimization_barrier((high, *before))
        high = near[2 * block :] + got_near[2 * block :] + high
        to_cw, to_ccw, near = lax.optimization_barrier((high[:block], high[block:], near))
        low = near[: 2 * block] + got_near[: 2 * block] + low
        mine, next_cw = low[:block], low[block:]
    else:
        near = near + got_near + send(far + got_far, links.y)
        to_cw, to_ccw, next_cw, mine = lax.optimization_barrier(
            tuple(near[i * block : (i + 1) * block] for i in (2, 3, 1, 0))
        )
    two_back = send(to_cw, links.cw)
    ahead = send(to_ccw, links.ccw)
    next_cw = next_cw + two_back
    back = send(next_cw, links.cw)
    return mine, ahead, back


def gather_and_chi(weights, own, links, ids, num_g):
    cw = send(own, links.cw)
    later, cw = lax.optimization_barrier((own, cw))
    ccw = send(later, links.ccw)
    cw_later, ccw = lax.optimization_barrier((cw, ccw))
    mine = {(0, 0): own, (0, 3): cw, (0, 1): ccw, (0, 2): send(cw_later, links.cw)}
    for r in range(4):
        mine[1, r] = send(mine[0, r], links.y)
    old = None
    first = 0
    for group in GROUPS:
        blocks = []
        for b, r in group:
            blocks += [[mine[b, r]], [send(mine[b, r], links.core)]]
        old = chi_group(weights, own, blocks, ids, first, num_g, old)
        first += len(blocks)
    return old


def phase_table(size_x, first, planes, norm):
    x = first + jnp.arange(SLOTS, dtype=jnp.int32)
    k = jnp.arange(size_x, dtype=jnp.int32)
    ang = (k[:, None] * x[None, :] % size_x).astype(f32) * (2.0 * math.pi / size_x)
    live = (jnp.arange(SLOTS) < planes).astype(f32) * norm
    cos_t, sin_t = jnp.cos(ang) * live, jnp.sin(ang) * live
    table = jnp.stack(
        [jnp.concatenate([cos_t, sin_t], axis=1), jnp.concatenate([cos_t, -sin_t], axis=1)]
    )
    return jnp.broadcast_to(table.reshape(-1, 1), (table.size, LANES))


def polarizability(psi_val, psi_cond, e_val, e_cond, occ, freq, gmap):
    num_val, planes, size_y, size_z = psi_val.shape
    num_cond = psi_cond.shape[0]
    num_g = gmap.shape[0]
    pairs = num_val * num_cond
    size_x = planes * lax.axis_size("blk")
    norm = 1.0 / math.sqrt(size_x * size_y * size_z)

    val = jnp.transpose(psi_val, (1, 2, 3, 0))
    cond = jnp.transpose(psi_cond, (0, 1, 3, 2))
    if planes < SLOTS:
        val = jnp.pad(val, ((0, SLOTS - planes), (0, 0), (0, 0), (0, 0)))
        cond = jnp.pad(cond, ((0, 0), (0, SLOTS - planes), (0, 0), (0, 0)))

    kz = gmap % size_z
    ky = gmap // size_z % size_y
    kx = gmap // (size_z * size_y)
    mirrored = kz > size_z // 2
    col = jnp.where(mirrored, size_z - kz, kz) * size_y + jnp.where(
        mirrored, (size_y - ky) % size_y, ky
    )
    pick = jnp.stack([col, kx + jnp.where(mirrored, size_x, 0)]) * SUB
    cs = phase_table(size_x, lax.axis_index("blk") * planes, planes, norm)

    count = lax.axis_size("blk")
    links = Links(count) if Links.fits(count) else None
    if links is not None:
        tables = np.concatenate([x.reshape(count, -1) for x in (links.near, links.order)], axis=1)
        table = jnp.asarray(tables)[lax.axis_index("blk")]
        pick = pick.reshape(2, count, -1)[:, table[:count]].reshape(2, -1)
        ids = table[count:]
    owned = []
    for c in range(num_cond):
        made = transform(pick[0], pick[1], val, cond, c, cs, num_g)
        if links is None:
            whole = jnp.concatenate(made)
            owned.append((lax.psum_scatter(whole, "blk", scatter_dimension=0, tiled=True),))
        else:
            before = owned[-1][1:] if c == num_cond - 1 else ()
            owned.append(reduce_scatter(*made, links, before))
    for c, parts in enumerate(owned):
        owned[c] = sum(parts[1:], parts[0])
    own = jnp.stack(owned).reshape(num_cond, -1, 2, 4, num_val)
    rows = own.shape[1] * 4
    turned = lax.dynamic_slice_in_dim(mirrored, lax.axis_index("blk") * rows, rows)
    sign = jnp.where(turned, -1.0, 1.0).astype(f32)
    signs = jnp.stack([jnp.ones_like(sign), sign], axis=1).reshape(-1, 4, 2, 1, 1)
    own = (jnp.transpose(own, (1, 3, 2, 0, 4)) * signs).reshape(-1, 2 * pairs)

    gaps = e_val[None, :] - e_cond[:, None]
    gaps = gaps.reshape(1, pairs)
    occ_row = jnp.broadcast_to(occ.astype(f32)[None, :], (num_cond, num_val)).reshape(1, pairs)
    weights = occ_row * gaps / (gaps * gaps + (freq * freq)[:, None]) / math.sqrt(pairs)

    if links is not None:
        return gather_and_chi(weights, own, links, ids, num_g)
    return chi(weights, own, lax.all_gather(own, "blk", axis=0, tiled=True))


def solution(mesh):
    step = jax.shard_map(
        polarizability,
        mesh=mesh,
        in_specs=(
            P("cell", "blk", None, None),
            P("cell", "blk", None, None),
            P("cell"),
            P("cell"),
            P("cell"),
            P("cell"),
            P("cell"),
        ),
        out_specs=(P("cell", "blk", None), P("cell", "blk", None)),
        check_vma=False,
    )
    if not Links.fits(mesh.shape["blk"]):
        return step
    return step
```

```python
import functools
import math

import jax
import jax.numpy as jnp
import ml_dtypes
import numpy as np
from jax import lax
from jax.experimental import pallas as pl
from jax.experimental.pallas import tpu as pltpu
from jax.sharding import PartitionSpec as P


VMEM_BYTES = 64 * 2**20
LANES = 128
SUB = 8
PARTS = 4
SLOTS = 4
f32 = jnp.float32
bf16 = jnp.bfloat16


def split_np(table):
    high = table.astype(ml_dtypes.bfloat16)
    low = (table - high.astype(np.float64)).astype(ml_dtypes.bfloat16)
    return np.concatenate([high, high, low], axis=1)


def split3(block):
    high = block.astype(bf16)
    low = (block - high.astype(f32)).astype(bf16)
    return jnp.concatenate([high, low, high], axis=0)


def z_table(size_z):
    half = size_z // 2
    z = np.arange(size_z)
    cos_rows = np.cos(2 * np.pi * ((np.arange(half + 1)[:, None] * z) % size_z) / size_z)
    sin_rows = -np.sin(2 * np.pi * ((np.arange(1, half)[:, None] * z) % size_z) / size_z)
    return np.concatenate([cos_rows, sin_rows], axis=0)


def y_tables(size_y):
    k = np.arange(size_y)
    ang = 2 * np.pi * ((k[:, None] * k[None, :]) % size_y) / size_y
    cos_t, sin_t = np.cos(ang), np.sin(ang)
    real_rows = np.concatenate([cos_t, sin_t], axis=1)
    imag_rows = np.concatenate([-sin_t, cos_t], axis=1)
    full = np.stack([real_rows, imag_rows], axis=0).reshape(2, size_y // 4, 4, 2 * size_y)
    full = full.transpose(1, 0, 2, 3).reshape(2 * size_y, 2 * size_y)
    return full, full[:, :size_y]


def roll_sub(x, shift):
    return pltpu.roll(x, shift % SUB, axis=x.ndim - 2)


def in_steps(count, at_once, step):
    def several(i, carry):
        for u in range(at_once):
            step(i * at_once + u)
        return carry

    lax.fori_loop(0, count // at_once, several, 0)
    for i in range(count // at_once * at_once, count):
        step(i)


def transform_kernel(
    col_ref,
    phase_ref,
    val_hbm,
    cond_ref,
    dz_ref,
    dy_ref,
    dyr_ref,
    cs_hbm,
    *refs,
):
    outs, scratch = refs[:PARTS], refs[PARTS:]
    transform_parts(
        col_ref, phase_ref, val_hbm, cond_ref, dz_ref, dy_ref, dyr_ref, cs_hbm, outs, *scratch
    )


def transform_parts(
    col_ref,
    phase_ref,
    val_hbm,
    cond_ref,
    dz_ref,
    dy_ref,
    dyr_ref,
    cs_hbm,
    outs,
    val_scr,
    cs_scr,
    z_scr,
    tab_scr,
    out_scr,
    in_sems,
    out_sems,
):
    slots, size_y, size_z, lanes = val_hbm.shape
    half = size_z // 2
    groups_y = size_y // SUB
    pitch = size_z + SUB

    def plane(x):
        return pltpu.make_async_copy(val_hbm.at[x], val_scr.at[x], in_sems.at[x])

    phases = pltpu.make_async_copy(cs_hbm, cs_scr, in_sems.at[slots])
    for x in range(slots):
        plane(x).start()
    phases.start()

    def z_stage(x, yg):
        cond = cond_ref[x]
        parts = []
        for j in range(SUB):
            block = val_scr[x, yg * SUB + j]
            y = yg * SUB + j
            parts.append(block * jnp.broadcast_to(cond[:, y : y + 1], (size_z, lanes)))
        rhs = split3(jnp.concatenate(parts, axis=1))
        got = jnp.dot(dz_ref[...], rhs, preferred_element_type=f32)
        for j in range(SUB):
            at = pl.multiple_of((yg * SUB + j) * pitch, SUB)
            z_scr[x, pl.ds(at, size_z), :] = got[:, j * lanes : (j + 1) * lanes]

    def z_plane(x, carry):
        plane(x).wait()
        for yg in range(groups_y):
            z_stage(x, yg)
        return carry

    lax.fori_loop(0, slots, z_plane, 0)

    shape = (size_y // 4, SUB, lanes)
    sub = lax.broadcasted_iota(jnp.int32, shape, 1)
    low2 = (sub % 4) < 2
    low1 = (sub % 2) == 0

    def put(kz, got):
        a = [got[:, x * lanes : (x + 1) * lanes].reshape(shape) for x in range(slots)]
        p0 = jnp.where(low2, a[0], roll_sub(a[2], 2))
        p2 = jnp.where(low2, roll_sub(a[0], -2), a[2])
        p1 = jnp.where(low2, a[1], roll_sub(a[3], 2))
        p3 = jnp.where(low2, roll_sub(a[1], -2), a[3])
        tab_scr[kz, :, 0] = jnp.where(low1, p0, roll_sub(p1, 1))
        tab_scr[kz, :, 1] = jnp.where(low1, roll_sub(p0, -1), p1)
        tab_scr[kz, :, 2] = jnp.where(low1, p2, roll_sub(p3, 1))
        tab_scr[kz, :, 3] = jnp.where(low1, roll_sub(p2, -1), p3)

    def rows(k):
        return jnp.concatenate(
            [z_scr[x, pl.ds(k, size_y, stride=pitch), :] for x in range(slots)], axis=1
        )

    for kz in (0, half):
        put(kz, jnp.dot(dyr_ref[...], split3(rows(kz)), preferred_element_type=f32))

    def y_stage(step):
        kz = step + 1
        block = jnp.concatenate([rows(kz), rows(half + kz)], axis=0)
        put(kz, jnp.dot(dy_ref[...], split3(block), preferred_element_type=f32))

    in_steps(half - 1, 5, y_stage)

    sub1 = lax.broadcasted_iota(jnp.int32, (SUB, lanes), 0)
    m2 = (sub1 % 4) < 2
    m1 = (sub1 % 2) == 0
    kzs, kyq, _, _, _ = tab_scr.shape
    tab = tab_scr.reshape(kzs * kyq * 4 * SUB, lanes)
    quads = outs[0].shape[0]
    low4 = sub1 < 4
    phases.wait()

    def quad(q):
        t = []
        for i in range(4):
            d = tab[pl.ds(pl.multiple_of(col_ref[q * 4 + i], SUB), SUB), :]
            at = pl.ds(pl.multiple_of(phase_ref[q * 4 + i], SUB), SUB)
            p = cs_scr[at, :]
            turned = roll_sub(p, 4)
            t.append(d * jnp.where(low4, p, turned) + roll_sub(d, 4) * jnp.where(low4, turned, -p))
        v0 = jnp.where(m2, t[0], roll_sub(t[2], 2)) + jnp.where(m2, roll_sub(t[0], -2), t[2])
        v1 = jnp.where(m2, t[1], roll_sub(t[3], 2)) + jnp.where(m2, roll_sub(t[1], -2), t[3])
        out_scr[q] = jnp.where(m1, v0, roll_sub(v1, 1)) + jnp.where(m1, roll_sub(v0, -1), v1)

    copies = []
    for n in reversed(range(PARTS)):
        first = n * quads
        in_steps(quads, math.gcd(quads, 2 * SUB), lambda q, first=first: quad(first + q))
        copies.append(
            pltpu.make_async_copy(out_scr.at[pl.ds(first, quads)], outs[n], out_sems.at[n])
        )
        copies[-1].start()
    for copy in copies:
        copy.wait()


def transform(col, phase, val, cond, c, cs, num_g):
    slots, size_y, size_z, lanes = val.shape
    dz = jnp.asarray(split_np(z_table(size_z)))
    full, real_only = y_tables(size_y)
    dy, dyr = jnp.asarray(split_np(full)), jnp.asarray(split_np(real_only))
    vmem = pl.BlockSpec(memory_space=pltpu.VMEM)
    smem = pl.BlockSpec(memory_space=pltpu.SMEM)
    hbm = pl.BlockSpec(memory_space=pl.ANY)
    return pl.pallas_call(
        transform_kernel,
        grid=(1,),
        out_shape=(jax.ShapeDtypeStruct((num_g // 4 // PARTS, SUB, lanes), f32),) * PARTS,
        in_specs=[
            smem,
            smem,
            hbm,
            pl.BlockSpec((None,) + cond.shape[1:], lambda i: (c, 0, 0, 0)),
            vmem,
            vmem,
            vmem,
            hbm,
        ],
        out_specs=(hbm,) * PARTS,
        scratch_shapes=[
            pltpu.VMEM(val.shape, f32),
            pltpu.VMEM(cs.shape, f32),
            pltpu.VMEM((slots, (size_z + SUB) * size_y, lanes), f32),
            pltpu.VMEM((size_z // 2 + 1, size_y // 4, 4, SUB, lanes), f32),
            pltpu.VMEM((num_g // 4, SUB, lanes), f32),
            pltpu.SemaphoreType.DMA((slots + 1,)),
            pltpu.SemaphoreType.DMA((PARTS,)),
        ],
        compiler_params=pltpu.CompilerParams(vmem_limit_bytes=VMEM_BYTES),
        name="transform",
    )(col, phase, val, cond, dz, dy, dyr, cs)


def split_lanes(block):
    high = block.astype(bf16)
    low = (block - high.astype(f32)).astype(bf16)
    return high, low


def fill_left(w_ref, own_ref, left_scr):
    freqs = w_ref.shape[0]
    rows, pairs2 = own_ref.shape
    pairs = pairs2 // 2

    def fill(w, carry):
        row = w_ref[pl.ds(w, 1), :]
        a = own_ref[:, :pairs] * row
        b = own_ref[:, pairs:] * row
        at = pl.ds(pl.multiple_of(w * rows, rows), rows)
        for n, side in enumerate((a + b, a, b)):
            high, low = split_lanes(side)
            left_scr[at, (3 * n) * pairs : (3 * n + 1) * pairs] = high
            left_scr[at, (3 * n + 1) * pairs : (3 * n + 2) * pairs] = high
            left_scr[at, (3 * n + 2) * pairs : (3 * n + 3) * pairs] = low
        return carry

    lax.fori_loop(0, freqs, fill, 0)


def chi_tile(block, left_scr, real_ref, imag_ref):
    freqs, rows, _ = real_ref.shape
    pairs = block.shape[1] // 2
    c, d = block[:, :pairs], block[:, pairs:]
    got = []
    for n, side in enumerate((c, c + d, c - d)):
        high, low = split_lanes(side)
        right = jnp.concatenate([high, low, high], axis=1)
        got.append(
            lax.dot_general(
                left_scr[:, 3 * n * pairs : 3 * (n + 1) * pairs],
                right,
                (((1,), (1,)), ((), ())),
                preferred_element_type=f32,
            )
        )
    real_ref[...] = (got[0] - got[2]).reshape(freqs, rows, -1)
    imag_ref[...] = (got[0] - got[1]).reshape(freqs, rows, -1)


def chi_kernel(w_ref, own_ref, all_ref, real_ref, imag_ref, left_scr):
    @pl.when(pl.program_id(0) == 0)
    def _():
        fill_left(w_ref, own_ref, left_scr)

    chi_tile(all_ref[...], left_scr, real_ref, imag_ref)


def chi(weights, own, everyone):
    freqs, pairs = weights.shape
    rows = own.shape[0]
    num_g = everyone.shape[0]
    tile = min(num_g, 4 * LANES)
    out = jax.ShapeDtypeStruct((freqs, rows, num_g), f32)
    out_spec = pl.BlockSpec((freqs, rows, tile), lambda t: (0, 0, t))
    return pl.pallas_call(
        chi_kernel,
        grid=(num_g // tile,),
        out_shape=(out, out),
        in_specs=[
            pl.BlockSpec((freqs, pairs), lambda t: (0, 0)),
            pl.BlockSpec((rows, 2 * pairs), lambda t: (0, 0)),
            pl.BlockSpec((tile, 2 * pairs), lambda t: (t, 0)),
        ],
        out_specs=(out_spec, out_spec),
        scratch_shapes=[pltpu.VMEM((freqs * rows, 9 * pairs), bf16)],
        name="chi",
    )(weights, own, everyone)


def chi_group_kernel(counts, with_old, *refs):
    total = sum(counts)
    n = len(counts)
    _, w_ref, own_ref = refs[:3]
    pieces = refs[3 : 3 + total]
    rest = refs[3 + total + (2 if with_old else 0) :]
    real_ref, imag_ref, left_scr, got_scr, sems = rest
    step = pl.program_id(0)

    def copies(i):
        at, first = 0, sum(counts[:i])
        for j in range(counts[i]):
            ref = pieces[first + j]
            yield pltpu.make_async_copy(
                ref, got_scr.at[i, pl.ds(at, ref.shape[0])], sems.at[first + j]
            )
            at += ref.shape[0]

    @pl.when(step == 0)
    def _():
        for i in range(n):
            for copy in copies(i):
                copy.start()
        fill_left(w_ref, own_ref, left_scr)

    for i in range(n):

        @pl.when(step == i)
        def _(i=i):
            for copy in copies(i):
                copy.wait()

    chi_tile(got_scr[step], left_scr, real_ref, imag_ref)


def chi_group(weights, own, blocks, ids, first, num_g, old):
    freqs, pairs = weights.shape
    rows = own.shape[0]
    counts = tuple(len(b) for b in blocks)
    pieces = [p for b in blocks for p in b]
    out = jax.ShapeDtypeStruct((freqs, rows, num_g), f32)
    out_spec = pl.BlockSpec((freqs, rows, rows), lambda t, ids: (0, 0, ids[first + t]))
    hbm = pl.BlockSpec(memory_space=pl.ANY)
    olds = () if old is None else old
    return pl.pallas_call(
        functools.partial(chi_group_kernel, counts, old is not None),
        grid_spec=pltpu.PrefetchScalarGridSpec(
            num_scalar_prefetch=1,
            grid=(len(blocks),),
            in_specs=[
                pl.BlockSpec((freqs, pairs), lambda t, ids: (0, 0)),
                pl.BlockSpec((rows, 2 * pairs), lambda t, ids: (0, 0)),
            ]
            + [hbm] * (len(pieces) + len(olds)),
            out_specs=(out_spec, out_spec),
            scratch_shapes=[
                pltpu.VMEM((freqs * rows, 9 * pairs), bf16),
                pltpu.VMEM((len(blocks), rows, 2 * pairs), f32),
                pltpu.SemaphoreType.DMA((len(pieces),)),
            ],
        ),
        out_shape=(out, out),
        input_output_aliases={3 + len(pieces) + i: i for i in range(len(olds))},
        compiler_params=pltpu.CompilerParams(vmem_limit_bytes=VMEM_BYTES),
        name="chi",
    )(ids, weights, own, *pieces, *olds)


GROUPS = (((0, 0),), ((1, 0), (0, 3)), ((0, 1), (1, 3)), ((0, 2), (1, 1)), ((1, 2),))
RING = (0, 2, 3, 1)


class Links:
    def __init__(self, count):
        def place(i):
            return i // 4, i // 2 % 2, i % 2

        def at(z, y, core):
            return z * 4 + y * 2 + core

        def turn(i, by):
            z, y, core = place(i)
            return at(RING[(RING.index(z) + by) % 4], y, core)

        every = range(count)
        self.core = [(i, i ^ 1) for i in every]
        self.y = [(i, i ^ 2) for i in every]
        self.cw = [(i, turn(i, 1)) for i in every]
        self.ccw = [(i, turn(i, -1)) for i in every]
        self.near = np.array(
            [
                [[[turn(i ^ (2 * b) ^ a, r) for r in range(4)] for b in range(2)] for a in range(2)]
                for i in every
            ],
            dtype=np.int32,
        )
        self.order = np.stack([self.near[:, :, b, r] for g in GROUPS for b, r in g], axis=1)

    @staticmethod
    def fits(count):
        return count == len(RING) * 4


def send(value, pairs):
    return lax.ppermute(value, "blk", pairs)


def reduce_scatter(near, far, near_other, far_other, links, before):
    block = near.shape[0] // 4
    got_far = send(far_other, links.core)
    got_near = send(near_other, links.core)
    cuts = ((2 * block, 4 * block), (0, 2 * block))
    high, low = (send(far[i:j] + got_far[i:j], links.y) for i, j in cuts)
    if before:
        high, *_ = lax.optimization_barrier((high, *before))
    high = near[2 * block :] + got_near[2 * block :] + high
    to_cw, to_ccw, near = lax.optimization_barrier((high[:block], high[block:], near))
    low = near[: 2 * block] + got_near[: 2 * block] + low
    mine, next_cw = low[:block], low[block:]
    two_back = send(to_cw, links.cw)
    ahead = send(to_ccw, links.ccw)
    next_cw = next_cw + two_back
    back = send(next_cw, links.cw)
    return mine, ahead, back


def gather_and_chi(weights, own, links, ids, num_g):
    cw = send(own, links.cw)
    later, cw = lax.optimization_barrier((own, cw))
    ccw = send(later, links.ccw)
    cw_later, ccw = lax.optimization_barrier((cw, ccw))
    mine = {(0, 0): own, (0, 3): cw, (0, 1): ccw, (0, 2): send(cw_later, links.cw)}
    for r in range(4):
        mine[1, r] = send(mine[0, r], links.y)
    old = None
    first = 0
    for group in GROUPS:
        blocks = []
        for b, r in group:
            blocks += [[mine[b, r]], [send(mine[b, r], links.core)]]
        old = chi_group(weights, own, blocks, ids, first, num_g, old)
        first += len(blocks)
    return old


def phase_table(size_x, first, planes, norm):
    x = first + jnp.arange(SLOTS, dtype=jnp.int32)
    k = jnp.arange(size_x, dtype=jnp.int32)
    ang = (k[:, None] * x[None, :] % size_x).astype(f32) * (2.0 * math.pi / size_x)
    live = (jnp.arange(SLOTS) < planes).astype(f32) * norm
    cos_t, sin_t = jnp.cos(ang) * live, jnp.sin(ang) * live
    table = jnp.stack(
        [jnp.concatenate([cos_t, sin_t], axis=1), jnp.concatenate([cos_t, -sin_t], axis=1)]
    )
    return jnp.broadcast_to(table.reshape(-1, 1), (table.size, LANES))


def polarizability(psi_val, psi_cond, e_val, e_cond, occ, freq, gmap):
    num_val, planes, size_y, size_z = psi_val.shape
    num_cond = psi_cond.shape[0]
    num_g = gmap.shape[0]
    pairs = num_val * num_cond
    size_x = planes * lax.axis_size("blk")
    norm = 1.0 / math.sqrt(size_x * size_y * size_z)

    val = jnp.transpose(psi_val, (1, 2, 3, 0))
    cond = jnp.transpose(psi_cond, (0, 1, 3, 2))
    if planes < SLOTS:
        val = jnp.pad(val, ((0, SLOTS - planes), (0, 0), (0, 0), (0, 0)))
        cond = jnp.pad(cond, ((0, 0), (0, SLOTS - planes), (0, 0), (0, 0)))

    kz = gmap % size_z
    ky = gmap // size_z % size_y
    kx = gmap // (size_z * size_y)
    mirrored = kz > size_z // 2
    col = jnp.where(mirrored, size_z - kz, kz) * size_y + jnp.where(
        mirrored, (size_y - ky) % size_y, ky
    )
    pick = jnp.stack([col, kx + jnp.where(mirrored, size_x, 0)]) * SUB
    cs = phase_table(size_x, lax.axis_index("blk") * planes, planes, norm)

    count = lax.axis_size("blk")
    links = Links(count) if Links.fits(count) else None
    if links is not None:
        tables = np.concatenate([x.reshape(count, -1) for x in (links.near, links.order)], axis=1)
        table = jnp.asarray(tables)[lax.axis_index("blk")]
        pick = pick.reshape(2, count, -1)[:, table[:count]].reshape(2, -1)
        ids = table[count:]
    owned = []
    for c in range(num_cond):
        made = transform(pick[0], pick[1], val, cond, c, cs, num_g)
        if links is None:
            whole = jnp.concatenate(made)
            owned.append((lax.psum_scatter(whole, "blk", scatter_dimension=0, tiled=True),))
        else:
            before = owned[-1][1:] if c == num_cond - 1 else ()
            owned.append(reduce_scatter(*made, links, before))
    for c, parts in enumerate(owned):
        owned[c] = sum(parts[1:], parts[0])
    own = jnp.stack(owned).reshape(num_cond, -1, 2, 4, num_val)
    rows = own.shape[1] * 4
    turned = lax.dynamic_slice_in_dim(mirrored, lax.axis_index("blk") * rows, rows)
    sign = jnp.where(turned, -1.0, 1.0).astype(f32)
    signs = jnp.stack([jnp.ones_like(sign), sign], axis=1).reshape(-1, 4, 2, 1, 1)
    own = (jnp.transpose(own, (1, 3, 2, 0, 4)) * signs).reshape(-1, 2 * pairs)

    gaps = e_val[None, :] - e_cond[:, None]
    gaps = gaps.reshape(1, pairs)
    occ_row = jnp.broadcast_to(occ.astype(f32)[None, :], (num_cond, num_val)).reshape(1, pairs)
    weights = occ_row * gaps / (gaps * gaps + (freq * freq)[:, None]) / math.sqrt(pairs)

    if links is not None:
        return gather_and_chi(weights, own, links, ids, num_g)
    return chi(weights, own, lax.all_gather(own, "blk", axis=0, tiled=True))


def solution(mesh):
    step = jax.shard_map(
        polarizability,
        mesh=mesh,
        in_specs=(
            P("cell", "blk", None, None),
            P("cell", "blk", None, None),
            P("cell"),
            P("cell"),
            P("cell"),
            P("cell"),
            P("cell"),
        ),
        out_specs=(P("cell", "blk", None), P("cell", "blk", None)),
        check_vma=False,
    )
    if not Links.fits(mesh.shape["blk"]):
        return step
    return step
```

```python
import functools
import math

import jax
import jax.numpy as jnp
import ml_dtypes
import numpy as np
from jax import lax
from jax.experimental import pallas as pl
from jax.experimental.pallas import tpu as pltpu
from jax.sharding import PartitionSpec as P


VMEM_BYTES = 64 * 2**20
LANES = 128
SUB = 8
PARTS = 4
SLOTS = 4
f32 = jnp.float32
bf16 = jnp.bfloat16


def split_np(table):
    high = table.astype(ml_dtypes.bfloat16)
    low = (table - high.astype(np.float64)).astype(ml_dtypes.bfloat16)
    return np.concatenate([high, high, low], axis=1)


def split3(block):
    high = block.astype(bf16)
    low = (block - high.astype(f32)).astype(bf16)
    return jnp.concatenate([high, low, high], axis=0)


def z_table(size_z):
    half = size_z // 2
    z = np.arange(size_z)
    cos_rows = np.cos(2 * np.pi * ((np.arange(half + 1)[:, None] * z) % size_z) / size_z)
    sin_rows = -np.sin(2 * np.pi * ((np.arange(1, half)[:, None] * z) % size_z) / size_z)
    return np.concatenate([cos_rows, sin_rows], axis=0)


def y_tables(size_y):
    k = np.arange(size_y)
    ang = 2 * np.pi * ((k[:, None] * k[None, :]) % size_y) / size_y
    cos_t, sin_t = np.cos(ang), np.sin(ang)
    real_rows = np.concatenate([cos_t, sin_t], axis=1)
    imag_rows = np.concatenate([-sin_t, cos_t], axis=1)
    full = np.stack([real_rows, imag_rows], axis=0).reshape(2, size_y // 4, 4, 2 * size_y)
    full = full.transpose(1, 0, 2, 3).reshape(2 * size_y, 2 * size_y)
    return full, full[:, :size_y]


def roll_sub(x, shift):
    return pltpu.roll(x, shift % SUB, axis=x.ndim - 2)


def in_steps(count, at_once, step):
    def several(i, carry):
        for u in range(at_once):
            step(i * at_once + u)
        return carry

    lax.fori_loop(0, count // at_once, several, 0)
    for i in range(count // at_once * at_once, count):
        step(i)


def transform_kernel(
    col_ref,
    phase_ref,
    val_hbm,
    cond_ref,
    dz_ref,
    dy_ref,
    dyr_ref,
    cs_hbm,
    *refs,
):
    outs, scratch = refs[:PARTS], refs[PARTS:]
    transform_parts(
        col_ref, phase_ref, val_hbm, cond_ref, dz_ref, dy_ref, dyr_ref, cs_hbm, outs, *scratch
    )


def transform_parts(
    col_ref,
    phase_ref,
    val_hbm,
    cond_ref,
    dz_ref,
    dy_ref,
    dyr_ref,
    cs_hbm,
    outs,
    val_scr,
    cs_scr,
    z_scr,
    tab_scr,
    out_scr,
    in_sems,
    out_sems,
):
    slots, size_y, size_z, lanes = val_hbm.shape
    half = size_z // 2
    groups_y = size_y // SUB
    pitch = size_z + SUB

    def plane(x):
        return pltpu.make_async_copy(val_hbm.at[x], val_scr.at[x], in_sems.at[x])

    phases = pltpu.make_async_copy(cs_hbm, cs_scr, in_sems.at[slots])
    for x in range(slots):
        plane(x).start()
    phases.start()

    def z_stage(x, yg):
        cond = cond_ref[x]
        parts = []
        for j in range(SUB):
            block = val_scr[x, yg * SUB + j]
            y = yg * SUB + j
            parts.append(block * jnp.broadcast_to(cond[:, y : y + 1], (size_z, lanes)))
        rhs = split3(jnp.concatenate(parts, axis=1))
        got = jnp.dot(dz_ref[...], rhs, preferred_element_type=f32)
        for j in range(SUB):
            at = pl.multiple_of((yg * SUB + j) * pitch, SUB)
            z_scr[x, pl.ds(at, size_z), :] = got[:, j * lanes : (j + 1) * lanes]

    def z_plane(x, carry):
        plane(x).wait()
        for yg in range(groups_y):
            z_stage(x, yg)
        return carry

    lax.fori_loop(0, slots, z_plane, 0)

    shape = (size_y // 4, SUB, lanes)
    sub = lax.broadcasted_iota(jnp.int32, shape, 1)
    low2 = (sub % 4) < 2
    low1 = (sub % 2) == 0

    def put(kz, got):
        a = [got[:, x * lanes : (x + 1) * lanes].reshape(shape) for x in range(slots)]
        p0 = jnp.where(low2, a[0], roll_sub(a[2], 2))
        p2 = jnp.where(low2, roll_sub(a[0], -2), a[2])
        p1 = jnp.where(low2, a[1], roll_sub(a[3], 2))
        p3 = jnp.where(low2, roll_sub(a[1], -2), a[3])
        tab_scr[kz, :, 0] = jnp.where(low1, p0, roll_sub(p1, 1))
        tab_scr[kz, :, 1] = jnp.where(low1, roll_sub(p0, -1), p1)
        tab_scr[kz, :, 2] = jnp.where(low1, p2, roll_sub(p3, 1))
        tab_scr[kz, :, 3] = jnp.where(low1, roll_sub(p2, -1), p3)

    def rows(k):
        return jnp.concatenate(
            [z_scr[x, pl.ds(k, size_y, stride=pitch), :] for x in range(slots)], axis=1
        )

    for kz in (0, half):
        put(kz, jnp.dot(dyr_ref[...], split3(rows(kz)), preferred_element_type=f32))

    def y_stage(step):
        kz = step + 1
        block = jnp.concatenate([rows(kz), rows(half + kz)], axis=0)
        put(kz, jnp.dot(dy_ref[...], split3(block), preferred_element_type=f32))

    in_steps(half - 1, 5, y_stage)

    sub1 = lax.broadcasted_iota(jnp.int32, (SUB, lanes), 0)
    m2 = (sub1 % 4) < 2
    m1 = (sub1 % 2) == 0
    kzs, kyq, _, _, _ = tab_scr.shape
    tab = tab_scr.reshape(kzs * kyq * 4 * SUB, lanes)
    quads = outs[0].shape[0]
    low4 = sub1 < 4
    phases.wait()

    def quad(q):
        t = []
        for i in range(4):
            d = tab[pl.ds(pl.multiple_of(col_ref[q * 4 + i], SUB), SUB), :]
            at = pl.ds(pl.multiple_of(phase_ref[q * 4 + i], SUB), SUB)
            p = cs_scr[at, :]
            turned = roll_sub(p, 4)
            t.append(d * jnp.where(low4, p, turned) + roll_sub(d, 4) * jnp.where(low4, turned, -p))
        v0 = jnp.where(m2, t[0], roll_sub(t[2], 2)) + jnp.where(m2, roll_sub(t[0], -2), t[2])
        v1 = jnp.where(m2, t[1], roll_sub(t[3], 2)) + jnp.where(m2, roll_sub(t[1], -2), t[3])
        out_scr[q] = jnp.where(m1, v0, roll_sub(v1, 1)) + jnp.where(m1, roll_sub(v0, -1), v1)

    copies = []
    for n in reversed(range(PARTS)):
        first = n * quads
        in_steps(quads, math.gcd(quads, 2 * SUB), lambda q, first=first: quad(first + q))
        copies.append(
            pltpu.make_async_copy(out_scr.at[pl.ds(first, quads)], outs[n], out_sems.at[n])
        )
        copies[-1].start()
    for copy in copies:
        copy.wait()


def transform(col, phase, val, cond, c, cs, num_g):
    slots, size_y, size_z, lanes = val.shape
    dz = jnp.asarray(split_np(z_table(size_z)))
    full, real_only = y_tables(size_y)
    dy, dyr = jnp.asarray(split_np(full)), jnp.asarray(split_np(real_only))
    vmem = pl.BlockSpec(memory_space=pltpu.VMEM)
    smem = pl.BlockSpec(memory_space=pltpu.SMEM)
    hbm = pl.BlockSpec(memory_space=pl.ANY)
    return pl.pallas_call(
        transform_kernel,
        grid=(1,),
        out_shape=(jax.ShapeDtypeStruct((num_g // 4 // PARTS, SUB, lanes), f32),) * PARTS,
        in_specs=[
            smem,
            smem,
            hbm,
            pl.BlockSpec((None,) + cond.shape[1:], lambda i: (c, 0, 0, 0)),
            vmem,
            vmem,
            vmem,
            hbm,
        ],
        out_specs=(hbm,) * PARTS,
        scratch_shapes=[
            pltpu.VMEM(val.shape, f32),
            pltpu.VMEM(cs.shape, f32),
            pltpu.VMEM((slots, (size_z + SUB) * size_y, lanes), f32),
            pltpu.VMEM((size_z // 2 + 1, size_y // 4, 4, SUB, lanes), f32),
            pltpu.VMEM((num_g // 4, SUB, lanes), f32),
            pltpu.SemaphoreType.DMA((slots + 1,)),
            pltpu.SemaphoreType.DMA((PARTS,)),
        ],
        compiler_params=pltpu.CompilerParams(vmem_limit_bytes=VMEM_BYTES),
        name="transform",
    )(col, phase, val, cond, dz, dy, dyr, cs)


def split_lanes(block):
    high = block.astype(bf16)
    low = (block - high.astype(f32)).astype(bf16)
    return high, low


def fill_left(w_ref, own_ref, left_scr):
    freqs = w_ref.shape[0]
    rows, pairs2 = own_ref.shape
    pairs = pairs2 // 2

    def fill(w, carry):
        row = w_ref[pl.ds(w, 1), :]
        a = own_ref[:, :pairs] * row
        b = own_ref[:, pairs:] * row
        at = pl.ds(pl.multiple_of(w * rows, rows), rows)
        for n, side in enumerate((a + b, a, b)):
            high, low = split_lanes(side)
            left_scr[at, (3 * n) * pairs : (3 * n + 1) * pairs] = high
            left_scr[at, (3 * n + 1) * pairs : (3 * n + 2) * pairs] = high
            left_scr[at, (3 * n + 2) * pairs : (3 * n + 3) * pairs] = low
        return carry

    lax.fori_loop(0, freqs, fill, 0)


def chi_tile(block, left_scr, real_ref, imag_ref):
    freqs, rows, _ = real_ref.shape
    pairs = block.shape[1] // 2
    c, d = block[:, :pairs], block[:, pairs:]
    got = []
    for n, side in enumerate((c, c + d, c - d)):
        high, low = split_lanes(side)
        right = jnp.concatenate([high, low, high], axis=1)
        got.append(
            lax.dot_general(
                left_scr[:, 3 * n * pairs : 3 * (n + 1) * pairs],
                right,
                (((1,), (1,)), ((), ())),
                preferred_element_type=f32,
            )
        )
    real_ref[...] = (got[0] - got[2]).reshape(freqs, rows, -1)
    imag_ref[...] = (got[0] - got[1]).reshape(freqs, rows, -1)


def chi_kernel(w_ref, own_ref, all_ref, real_ref, imag_ref, left_scr):
    @pl.when(pl.program_id(0) == 0)
    def _():
        fill_left(w_ref, own_ref, left_scr)

    chi_tile(all_ref[...], left_scr, real_ref, imag_ref)


def chi(weights, own, everyone):
    freqs, pairs = weights.shape
    rows = own.shape[0]
    num_g = everyone.shape[0]
    tile = min(num_g, 4 * LANES)
    out = jax.ShapeDtypeStruct((freqs, rows, num_g), f32)
    out_spec = pl.BlockSpec((freqs, rows, tile), lambda t: (0, 0, t))
    return pl.pallas_call(
        chi_kernel,
        grid=(num_g // tile,),
        out_shape=(out, out),
        in_specs=[
            pl.BlockSpec((freqs, pairs), lambda t: (0, 0)),
            pl.BlockSpec((rows, 2 * pairs), lambda t: (0, 0)),
            pl.BlockSpec((tile, 2 * pairs), lambda t: (t, 0)),
        ],
        out_specs=(out_spec, out_spec),
        scratch_shapes=[pltpu.VMEM((freqs * rows, 9 * pairs), bf16)],
        name="chi",
    )(weights, own, everyone)


def chi_group_kernel(counts, with_old, *refs):
    total = sum(counts)
    n = len(counts)
    _, w_ref, own_ref = refs[:3]
    pieces = refs[3 : 3 + total]
    rest = refs[3 + total + (2 if with_old else 0) :]
    real_ref, imag_ref, left_scr, got_scr, sems = rest
    step = pl.program_id(0)

    def copies(i):
        at, first = 0, sum(counts[:i])
        for j in range(counts[i]):
            ref = pieces[first + j]
            yield pltpu.make_async_copy(
                ref, got_scr.at[i, pl.ds(at, ref.shape[0])], sems.at[first + j]
            )
            at += ref.shape[0]

    @pl.when(step == 0)
    def _():
        for i in range(n):
            for copy in copies(i):
                copy.start()
        fill_left(w_ref, own_ref, left_scr)

    for i in range(n):

        @pl.when(step == i)
        def _(i=i):
            for copy in copies(i):
                copy.wait()

    chi_tile(got_scr[step], left_scr, real_ref, imag_ref)


def chi_group(weights, own, blocks, ids, first, num_g, old):
    freqs, pairs = weights.shape
    rows = own.shape[0]
    counts = tuple(len(b) for b in blocks)
    pieces = [p for b in blocks for p in b]
    out = jax.ShapeDtypeStruct((freqs, rows, num_g), f32)
    out_spec = pl.BlockSpec((freqs, rows, rows), lambda t, ids: (0, 0, ids[first + t]))
    hbm = pl.BlockSpec(memory_space=pl.ANY)
    olds = () if old is None else old
    return pl.pallas_call(
        functools.partial(chi_group_kernel, counts, old is not None),
        grid_spec=pltpu.PrefetchScalarGridSpec(
            num_scalar_prefetch=1,
            grid=(len(blocks),),
            in_specs=[
                pl.BlockSpec((freqs, pairs), lambda t, ids: (0, 0)),
                pl.BlockSpec((rows, 2 * pairs), lambda t, ids: (0, 0)),
            ]
            + [hbm] * (len(pieces) + len(olds)),
            out_specs=(out_spec, out_spec),
            scratch_shapes=[
                pltpu.VMEM((freqs * rows, 9 * pairs), bf16),
                pltpu.VMEM((len(blocks), rows, 2 * pairs), f32),
                pltpu.SemaphoreType.DMA((len(pieces),)),
            ],
        ),
        out_shape=(out, out),
        input_output_aliases={3 + len(pieces) + i: i for i in range(len(olds))},
        compiler_params=pltpu.CompilerParams(vmem_limit_bytes=VMEM_BYTES),
        name="chi",
    )(ids, weights, own, *pieces, *olds)


GROUPS = (((0, 0),), ((1, 0), (0, 3)), ((0, 1), (1, 3)), ((0, 2), (1, 1)), ((1, 2),))
RING = (0, 2, 3, 1)


class Links:
    def __init__(self, count):
        def place(i):
            return i // 4, i // 2 % 2, i % 2

        def at(z, y, core):
            return z * 4 + y * 2 + core

        def turn(i, by):
            z, y, core = place(i)
            return at(RING[(RING.index(z) + by) % 4], y, core)

        every = range(count)
        self.core = [(i, i ^ 1) for i in every]
        self.y = [(i, i ^ 2) for i in every]
        self.cw = [(i, turn(i, 1)) for i in every]
        self.ccw = [(i, turn(i, -1)) for i in every]
        self.near = np.array(
            [
                [[[turn(i ^ (2 * b) ^ a, r) for r in range(4)] for b in range(2)] for a in range(2)]
                for i in every
            ],
            dtype=np.int32,
        )
        self.order = np.stack([self.near[:, :, b, r] for g in GROUPS for b, r in g], axis=1)

    @staticmethod
    def fits(count):
        return count == len(RING) * 4


def send(value, pairs):
    return lax.ppermute(value, "blk", pairs)


def reduce_scatter(near, far, near_other, far_other, links, before):
    block = near.shape[0] // 4
    got_far = send(far_other, links.core)
    got_near = send(near_other, links.core)
    cuts = ((2 * block, 4 * block), (0, 2 * block))
    high, low = (send(far[i:j] + got_far[i:j], links.y) for i, j in cuts)
    if before:
        high, *_ = lax.optimization_barrier((high, *before))
    high = near[2 * block :] + got_near[2 * block :] + high
    to_cw, to_ccw, near = lax.optimization_barrier((high[:block], high[block:], near))
    low = near[: 2 * block] + got_near[: 2 * block] + low
    mine, next_cw = low[:block], low[block:]
    two_back = send(to_cw, links.cw)
    ahead = send(to_ccw, links.ccw)
    next_cw = next_cw + two_back
    back = send(next_cw, links.cw)
    return mine, ahead, back


def gather_and_chi(weights, own, links, ids, num_g):
    cw = send(own, links.cw)
    later, cw = lax.optimization_barrier((own, cw))
    ccw = send(later, links.ccw)
    cw_later, ccw = lax.optimization_barrier((cw, ccw))
    mine = {(0, 0): [own], (0, 3): [cw], (0, 1): [ccw]}
    mine[0, 2] = [send(cw_later, links.cw)]
    for r in (0, 3, 1):
        mine[1, r] = [send(mine[0, r][0], links.y)]
    half = own.shape[0] // 2
    mine[1, 2] = [send(mine[0, 2][0][:half], links.y), send(mine[1, 1][0][half:], links.ccw)]
    old = None
    first = 0
    for group in GROUPS:
        blocks = []
        for b, r in group:
            twins = [send(piece, links.core) for piece in mine[b, r]]
            blocks += [mine[b, r], twins]
        old = chi_group(weights, own, blocks, ids, first, num_g, old)
        first += len(blocks)
    return old


def phase_table(size_x, first, planes, norm):
    x = first + jnp.arange(SLOTS, dtype=jnp.int32)
    k = jnp.arange(size_x, dtype=jnp.int32)
    ang = (k[:, None] * x[None, :] % size_x).astype(f32) * (2.0 * math.pi / size_x)
    live = (jnp.arange(SLOTS) < planes).astype(f32) * norm
    cos_t, sin_t = jnp.cos(ang) * live, jnp.sin(ang) * live
    table = jnp.stack(
        [jnp.concatenate([cos_t, sin_t], axis=1), jnp.concatenate([cos_t, -sin_t], axis=1)]
    )
    return jnp.broadcast_to(table.reshape(-1, 1), (table.size, LANES))


def polarizability(psi_val, psi_cond, e_val, e_cond, occ, freq, gmap):
    num_val, planes, size_y, size_z = psi_val.shape
    num_cond = psi_cond.shape[0]
    num_g = gmap.shape[0]
    pairs = num_val * num_cond
    size_x = planes * lax.axis_size("blk")
    norm = 1.0 / math.sqrt(size_x * size_y * size_z)

    val = jnp.transpose(psi_val, (1, 2, 3, 0))
    cond = jnp.transpose(psi_cond, (0, 1, 3, 2))
    if planes < SLOTS:
        val = jnp.pad(val, ((0, SLOTS - planes), (0, 0), (0, 0), (0, 0)))
        cond = jnp.pad(cond, ((0, 0), (0, SLOTS - planes), (0, 0), (0, 0)))

    kz = gmap % size_z
    ky = gmap // size_z % size_y
    kx = gmap // (size_z * size_y)
    mirrored = kz > size_z // 2
    col = jnp.where(mirrored, size_z - kz, kz) * size_y + jnp.where(
        mirrored, (size_y - ky) % size_y, ky
    )
    pick = jnp.stack([col, kx + jnp.where(mirrored, size_x, 0)]) * SUB
    cs = phase_table(size_x, lax.axis_index("blk") * planes, planes, norm)

    count = lax.axis_size("blk")
    links = Links(count) if Links.fits(count) else None
    if links is not None:
        tables = np.concatenate([x.reshape(count, -1) for x in (links.near, links.order)], axis=1)
        table = jnp.asarray(tables)[lax.axis_index("blk")]
        pick = pick.reshape(2, count, -1)[:, table[:count]].reshape(2, -1)
        ids = table[count:]
    owned = []
    for c in range(num_cond):
        made = transform(pick[0], pick[1], val, cond, c, cs, num_g)
        if links is None:
            whole = jnp.concatenate(made)
            owned.append((lax.psum_scatter(whole, "blk", scatter_dimension=0, tiled=True),))
        else:
            before = owned[-1][1:] if c == num_cond - 1 else ()
            owned.append(reduce_scatter(*made, links, before))
    for c, parts in enumerate(owned):
        owned[c] = sum(parts[1:], parts[0])
    own = jnp.stack(owned).reshape(num_cond, -1, 2, 4, num_val)
    rows = own.shape[1] * 4
    turned = lax.dynamic_slice_in_dim(mirrored, lax.axis_index("blk") * rows, rows)
    sign = jnp.where(turned, -1.0, 1.0).astype(f32)
    signs = jnp.stack([jnp.ones_like(sign), sign], axis=1).reshape(-1, 4, 2, 1, 1)
    own = (jnp.transpose(own, (1, 3, 2, 0, 4)) * signs).reshape(-1, 2 * pairs)

    gaps = e_val[None, :] - e_cond[:, None]
    gaps = gaps.reshape(1, pairs)
    occ_row = jnp.broadcast_to(occ.astype(f32)[None, :], (num_cond, num_val)).reshape(1, pairs)
    weights = occ_row * gaps / (gaps * gaps + (freq * freq)[:, None]) / math.sqrt(pairs)

    if links is not None:
        return gather_and_chi(weights, own, links, ids, num_g)
    return chi(weights, own, lax.all_gather(own, "blk", axis=0, tiled=True))


def solution(mesh):
    step = jax.shard_map(
        polarizability,
        mesh=mesh,
        in_specs=(
            P("cell", "blk", None, None),
            P("cell", "blk", None, None),
            P("cell"),
            P("cell"),
            P("cell"),
            P("cell"),
            P("cell"),
        ),
        out_specs=(P("cell", "blk", None), P("cell", "blk", None)),
        check_vma=False,
    )
    if not Links.fits(mesh.shape["blk"]):
        return step
    return step
```

```python
import functools
import math

import jax
import jax.numpy as jnp
import ml_dtypes
import numpy as np
from jax import lax
from jax.experimental import pallas as pl
from jax.experimental.pallas import tpu as pltpu
from jax.sharding import PartitionSpec as P


VMEM_BYTES = 64 * 2**20
LANES = 128
SUB = 8
PARTS = 4
SLOTS = 4
f32 = jnp.float32
bf16 = jnp.bfloat16


def split_np(table):
    high = table.astype(ml_dtypes.bfloat16)
    low = (table - high.astype(np.float64)).astype(ml_dtypes.bfloat16)
    return np.concatenate([high, high, low], axis=1)


def split3(block):
    high = block.astype(bf16)
    low = (block - high.astype(f32)).astype(bf16)
    return jnp.concatenate([high, low, high], axis=0)


def z_table(size_z):
    half = size_z // 2
    z = np.arange(size_z)
    cos_rows = np.cos(2 * np.pi * ((np.arange(half + 1)[:, None] * z) % size_z) / size_z)
    sin_rows = -np.sin(2 * np.pi * ((np.arange(1, half)[:, None] * z) % size_z) / size_z)
    return np.concatenate([cos_rows, sin_rows], axis=0)


def y_tables(size_y):
    k = np.arange(size_y)
    ang = 2 * np.pi * ((k[:, None] * k[None, :]) % size_y) / size_y
    cos_t, sin_t = np.cos(ang), np.sin(ang)
    real_rows = np.concatenate([cos_t, sin_t], axis=1)
    imag_rows = np.concatenate([-sin_t, cos_t], axis=1)
    full = np.stack([real_rows, imag_rows], axis=0).reshape(2, size_y // 4, 4, 2 * size_y)
    full = full.transpose(1, 0, 2, 3).reshape(2 * size_y, 2 * size_y)
    return full, full[:, :size_y]


def roll_sub(x, shift):
    return pltpu.roll(x, shift % SUB, axis=x.ndim - 2)


def in_steps(count, at_once, step):
    def several(i, carry):
        for u in range(at_once):
            step(i * at_once + u)
        return carry

    lax.fori_loop(0, count // at_once, several, 0)
    for i in range(count // at_once * at_once, count):
        step(i)


def transform_kernel(
    col_ref,
    phase_ref,
    val_hbm,
    cond_ref,
    dz_ref,
    dy_ref,
    dyr_ref,
    cs_hbm,
    *refs,
):
    outs, scratch = refs[:PARTS], refs[PARTS:]
    transform_parts(
        col_ref, phase_ref, val_hbm, cond_ref, dz_ref, dy_ref, dyr_ref, cs_hbm, outs, *scratch
    )


def transform_parts(
    col_ref,
    phase_ref,
    val_hbm,
    cond_ref,
    dz_ref,
    dy_ref,
    dyr_ref,
    cs_hbm,
    outs,
    val_scr,
    cs_scr,
    z_scr,
    tab_scr,
    out_scr,
    in_sems,
    out_sems,
):
    slots, size_y, size_z, lanes = val_hbm.shape
    half = size_z // 2
    groups_y = size_y // SUB
    pitch = size_z + SUB

    def plane(x):
        return pltpu.make_async_copy(val_hbm.at[x], val_scr.at[x], in_sems.at[x])

    phases = pltpu.make_async_copy(cs_hbm, cs_scr, in_sems.at[slots])
    for x in range(slots):
        plane(x).start()
    phases.start()

    def z_stage(x, yg):
        cond = cond_ref[x]
        parts = []
        for j in range(SUB):
            block = val_scr[x, yg * SUB + j]
            y = yg * SUB + j
            parts.append(block * jnp.broadcast_to(cond[:, y : y + 1], (size_z, lanes)))
        rhs = split3(jnp.concatenate(parts, axis=1))
        got = jnp.dot(dz_ref[...], rhs, preferred_element_type=f32)
        for j in range(SUB):
            at = pl.multiple_of((yg * SUB + j) * pitch, SUB)
            z_scr[x, pl.ds(at, size_z), :] = got[:, j * lanes : (j + 1) * lanes]

    def z_plane(x, carry):
        plane(x).wait()
        for yg in range(groups_y):
            z_stage(x, yg)
        return carry

    lax.fori_loop(0, slots, z_plane, 0)

    shape = (size_y // 4, SUB, lanes)
    sub = lax.broadcasted_iota(jnp.int32, shape, 1)
    low2 = (sub % 4) < 2
    low1 = (sub % 2) == 0

    def put(kz, got):
        a = [got[:, x * lanes : (x + 1) * lanes].reshape(shape) for x in range(slots)]
        p0 = jnp.where(low2, a[0], roll_sub(a[2], 2))
        p2 = jnp.where(low2, roll_sub(a[0], -2), a[2])
        p1 = jnp.where(low2, a[1], roll_sub(a[3], 2))
        p3 = jnp.where(low2, roll_sub(a[1], -2), a[3])
        tab_scr[kz, :, 0] = jnp.where(low1, p0, roll_sub(p1, 1))
        tab_scr[kz, :, 1] = jnp.where(low1, roll_sub(p0, -1), p1)
        tab_scr[kz, :, 2] = jnp.where(low1, p2, roll_sub(p3, 1))
        tab_scr[kz, :, 3] = jnp.where(low1, roll_sub(p2, -1), p3)

    def rows(k):
        return jnp.concatenate(
            [z_scr[x, pl.ds(k, size_y, stride=pitch), :] for x in range(slots)], axis=1
        )

    for kz in (0, half):
        put(kz, jnp.dot(dyr_ref[...], split3(rows(kz)), preferred_element_type=f32))

    def y_stage(step):
        kz = step + 1
        block = jnp.concatenate([rows(kz), rows(half + kz)], axis=0)
        put(kz, jnp.dot(dy_ref[...], split3(block), preferred_element_type=f32))

    in_steps(half - 1, 5, y_stage)

    sub1 = lax.broadcasted_iota(jnp.int32, (SUB, lanes), 0)
    m2 = (sub1 % 4) < 2
    m1 = (sub1 % 2) == 0
    kzs, kyq, _, _, _ = tab_scr.shape
    tab = tab_scr.reshape(kzs * kyq * 4 * SUB, lanes)
    quads = outs[0].shape[0]
    low4 = sub1 < 4
    phases.wait()

    def quad(q):
        t = []
        for i in range(4):
            d = tab[pl.ds(pl.multiple_of(col_ref[q * 4 + i], SUB), SUB), :]
            at = pl.ds(pl.multiple_of(phase_ref[q * 4 + i], SUB), SUB)
            p = cs_scr[at, :]
            turned = roll_sub(p, 4)
            t.append(d * jnp.where(low4, p, turned) + roll_sub(d, 4) * jnp.where(low4, turned, -p))
        v0 = jnp.where(m2, t[0], roll_sub(t[2], 2)) + jnp.where(m2, roll_sub(t[0], -2), t[2])
        v1 = jnp.where(m2, t[1], roll_sub(t[3], 2)) + jnp.where(m2, roll_sub(t[1], -2), t[3])
        out_scr[q] = jnp.where(m1, v0, roll_sub(v1, 1)) + jnp.where(m1, roll_sub(v0, -1), v1)

    copies = []
    for n in reversed(range(PARTS)):
        first = n * quads
        in_steps(quads, math.gcd(quads, 4 * SUB), lambda q, first=first: quad(first + q))
        copies.append(
            pltpu.make_async_copy(out_scr.at[pl.ds(first, quads)], outs[n], out_sems.at[n])
        )
        copies[-1].start()
    for copy in copies:
        copy.wait()


def transform(col, phase, val, cond, c, cs, num_g):
    slots, size_y, size_z, lanes = val.shape
    dz = jnp.asarray(split_np(z_table(size_z)))
    full, real_only = y_tables(size_y)
    dy, dyr = jnp.asarray(split_np(full)), jnp.asarray(split_np(real_only))
    vmem = pl.BlockSpec(memory_space=pltpu.VMEM)
    smem = pl.BlockSpec(memory_space=pltpu.SMEM)
    hbm = pl.BlockSpec(memory_space=pl.ANY)
    return pl.pallas_call(
        transform_kernel,
        grid=(1,),
        out_shape=(jax.ShapeDtypeStruct((num_g // 4 // PARTS, SUB, lanes), f32),) * PARTS,
        in_specs=[
            smem,
            smem,
            hbm,
            pl.BlockSpec((None,) + cond.shape[1:], lambda i: (c, 0, 0, 0)),
            vmem,
            vmem,
            vmem,
            hbm,
        ],
        out_specs=(hbm,) * PARTS,
        scratch_shapes=[
            pltpu.VMEM(val.shape, f32),
            pltpu.VMEM(cs.shape, f32),
            pltpu.VMEM((slots, (size_z + SUB) * size_y, lanes), f32),
            pltpu.VMEM((size_z // 2 + 1, size_y // 4, 4, SUB, lanes), f32),
            pltpu.VMEM((num_g // 4, SUB, lanes), f32),
            pltpu.SemaphoreType.DMA((slots + 1,)),
            pltpu.SemaphoreType.DMA((PARTS,)),
        ],
        compiler_params=pltpu.CompilerParams(vmem_limit_bytes=VMEM_BYTES),
        name="transform",
    )(col, phase, val, cond, dz, dy, dyr, cs)


def split_lanes(block):
    high = block.astype(bf16)
    low = (block - high.astype(f32)).astype(bf16)
    return high, low


def fill_left(w_ref, own_ref, left_scr):
    freqs = w_ref.shape[0]
    rows, pairs2 = own_ref.shape
    pairs = pairs2 // 2

    def fill(w, carry):
        row = w_ref[pl.ds(w, 1), :]
        a = own_ref[:, :pairs] * row
        b = own_ref[:, pairs:] * row
        at = pl.ds(pl.multiple_of(w * rows, rows), rows)
        for n, side in enumerate((a + b, a, b)):
            high, low = split_lanes(side)
            left_scr[at, (3 * n) * pairs : (3 * n + 1) * pairs] = high
            left_scr[at, (3 * n + 1) * pairs : (3 * n + 2) * pairs] = high
            left_scr[at, (3 * n + 2) * pairs : (3 * n + 3) * pairs] = low
        return carry

    lax.fori_loop(0, freqs, fill, 0)


def chi_tile(block, left_scr, real_ref, imag_ref):
    freqs, rows, _ = real_ref.shape
    pairs = block.shape[1] // 2
    c, d = block[:, :pairs], block[:, pairs:]
    got = []
    for n, side in enumerate((c, c + d, c - d)):
        high, low = split_lanes(side)
        right = jnp.concatenate([high, low, high], axis=1)
        got.append(
            lax.dot_general(
                left_scr[:, 3 * n * pairs : 3 * (n + 1) * pairs],
                right,
                (((1,), (1,)), ((), ())),
                preferred_element_type=f32,
            )
        )
    real_ref[...] = (got[0] - got[2]).reshape(freqs, rows, -1)
    imag_ref[...] = (got[0] - got[1]).reshape(freqs, rows, -1)


def chi_kernel(w_ref, own_ref, all_ref, real_ref, imag_ref, left_scr):
    @pl.when(pl.program_id(0) == 0)
    def _():
        fill_left(w_ref, own_ref, left_scr)

    chi_tile(all_ref[...], left_scr, real_ref, imag_ref)


def chi(weights, own, everyone):
    freqs, pairs = weights.shape
    rows = own.shape[0]
    num_g = everyone.shape[0]
    tile = min(num_g, 4 * LANES)
    out = jax.ShapeDtypeStruct((freqs, rows, num_g), f32)
    out_spec = pl.BlockSpec((freqs, rows, tile), lambda t: (0, 0, t))
    return pl.pallas_call(
        chi_kernel,
        grid=(num_g // tile,),
        out_shape=(out, out),
        in_specs=[
            pl.BlockSpec((freqs, pairs), lambda t: (0, 0)),
            pl.BlockSpec((rows, 2 * pairs), lambda t: (0, 0)),
            pl.BlockSpec((tile, 2 * pairs), lambda t: (t, 0)),
        ],
        out_specs=(out_spec, out_spec),
        scratch_shapes=[pltpu.VMEM((freqs * rows, 9 * pairs), bf16)],
        name="chi",
    )(weights, own, everyone)


def chi_group_kernel(counts, with_old, *refs):
    total = sum(counts)
    n = len(counts)
    _, w_ref, own_ref = refs[:3]
    pieces = refs[3 : 3 + total]
    rest = refs[3 + total + (2 if with_old else 0) :]
    real_ref, imag_ref, left_scr, got_scr, sems = rest
    step = pl.program_id(0)

    def copies(i):
        at, first = 0, sum(counts[:i])
        for j in range(counts[i]):
            ref = pieces[first + j]
            yield pltpu.make_async_copy(
                ref, got_scr.at[i, pl.ds(at, ref.shape[0])], sems.at[first + j]
            )
            at += ref.shape[0]

    @pl.when(step == 0)
    def _():
        for i in range(n):
            for copy in copies(i):
                copy.start()
        fill_left(w_ref, own_ref, left_scr)

    for i in range(n):

        @pl.when(step == i)
        def _(i=i):
            for copy in copies(i):
                copy.wait()

    chi_tile(got_scr[step], left_scr, real_ref, imag_ref)


def chi_group(weights, own, blocks, ids, first, num_g, old):
    freqs, pairs = weights.shape
    rows = own.shape[0]
    counts = tuple(len(b) for b in blocks)
    pieces = [p for b in blocks for p in b]
    out = jax.ShapeDtypeStruct((freqs, rows, num_g), f32)
    out_spec = pl.BlockSpec((freqs, rows, rows), lambda t, ids: (0, 0, ids[first + t]))
    hbm = pl.BlockSpec(memory_space=pl.ANY)
    olds = () if old is None else old
    return pl.pallas_call(
        functools.partial(chi_group_kernel, counts, old is not None),
        grid_spec=pltpu.PrefetchScalarGridSpec(
            num_scalar_prefetch=1,
            grid=(len(blocks),),
            in_specs=[
                pl.BlockSpec((freqs, pairs), lambda t, ids: (0, 0)),
                pl.BlockSpec((rows, 2 * pairs), lambda t, ids: (0, 0)),
            ]
            + [hbm] * (len(pieces) + len(olds)),
            out_specs=(out_spec, out_spec),
            scratch_shapes=[
                pltpu.VMEM((freqs * rows, 9 * pairs), bf16),
                pltpu.VMEM((len(blocks), rows, 2 * pairs), f32),
                pltpu.SemaphoreType.DMA((len(pieces),)),
            ],
        ),
        out_shape=(out, out),
        input_output_aliases={3 + len(pieces) + i: i for i in range(len(olds))},
        compiler_params=pltpu.CompilerParams(vmem_limit_bytes=VMEM_BYTES),
        name="chi",
    )(ids, weights, own, *pieces, *olds)


GROUPS = (((0, 0),), ((1, 0), (0, 3)), ((0, 1), (1, 3)), ((0, 2), (1, 1)), ((1, 2),))
RING = (0, 2, 3, 1)


class Links:
    def __init__(self, count):
        def place(i):
            return i // 4, i // 2 % 2, i % 2

        def at(z, y, core):
            return z * 4 + y * 2 + core

        def turn(i, by):
            z, y, core = place(i)
            return at(RING[(RING.index(z) + by) % 4], y, core)

        every = range(count)
        self.core = [(i, i ^ 1) for i in every]
        self.y = [(i, i ^ 2) for i in every]
        self.cw = [(i, turn(i, 1)) for i in every]
        self.ccw = [(i, turn(i, -1)) for i in every]
        self.near = np.array(
            [
                [[[turn(i ^ (2 * b) ^ a, r) for r in range(4)] for b in range(2)] for a in range(2)]
                for i in every
            ],
            dtype=np.int32,
        )
        self.order = np.stack([self.near[:, :, b, r] for g in GROUPS for b, r in g], axis=1)

    @staticmethod
    def fits(count):
        return count == len(RING) * 4


def send(value, pairs):
    return lax.ppermute(value, "blk", pairs)


def reduce_scatter(near, far, near_other, far_other, links):
    block = near.shape[0] // 4
    got_far = send(far_other, links.core)
    got_near = send(near_other, links.core)
    cuts = ((2 * block, 4 * block), (0, 2 * block))
    high, low = (send(far[i:j] + got_far[i:j], links.y) for i, j in cuts)
    high = near[2 * block :] + got_near[2 * block :] + high
    to_cw, to_ccw, near = lax.optimization_barrier((high[:block], high[block:], near))
    low = near[: 2 * block] + got_near[: 2 * block] + low
    mine, next_cw = low[:block], low[block:]
    two_back = send(to_cw, links.cw)
    ahead = send(to_ccw, links.ccw)
    next_cw = next_cw + two_back
    back = send(next_cw, links.cw)
    return mine, ahead, back


def gather_and_chi(weights, own, links, ids, num_g):
    cw = send(own, links.cw)
    later, cw = lax.optimization_barrier((own, cw))
    ccw = send(later, links.ccw)
    cw_later, ccw = lax.optimization_barrier((cw, ccw))
    mine = {(0, 0): own, (0, 3): cw, (0, 1): ccw, (0, 2): send(cw_later, links.cw)}
    for r in range(4):
        mine[1, r] = send(mine[0, r], links.y)
    old = None
    first = 0
    for group in GROUPS:
        blocks = []
        for b, r in group:
            blocks += [[mine[b, r]], [send(mine[b, r], links.core)]]
        old = chi_group(weights, own, blocks, ids, first, num_g, old)
        first += len(blocks)
    return old


def phase_table(size_x, first, planes, norm):
    x = first + jnp.arange(SLOTS, dtype=jnp.int32)
    k = jnp.arange(size_x, dtype=jnp.int32)
    ang = (k[:, None] * x[None, :] % size_x).astype(f32) * (2.0 * math.pi / size_x)
    live = (jnp.arange(SLOTS) < planes).astype(f32) * norm
    cos_t, sin_t = jnp.cos(ang) * live, jnp.sin(ang) * live
    table = jnp.stack(
        [jnp.concatenate([cos_t, sin_t], axis=1), jnp.concatenate([cos_t, -sin_t], axis=1)]
    )
    return jnp.broadcast_to(table.reshape(-1, 1), (table.size, LANES))


def polarizability(psi_val, psi_cond, e_val, e_cond, occ, freq, gmap):
    num_val, planes, size_y, size_z = psi_val.shape
    num_cond = psi_cond.shape[0]
    num_g = gmap.shape[0]
    pairs = num_val * num_cond
    size_x = planes * lax.axis_size("blk")
    norm = 1.0 / math.sqrt(size_x * size_y * size_z)

    val = jnp.transpose(psi_val, (1, 2, 3, 0))
    cond = jnp.transpose(psi_cond, (0, 1, 3, 2))
    if planes < SLOTS:
        val = jnp.pad(val, ((0, SLOTS - planes), (0, 0), (0, 0), (0, 0)))
        cond = jnp.pad(cond, ((0, 0), (0, SLOTS - planes), (0, 0), (0, 0)))

    kz = gmap % size_z
    ky = gmap // size_z % size_y
    kx = gmap // (size_z * size_y)
    mirrored = kz > size_z // 2
    col = jnp.where(mirrored, size_z - kz, kz) * size_y + jnp.where(
        mirrored, (size_y - ky) % size_y, ky
    )
    pick = jnp.stack([col, kx + jnp.where(mirrored, size_x, 0)]) * SUB
    cs = phase_table(size_x, lax.axis_index("blk") * planes, planes, norm)

    count = lax.axis_size("blk")
    links = Links(count) if Links.fits(count) else None
    if links is not None:
        tables = np.concatenate([x.reshape(count, -1) for x in (links.near, links.order)], axis=1)
        table = jnp.asarray(tables)[lax.axis_index("blk")]
        pick = pick.reshape(2, count, -1)[:, table[:count]].reshape(2, -1)
        ids = table[count:]
    owned = []
    for c in range(num_cond):
        made = transform(pick[0], pick[1], val, cond, c, cs, num_g)
        if links is None:
            whole = jnp.concatenate(made)
            owned.append((lax.psum_scatter(whole, "blk", scatter_dimension=0, tiled=True),))
        else:
            owned.append(reduce_scatter(*made, links))
    for c, parts in enumerate(owned):
        owned[c] = sum(parts[1:], parts[0])
    own = jnp.stack(owned).reshape(num_cond, -1, 2, 4, num_val)
    rows = own.shape[1] * 4
    turned = lax.dynamic_slice_in_dim(mirrored, lax.axis_index("blk") * rows, rows)
    sign = jnp.where(turned, -1.0, 1.0).astype(f32)
    signs = jnp.stack([jnp.ones_like(sign), sign], axis=1).reshape(-1, 4, 2, 1, 1)
    own = (jnp.transpose(own, (1, 3, 2, 0, 4)) * signs).reshape(-1, 2 * pairs)

    gaps = e_val[None, :] - e_cond[:, None]
    gaps = gaps.reshape(1, pairs)
    occ_row = jnp.broadcast_to(occ.astype(f32)[None, :], (num_cond, num_val)).reshape(1, pairs)
    weights = occ_row * gaps / (gaps * gaps + (freq * freq)[:, None]) / math.sqrt(pairs)

    if links is not None:
        return gather_and_chi(weights, own, links, ids, num_g)
    return chi(weights, own, lax.all_gather(own, "blk", axis=0, tiled=True))


def solution(mesh):
    step = jax.shard_map(
        polarizability,
        mesh=mesh,
        in_specs=(
            P("cell", "blk", None, None),
            P("cell", "blk", None, None),
            P("cell"),
            P("cell"),
            P("cell"),
            P("cell"),
            P("cell"),
        ),
        out_specs=(P("cell", "blk", None), P("cell", "blk", None)),
        check_vma=False,
    )
    if not Links.fits(mesh.shape["blk"]):
        return step
    return step
```
